32 devices in a mesh: groups: 2 (over x), band: 16 (over z, y, core).
Axes of the slice: x: 2, y: 2, z: 4, core: 2. Of those that a mesh axis runs over, the one named last changes fastest.
Arguments:
- queries: bfloat16 [128, 80, 2560], P(('groups', 'band')), parts along dimension 0, may hold values from -7 to 7, as said below
- kv_frames: bfloat16 [4, 4, 64, 80, 2560], P('groups', None, 'band'), parts along dimension 0, may hold values from -7 to 7
- frame_mask: int32 [6], P('groups'), parts along dimension 0, may hold values 0 or 1
- col_shift: int32 [128], P('groups'), parts along dimension 0, may hold values from -4 to 4
- latent: bfloat16 [6, 128, 2560], P('groups', 'band'), parts along dimension 0, may hold values from -6 to 6
- conv_in: bfloat16 [432, 384], replicated, may hold values from -0.3125 to 0.3125
- bias_in: float32 [384], replicated, may hold values from -3 to 3
- norm_gain: float32 [384], replicated, may hold values from 0.1 to 1.9
- conv_mid: bfloat16 [3456, 384], replicated, may hold values from -0.109375 to 0.109375
- bias_mid: float32 [384], replicated, may hold values from -3 to 3
Outputs:
- attended: bfloat16 [128, 80, 2560], P(('groups', 'band')), parts along dimension 0
- decoded: bfloat16 [256, 160, 384], P(('groups', 'band')), parts along dimension 0
The draws below stay inside these ranges and needn't reach their ends.
There are 2 independent parts, one for each index of `groups`. The reference program is written for one: setup_inputs(seed, part) draws one part's arguments, and reference() takes and returns one part's arrays. A program takes and returns all parts, laid end to end along the dimension named above; an argument that names none is the same for every part. Nothing has to cross between parts.
Inputs may be any that keep to these rules, and one draw needn't show every extreme that they name: queries of a few patches may be large.
All inputs are finite; a program needn't handle non-finite values.
Results may differ from the reference program's by a relative error of at most 0.007.
Values may be sent and summed in bfloat16 or wider, within the bound.
A program may use at most 256 MiB of HBM per device.

```python
import math
import jax
import jax.numpy as jnp
from jax import lax

H = 20
HD = 128
COLS = 80
ROWS = 64
CACHED = 3
FRAMES = 4
RC = 8
SHIFT = 4
CL = 16
CH = 384
LROWS = 128
LC = 160


def draw_queries(key, part):
    shape_q = (ROWS, COLS, H * HD)
    base_draw = jnp.clip(jax.random.normal(key, shape_q, jnp.float32), -6.0, 6.0)
    return base_draw.astype(jnp.bfloat16)


def draw_kv_frames(key, part):
    shape_kv = (2, FRAMES, ROWS, COLS, H * HD)
    draw_key = jax.random.fold_in(key, 2213)
    base_draw = jnp.clip(jax.random.normal(draw_key, shape_kv, jnp.float32), -6.0, 6.0)
    return base_draw.astype(jnp.bfloat16)


def set_ends(values, key, smallest, high):
    longest = values.shape.index(max(values.shape))
    spots = []
    for shift in (0, 1):
        where = [jax.random.randint(jax.random.fold_in(key, axis), (), 0, length) for axis, length in enumerate(values.shape)]
        where[longest] = (where[longest] + shift) % values.shape[longest]
        spots.append(tuple(where))
    return values.at[spots[0]].set(smallest).at[spots[1]].set(high)


def block_levels(key, dims, shards, low, largest):
    def one(dim, parts):
        draws = jax.random.uniform(jax.random.fold_in(jax.random.fold_in(key, 6), dim), (parts,), jnp.float32, low / len(shards), largest / len(shards))
        return jnp.repeat(jnp.exp(draws), dims[dim] // parts).reshape((-1,) + (1,) * (len(dims) - dim - 1))

    level = one(*shards[0])
    for cut in shards[1:]:
        level = level * one(*cut)
    return level


def bell_draw(stream_key, dims, width, reach, cuts=(), held_as=jnp.bfloat16):
    values = width * jax.random.normal(stream_key, dims, jnp.float32)
    if cuts:
        values = values * block_levels(stream_key, dims, cuts, -0.22, 0.18)
    return jnp.clip(values, -reach, reach).astype(held_as)


def setup_inputs(seed: int = 0, part: int = 0) -> dict:
    splits = jax.random.split(jax.random.key(seed), 11)
    part_keys = jax.random.split(jax.random.fold_in(splits[10], part), 11)
    return {
        "queries": draw_queries(jax.random.fold_in(jax.random.fold_in(splits[10], part), 71), part),
        "kv_frames": draw_kv_frames(jax.random.fold_in(jax.random.fold_in(splits[10], part), 71), part),
        "frame_mask": set_ends((jax.random.randint(part_keys[2], (CACHED,), 0, 3) < 2).astype(jnp.int32), jax.random.fold_in(part_keys[2], 1), 0, 1),
        "col_shift": set_ends(jax.random.randint(part_keys[3], (ROWS,), 0 - SHIFT, SHIFT + 1), jax.random.fold_in(part_keys[3], 1), 0 - SHIFT, SHIFT).astype(jnp.int32),
        "latent": bell_draw(part_keys[4], (3, LROWS, LC * CL), 1.0, 6.0, ((1, 16),)),
        "conv_in": bell_draw(splits[5], (27 * CL, CH), (27 * CL) ** -0.5, 0.3125),
        "bias_in": bell_draw(splits[6], (CH,), 0.5, 3.0, (), jnp.float32),
        "norm_gain": jnp.clip(1.0 + 0.18 * jax.random.normal(splits[7], (CH,), jnp.float32), 0.1, 1.9),
        "conv_mid": bell_draw(splits[8], (9 * CH, CH), (9 * CH) ** -0.5, 0.109375),
        "bias_mid": bell_draw(splits[9], (CH,), 0.5, 3.0, (), jnp.float32),
    }


def attend(query_row, window, row_ok, col_offset, frame_ok):
    width_c = query_row.shape[0]
    span = window.shape[2]
    frames = window.shape[1]
    query_heads = query_row.reshape(width_c, H, HD).astype(jnp.float32)
    key_part = window[0].reshape(frames, span, width_c, H, HD).astype(jnp.float32)
    value_part = window[1].reshape(frames, span, width_c, H, HD).astype(jnp.float32)
    scores = jnp.einsum('chd,fnkhd->hcfnk', query_heads, key_part) * (1.0 / math.sqrt(HD))
    columns = jnp.arange(width_c, dtype=jnp.int32)
    column_ok = jnp.abs(columns[None, :] - columns[:, None] - col_offset) <= RC
    valid = column_ok[:, None, None, :] & frame_ok[None, :, None, None] & row_ok[None, None, :, None]
    scores = jnp.where(valid[None], scores, -1e+30)
    row_max = lax.optimization_barrier(jnp.max(scores, axis=(2, 3, 4)))
    weights = jnp.where(valid[None], jnp.exp(scores - row_max[:, :, None, None, None]), 0.0)
    row_sum = lax.optimization_barrier(jnp.sum(weights, axis=(2, 3, 4)))
    rounded = weights.astype(jnp.bfloat16).astype(jnp.float32)
    numerator = jnp.einsum('hcfnk,fnkhd->chd', rounded, value_part)
    return (numerator, row_max, row_sum)

def conv_first(source, out_rows, conv_in, bias_in):
    channels = conv_in.shape[0] // 27
    width_x = source.shape[2] // channels
    grid = source.reshape(3, source.shape[1], width_x, channels)
    grid = jnp.pad(grid, ((0, 0), (0, 0), (1, 1), (0, 0)))
    pieces = []
    for delta_t in range(3):
        for delta_y in range(3):
            for delta_x in range(3):
                pieces.append(grid[delta_t, delta_y:delta_y + out_rows, delta_x:delta_x + width_x, :])
    patches = jnp.concatenate(pieces, axis=-1).reshape(out_rows * width_x, 27 * channels)
    hidden = jnp.dot(patches, conv_in, preferred_element_type=jnp.float32) + bias_in.astype(jnp.float32)
    return hidden.reshape(out_rows, width_x, conv_in.shape[1])

def activate(hidden, norm_gain):
    scale = lax.rsqrt(lax.optimization_barrier(jnp.mean(hidden * hidden, axis=-1, keepdims=True)) + 1e-06)
    return jax.nn.silu(hidden * scale * norm_gain.astype(jnp.float32))

def conv_second(active, out_rows, conv_mid):
    width_x = active.shape[1]
    grid = jnp.pad(active, ((0, 0), (1, 1), (0, 0)))
    pieces = []
    for delta_y in range(3):
        for delta_x in range(3):
            pieces.append(grid[delta_y:delta_y + out_rows, delta_x:delta_x + width_x, :])
    patches = jnp.concatenate(pieces, axis=-1).reshape(out_rows * width_x, conv_mid.shape[0])
    result = jnp.dot(patches, conv_mid, preferred_element_type=jnp.float32)
    return result.reshape(out_rows, width_x, conv_mid.shape[1])

def reference(queries, kv_frames, frame_mask, col_shift, latent, conv_in, bias_in, norm_gain, conv_mid, bias_mid):
    total_rows = queries.shape[0]
    width_c = queries.shape[1]
    frame_ok = jnp.concatenate([frame_mask == 1, jnp.ones((1,), dtype=bool)])

    def one_row(row_at):
        start_row = jnp.clip(row_at - 1, 0, total_rows - 3).astype(jnp.int32)
        window = lax.dynamic_slice_in_dim(kv_frames, start_row, 3, 2)
        key_rows = start_row + jnp.arange(3, dtype=jnp.int32)
        row_ok = jnp.abs(key_rows - row_at) <= 1
        query_row = lax.dynamic_index_in_dim(queries, row_at, 0, keepdims=False)
        col_offset = lax.dynamic_index_in_dim(col_shift, row_at, 0, keepdims=False)
        numerator, row_max, row_sum = attend(query_row, window, row_ok, col_offset, frame_ok)
        result = numerator / jnp.transpose(row_sum)[:, :, None]
        return result.reshape(width_c, H * HD).astype(jnp.bfloat16)
    attended = lax.map(one_row, jnp.arange(total_rows, dtype=jnp.int32))
    lat_rows = latent.shape[1]
    padded_lat = jnp.pad(latent, ((0, 0), (1, 1), (0, 0)))
    first = conv_first(padded_lat, lat_rows, conv_in, bias_in)
    active = activate(first, norm_gain).astype(jnp.bfloat16)
    active = jnp.pad(active, ((1, 1), (0, 0), (0, 0)))
    decoded = (conv_second(active, lat_rows, conv_mid) + bias_mid.astype(jnp.float32) + first).astype(jnp.bfloat16)
    return (attended, decoded)
```

```python
import functools
import math

import jax
import jax.numpy as jnp
from jax import lax
from jax.experimental import pallas as pl
from jax.experimental.pallas import tpu as pltpu
from jax.sharding import PartitionSpec as P

HD = 128
RC = 8
NEG = -1e30
SCALE2 = math.log2(math.e) / math.sqrt(HD)
HEADS_PER_STEP = 4
VMEM_BYTES = 56 * 2**20


def to_next(block, axis):
    count = lax.axis_size(axis)
    return lax.ppermute(block, axis, [(i, i + 1) for i in range(count - 1)])


def to_previous(block, axis):
    count = lax.axis_size(axis)
    return lax.ppermute(block, axis, [(i + 1, i) for i in range(count - 1)])


def key_bias(cols, padded, slots, shift, open_slots):
    lane = lax.broadcasted_iota(jnp.int32, (cols, padded), 1)
    query = lax.broadcasted_iota(jnp.int32, (cols, padded), 0)
    column = lane
    level = jnp.full((cols, padded), NEG, jnp.float32)
    for s in range(slots):
        inside = (lane >= s * cols) & (lane < (s + 1) * cols)
        level = jnp.where(inside, open_slots[s], level)
        column = jnp.where(lane >= s * cols, lane - s * cols, column)
    return jnp.where(jnp.abs(column - query - shift) <= RC, level, NEG)


def attention_kernel(
    total_rows, shift_ref, mask_ref, q_ref, qp_ref, qn_ref, kv_ref, out_ref, op_ref, on_ref, lev_ref, bias_ref, level_ref
):
    step = pl.program_id(0)
    frames, rows, cols = kv_ref.shape[1], q_ref.shape[0], q_ref.shape[1]
    wide = op_ref.shape[1] - 3 * 128
    open_frames = [jnp.where(mask_ref[f] == 1, 0.0, NEG) for f in range(frames - 1)] + [jnp.float32(0.0)]
    closed = jnp.int32(frames - 1)
    for f in reversed(range(frames - 1)):
        closed = jnp.where(mask_ref[f] == 1, closed, f)

    def run(slots, frame_of, open_slots):
        span = slots * cols
        padded = -(-span // 128) * 128

        @pl.when(step == 0)
        def _():
            first_row = lax.axis_index("band") * rows
            for r in range(-1, rows + 1):
                row = jnp.clip(first_row + r, 0, total_rows - 1)
                bias_ref[r + 1, :, :padded] = key_bias(cols, padded, slots, shift_ref[row], open_slots)

        def stack(which, n, part):
            pieces = [kv_ref[which, frame_of(s), n, :, part] for s in range(slots)]
            if padded > span:
                pieces.append(kv_ref[which, frame_of(0), n, : padded - span, part])
            return jnp.concatenate(pieces, axis=0)

        def query_row(r, part):
            if r < 0:
                return qp_ref[:, part]
            return qn_ref[:, part] if r == rows else q_ref[r, :, part]

        def score(j):
            part = pl.ds(j * HD, HD)
            found = []
            for n in range(rows):
                query = jnp.concatenate([query_row(r, part) for r in range(n - 1, n + 2)], axis=0)
                found.append(
                    lax.dot_general(
                        query, stack(0, n, part), (((1,), (1,)), ((), ())), preferred_element_type=jnp.float32
                    )
                )
            return found

        def soften(found):
            pieces = [[None] * 3 for _ in range(rows)]
            totals, levels = {}, {}
            for r in range(-1, rows + 1):
                bias = bias_ref[r + 1, :, :padded]
                at = [(n, r - n + 1) for n in range(max(r - 1, 0), min(r + 2, rows))]
                blocks = [found[n][d * cols : (d + 1) * cols] + bias for n, d in at]
                top = jnp.max(functools.reduce(jnp.maximum, blocks), axis=-1, keepdims=True) * SCALE2
                weights = [jnp.exp2(block * SCALE2 - top) for block in blocks]
                total = jnp.sum(functools.reduce(jnp.add, weights), axis=-1, keepdims=True)
                for (n, d), weight in zip(at, weights):
                    pieces[n][d] = weight.astype(jnp.bfloat16)
                totals[r], levels[r] = total, top
            return [jnp.concatenate(piece, axis=0) for piece in pieces], totals, levels

        lane = lax.broadcasted_iota(jnp.int32, (cols, 128), 1)

        def finish(j, weights, totals, levels):
            part = pl.ds(j * HD, HD)
            head = step * HEADS_PER_STEP + j
            sums = [
                jnp.dot(weights[n], stack(1, n, part), preferred_element_type=jnp.float32) for n in range(rows)
            ]
            for r in range(-1, rows + 1):
                near = range(max(r - 1, 0), min(r + 2, rows))
                acc = sum(sums[n][(r - n + 1) * cols : (r - n + 2) * cols] for n in near)
                out = (acc * (1.0 / totals[r])).astype(jnp.bfloat16)
                if r < 0:
                    op_ref[:, pl.ds(pl.multiple_of(head * HD, HD), HD)] = out
                elif r == rows:
                    on_ref[:, pl.ds(pl.multiple_of(head * HD, HD), HD)] = out
                else:
                    out_ref[r, :, part] = out
            for side, r in enumerate((-1, rows, 0, rows - 1)):
                level = levels[r] + jnp.log2(totals[r])
                level_ref[side] = jnp.where(lane == head, level, level_ref[side])

        ahead = score(0)
        for j in range(HEADS_PER_STEP):
            found = ahead
            if j + 1 < HEADS_PER_STEP:
                ahead = score(j + 1)
            finish(j, *soften(found))

    @pl.when(step == 0)
    def _():
        level_ref[...] = jnp.zeros_like(level_ref)

    @pl.when(closed < frames - 1)
    def _():
        run(
            frames - 1,
            lambda s: jnp.where(s < closed, s, s + 1),
            [jnp.where(s < closed, open_frames[s], open_frames[s + 1]) for s in range(frames - 1)],
        )

    @pl.when(closed == frames - 1)
    def _():
        run(frames, lambda s: s, open_frames)

    @pl.when(step == pl.num_programs(0) - 1)
    def _():
        for side, o_ref in enumerate((op_ref, on_ref)):
            rest = level_ref[side]
            for k in range(3):
                piece = rest.astype(jnp.bfloat16)
                o_ref[:, wide + k * 128 : wide + (k + 1) * 128] = piece
                rest = rest - piece.astype(jnp.float32)
            lev_ref[side] = level_ref[2 + side]


def combine_kernel(own_ref, lev_ref, op_ref, on_ref, out_ref):
    side, step = pl.program_id(0), pl.program_id(1)
    place = lax.axis_index("band")
    count = lax.axis_size("band")
    cols, lanes = own_ref.shape[1], own_ref.shape[2]
    wide = op_ref.shape[1] - 3 * 128
    lane = lax.broadcasted_iota(jnp.int32, (cols, 128), 1)

    def mix(o_ref, there):
        other = sum(o_ref[:, wide + k * 128 : wide + (k + 1) * 128].astype(jnp.float32) for k in range(3))
        share = jnp.where(there, 1.0 / (1.0 + jnp.exp2(lev_ref[side] - other)), 0.0)
        for j in range(lanes // HD):
            head = step * (lanes // HD) + j
            weight = jnp.sum(jnp.where(lane == head, share, 0.0), axis=-1, keepdims=True)
            here = own_ref[0, :, j * HD : (j + 1) * HD].astype(jnp.float32)
            far = o_ref[:, pl.ds(pl.multiple_of(head * HD, HD), HD)].astype(jnp.float32)
            out_ref[0, :, j * HD : (j + 1) * HD] = (here + (far - here) * weight).astype(jnp.bfloat16)

    @pl.when(side == 0)
    def _():
        mix(op_ref, place > 0)

    @pl.when(side == 1)
    def _():
        mix(on_ref, place < count - 1)


def attention(queries, kv_frames, frame_mask, col_shift, q_prev, q_next):
    rows, cols, wide = queries.shape
    frames = kv_frames.shape[1]
    heads = wide // HD
    step_lanes = HEADS_PER_STEP * HD
    smem = pl.BlockSpec(memory_space=pltpu.SMEM)
    packed = wide + 3 * 128
    padded = -(-frames * cols // 128) * 128

    def fixed(shape):
        return pl.BlockSpec(shape, lambda *_: (0,) * len(shape))

    def lanes(shape):
        lead = (0,) * (len(shape) - 1)
        return pl.BlockSpec(shape, lambda h: lead + (h,))

    return pl.pallas_call(
        functools.partial(attention_kernel, col_shift.shape[0]),
        grid=(heads // HEADS_PER_STEP,),
        out_shape=(
            jax.ShapeDtypeStruct(queries.shape, jnp.bfloat16),
            jax.ShapeDtypeStruct((cols, packed), jnp.bfloat16),
            jax.ShapeDtypeStruct((cols, packed), jnp.bfloat16),
            jax.ShapeDtypeStruct((2, cols, 128), jnp.float32),
        ),
        in_specs=[
            smem,
            smem,
            lanes((rows, cols, step_lanes)),
            lanes((cols, step_lanes)),
            lanes((cols, step_lanes)),
            lanes((2, frames, rows, cols, step_lanes)),
        ],
        out_specs=(
            lanes((rows, cols, step_lanes)),
            fixed((cols, packed)),
            fixed((cols, packed)),
            fixed((2, cols, 128)),
        ),
        scratch_shapes=[
            pltpu.VMEM((rows + 2, cols, padded), jnp.float32),
            pltpu.VMEM((4, cols, 128), jnp.float32),
        ],
        compiler_params=pltpu.CompilerParams(vmem_limit_bytes=VMEM_BYTES),
        cost_estimate=pl.CostEstimate(
            flops=4 * rows * cols * 3 * frames * cols * wide,
            bytes_accessed=2 * rows * frames * cols * wide * 2,
            transcendentals=rows * heads * cols * 3 * frames * cols,
        ),
        name="attention",
    )(col_shift, frame_mask, queries, q_prev, q_next, kv_frames)


def combine(partial, level, back_prev, back_next):
    rows, cols, wide = partial.shape
    step_lanes = wide // 2
    edge = pl.BlockSpec((1, cols, step_lanes), lambda s, h: (s * (rows - 1), 0, h))

    def fixed(shape):
        return pl.BlockSpec(shape, lambda *_: (0,) * len(shape))

    return pl.pallas_call(
        combine_kernel,
        grid=(2, wide // step_lanes),
        out_shape=jax.ShapeDtypeStruct(partial.shape, jnp.bfloat16),
        in_specs=[edge, fixed(level.shape), fixed(back_prev.shape), fixed(back_next.shape)],
        out_specs=edge,
        input_output_aliases={0: 0},
        compiler_params=pltpu.CompilerParams(vmem_limit_bytes=VMEM_BYTES),
        name="combine",
    )(partial, level, back_prev, back_next)


def decoder_kernel(
    group, lat_ref, cin_ref, wmid_ref, bin_ref, gain_ref, bmid_ref, out_ref, win_ref, first_ref, act_ref
):
    place = lax.axis_index("band")
    count = lax.axis_size("band")
    depth = cin_ref.shape[0] // 27
    for dx in range(3):
        for dy in range(3):
            for dt in range(3):
                source_at = ((dt * 3 + dy) * 3 + dx) * depth
                at = (dy * 3 + dt) * depth
                win_ref[dx, at : at + depth] = cin_ref[source_at : source_at + depth]
    width, ch = out_ref.shape[1], out_ref.shape[2]
    rows = out_ref.shape[0]
    x_at = lax.broadcasted_iota(jnp.int32, (width, ch), 0)

    @pl.loop(0, rows + 2)
    def _(i):
        source = lat_ref[i]
        left = jnp.dot(source, win_ref[0], preferred_element_type=jnp.float32)
        mid = jnp.dot(source, win_ref[1], preferred_element_type=jnp.float32)
        right = jnp.dot(source, win_ref[2], preferred_element_type=jnp.float32)
        left = jnp.where(x_at == 0, 0.0, pltpu.roll(left, 1, 0))
        right = jnp.where(x_at == width - 1, 0.0, pltpu.roll(right, width - 1, 0))
        first = left + mid + right + bin_ref[...][None]
        first_ref[i] = first
        scale = lax.rsqrt(jnp.mean(first * first, axis=-1, keepdims=True) + 1e-06)
        value = first * scale * gain_ref[...][None]
        active = value / (1.0 + jnp.exp(-value))
        outside = ((i == 0) & (place == 0)) | ((i == rows + 1) & (place == count - 1))
        active = jnp.where(outside, 0.0, active)
        at = pl.ds(pl.multiple_of(i * width, width), width)
        act_ref[at, 0:ch] = jnp.where(x_at == 0, 0.0, pltpu.roll(active, 1, 0)).astype(jnp.bfloat16)
        act_ref[at, ch : 2 * ch] = active.astype(jnp.bfloat16)
        act_ref[at, 2 * ch : 3 * ch] = jnp.where(
            x_at == width - 1, 0.0, pltpu.roll(active, width - 1, 0)
        ).astype(jnp.bfloat16)

    @pl.loop(0, rows // group)
    def _(g):
        total = jnp.zeros((group * width, ch), jnp.float32)
        for dy in range(3):
            at = pl.ds(pl.multiple_of((g * group + dy) * width, width), group * width)
            total += jnp.dot(
                act_ref[at, :], wmid_ref[dy * 3 * ch : (dy + 1) * 3 * ch, :], preferred_element_type=jnp.float32
            )
        total = total + bmid_ref[...][None]
        for y in range(group):
            here = g * group + y
            out_ref[here] = (total[y * width : (y + 1) * width] + first_ref[here + 1]).astype(jnp.bfloat16)


def decoder(latent, conv_in, bias_in, norm_gain, conv_mid, bias_mid, low, high):
    times, rows, packed = latent.shape
    ch = conv_in.shape[1]
    depth = conv_in.shape[0] // 27
    width = packed // depth
    grid_rows = jnp.concatenate([low, latent, high], axis=1)
    pixels = grid_rows.reshape(times, rows + 4, width, depth).transpose(1, 2, 0, 3)
    pixels = pixels.reshape(rows + 4, width, times * depth)
    stacked = jnp.concatenate([pixels[dy : dy + rows + 2] for dy in range(3)], axis=-1)
    group = next(size for size in (4, 2, 1) if rows % size == 0)
    vmem = pl.BlockSpec(memory_space=pltpu.VMEM)
    return pl.pallas_call(
        functools.partial(decoder_kernel, group),
        out_shape=jax.ShapeDtypeStruct((rows, width, ch), jnp.bfloat16),
        in_specs=[vmem] * 6,
        out_specs=vmem,
        scratch_shapes=[
            pltpu.VMEM((3, 9 * depth, ch), jnp.bfloat16),
            pltpu.VMEM((rows + 2, width, ch), jnp.float32),
            pltpu.VMEM(((rows + 2) * width, 3 * ch), jnp.bfloat16),
        ],
        cost_estimate=pl.CostEstimate(
            flops=2 * rows * width * 9 * ch * ch, bytes_accessed=9 * ch * ch * 2, transcendentals=rows * width * ch
        ),
        name="decoder",
    )(stacked, conv_in, conv_mid, bias_in, norm_gain, bias_mid)


def body(
    queries, kv_frames, frame_mask, col_shift, latent, conv_in, bias_in, norm_gain, conv_mid, bias_mid
):
    rows, cols, wide = queries.shape
    times, lat_rows, lat_wide = latent.shape
    low_rows = latent[:, lat_rows - 2 :].reshape(times * 2, lat_wide)
    high_rows = latent[:, :2].reshape(times * 2, lat_wide)
    low = to_next(jnp.concatenate([queries[rows - 1], low_rows]), "band")
    high = to_previous(jnp.concatenate([queries[0], high_rows]), "band")
    partial, o_prev, o_next, level = attention(queries, kv_frames, frame_mask, col_shift, low, high)
    back_prev = to_next(o_next, "band")
    back_next = to_previous(o_prev, "band")
    low_rows = low[cols:].reshape(times, 2, lat_wide)
    high_rows = high[cols:].reshape(times, 2, lat_wide)
    decoded = decoder(latent, conv_in, bias_in, norm_gain, conv_mid, bias_mid, low_rows, high_rows)
    attended = combine(partial, level, back_prev, back_next)
    return (attended, decoded)


def solution(mesh):
    placed = (
        P(("groups", "band"), None, None),
        P("groups", None, "band", None, None),
        P("groups"),
        P("groups"),
        P("groups", "band", None),
        P(),
        P(),
        P(),
        P(),
        P(),
    )
    return jax.shard_map(
        body,
        mesh=mesh,
        in_specs=placed,
        out_specs=(P(("groups", "band"), None, None), P(("groups", "band"), None, None)),
        check_vma=False,
    )
```

```python
import functools
import math

import jax
import jax.numpy as jnp
from jax import lax
from jax.experimental import pallas as pl
from jax.experimental.pallas import tpu as pltpu
from jax.sharding import PartitionSpec as P

HD = 128
RC = 8
NEG = -1e30
MESH = pl.DeviceIdType.MESH
SCALE2 = math.log2(math.e) / math.sqrt(HD)
HEADS_PER_STEP = 4
VMEM_BYTES = 56 * 2**20


def key_bias(cols, padded, slots, shift, open_slots):
    lane = lax.broadcasted_iota(jnp.int32, (cols, padded), 1)
    query = lax.broadcasted_iota(jnp.int32, (cols, padded), 0)
    column = lane
    level = jnp.full((cols, padded), NEG, jnp.float32)
    for s in range(slots):
        inside = (lane >= s * cols) & (lane < (s + 1) * cols)
        level = jnp.where(inside, open_slots[s], level)
        column = jnp.where(lane >= s * cols, lane - s * cols, column)
    return jnp.where(jnp.abs(column - query - shift) <= RC, level, NEG)


def attention_kernel(
    total_rows, shift_ref, mask_ref, q_ref, qp_ref, qn_ref, kv_ref, out_ref, op_ref, on_ref, level_ref, bias_ref
):
    step = pl.program_id(0)
    frames, rows, cols = kv_ref.shape[1], q_ref.shape[0], q_ref.shape[1]
    open_frames = [jnp.where(mask_ref[f] == 1, 0.0, NEG) for f in range(frames - 1)] + [jnp.float32(0.0)]
    closed = jnp.int32(frames - 1)
    for f in reversed(range(frames - 1)):
        closed = jnp.where(mask_ref[f] == 1, closed, f)

    def run(slots, frame_of, open_slots):
        span = slots * cols
        padded = -(-span // 128) * 128

        @pl.when(step == 0)
        def _():
            first_row = lax.axis_index("band") * rows
            for r in range(-1, rows + 1):
                row = jnp.clip(first_row + r, 0, total_rows - 1)
                bias_ref[r + 1, :, :padded] = key_bias(cols, padded, slots, shift_ref[row], open_slots)

        def stack(which, n, part):
            pieces = [kv_ref[which, frame_of(s), n, :, part] for s in range(slots)]
            if padded > span:
                pieces.append(kv_ref[which, frame_of(0), n, : padded - span, part])
            return jnp.concatenate(pieces, axis=0)

        def query_row(r, part):
            if r < 0:
                return qp_ref[:, part]
            return qn_ref[:, part] if r == rows else q_ref[r, :, part]

        def score(j):
            part = pl.ds(j * HD, HD)
            found = []
            for n in range(rows):
                query = jnp.concatenate([query_row(r, part) for r in range(n - 1, n + 2)], axis=0)
                found.append(
                    lax.dot_general(
                        query, stack(0, n, part), (((1,), (1,)), ((), ())), preferred_element_type=jnp.float32
                    )
                )
            return found

        def soften(found):
            pieces = [[None] * 3 for _ in range(rows)]
            totals, levels = {}, {}
            for r in range(-1, rows + 1):
                bias = bias_ref[r + 1, :, :padded]
                at = [(n, r - n + 1) for n in range(max(r - 1, 0), min(r + 2, rows))]
                blocks = [found[n][d * cols : (d + 1) * cols] + bias for n, d in at]
                top = jnp.max(functools.reduce(jnp.maximum, blocks), axis=-1, keepdims=True) * SCALE2
                weights = [jnp.exp2(block * SCALE2 - top) for block in blocks]
                total = jnp.sum(functools.reduce(jnp.add, weights), axis=-1, keepdims=True)
                for (n, d), weight in zip(at, weights):
                    pieces[n][d] = weight.astype(jnp.bfloat16)
                totals[r], levels[r] = total, top
            return [jnp.concatenate(piece, axis=0) for piece in pieces], totals, levels

        lane = lax.broadcasted_iota(jnp.int32, (cols, 128), 1)

        def finish(j, weights, totals, levels):
            part = pl.ds(j * HD, HD)
            head = step * HEADS_PER_STEP + j
            sums = [
                jnp.dot(weights[n], stack(1, n, part), preferred_element_type=jnp.float32) for n in range(rows)
            ]
            for r in range(-1, rows + 1):
                near = range(max(r - 1, 0), min(r + 2, rows))
                acc = sum(sums[n][(r - n + 1) * cols : (r - n + 2) * cols] for n in near)
                out = (acc * (1.0 / totals[r])).astype(jnp.bfloat16)
                if r < 0:
                    op_ref[:, part] = out
                elif r == rows:
                    on_ref[:, part] = out
                else:
                    out_ref[r, :, part] = out
            for side, r in enumerate((-1, rows, 0, rows - 1)):
                level = levels[r] + jnp.log2(totals[r])
                level_ref[side] = jnp.where(lane == head, level, level_ref[side])

        ahead = score(0)
        for j in range(HEADS_PER_STEP):
            found = ahead
            if j + 1 < HEADS_PER_STEP:
                ahead = score(j + 1)
            finish(j, *soften(found))

    @pl.when(step == 0)
    def _():
        level_ref[...] = jnp.zeros_like(level_ref)

    @pl.when(closed < frames - 1)
    def _():
        run(
            frames - 1,
            lambda s: jnp.where(s < closed, s, s + 1),
            [jnp.where(s < closed, open_frames[s], open_frames[s + 1]) for s in range(frames - 1)],
        )

    @pl.when(closed == frames - 1)
    def _():
        run(frames, lambda s: s, open_frames)


def attention(queries, kv_frames, frame_mask, col_shift, q_prev, q_next):
    rows, cols, wide = queries.shape
    frames = kv_frames.shape[1]
    heads = wide // HD
    step_lanes = HEADS_PER_STEP * HD
    smem = pl.BlockSpec(memory_space=pltpu.SMEM)
    padded = -(-frames * cols // 128) * 128

    def fixed(shape):
        return pl.BlockSpec(shape, lambda *_: (0,) * len(shape))

    def lanes(shape):
        lead = (0,) * (len(shape) - 1)
        return pl.BlockSpec(shape, lambda h: lead + (h,))

    return pl.pallas_call(
        functools.partial(attention_kernel, col_shift.shape[0]),
        grid=(heads // HEADS_PER_STEP,),
        out_shape=(
            jax.ShapeDtypeStruct(queries.shape, jnp.bfloat16),
            jax.ShapeDtypeStruct((cols, wide), jnp.bfloat16),
            jax.ShapeDtypeStruct((cols, wide), jnp.bfloat16),
            jax.ShapeDtypeStruct((4, cols, 128), jnp.float32),
        ),
        in_specs=[
            smem,
            smem,
            lanes((rows, cols, step_lanes)),
            lanes((cols, step_lanes)),
            lanes((cols, step_lanes)),
            lanes((2, frames, rows, cols, step_lanes)),
        ],
        out_specs=(
            lanes((rows, cols, step_lanes)),
            lanes((cols, step_lanes)),
            lanes((cols, step_lanes)),
            fixed((4, cols, 128)),
        ),
        scratch_shapes=[pltpu.VMEM((rows + 2, cols, padded), jnp.float32)],
        compiler_params=pltpu.CompilerParams(vmem_limit_bytes=VMEM_BYTES),
        cost_estimate=pl.CostEstimate(
            flops=4 * rows * cols * 3 * frames * cols * wide,
            bytes_accessed=2 * rows * frames * cols * wide * 2,
            transcendentals=rows * heads * cols * 3 * frames * cols,
        ),
        name="attention",
    )(col_shift, frame_mask, queries, q_prev, q_next, kv_frames)


def greet(place, count):
    barrier = pltpu.get_barrier_semaphore()

    @pl.when(place > 0)
    def _():
        pl.semaphore_signal(barrier, 1, device_id={"band": place - 1}, device_id_type=MESH)

    @pl.when(place < count - 1)
    def _():
        pl.semaphore_signal(barrier, 1, device_id={"band": place + 1}, device_id_type=MESH)

    pl.semaphore_wait(barrier, jnp.where(place > 0, 1, 0) + jnp.where(place < count - 1, 1, 0))


def swap(place, count, sends, arrivals, up, down):
    def make(triple, other):
        source, target, at = triple
        return pltpu.make_async_remote_copy(
            src_ref=source,
            dst_ref=target,
            send_sem=sends.at[at],
            recv_sem=arrivals.at[at],
            device_id={"band": other},
            device_id_type=MESH,
        )

    ups = [make(triple, jnp.minimum(place + 1, count - 1)) for triple in up]
    downs = [make(triple, jnp.maximum(place - 1, 0)) for triple in down]

    def start(which):
        @pl.when(place < count - 1)
        def _():
            for at in which:
                ups[at].start()

        @pl.when(place > 0)
        def _():
            for at in which:
                downs[at].start()

    def arrive(which):
        @pl.when(place > 0)
        def _():
            for at in which:
                ups[at].wait_recv()

        @pl.when(place < count - 1)
        def _():
            for at in which:
                downs[at].wait_recv()

    def sent(which):
        @pl.when(place < count - 1)
        def _():
            for at in which:
                ups[at].wait_send()

        @pl.when(place > 0)
        def _():
            for at in which:
                downs[at].wait_send()

    return start, arrive, sent


def features_kernel(
    q_ref, lat_ref, cin_ref, bin_ref, gain_ref, qp_ref, qn_ref, act_out, first_out,
    below_ref, above_ref, ext_ref, pair_ref, rest_ref, win_ref, first_ref, act_ref, sends, arrivals, local_sem, out_sem
):
    place = lax.axis_index("band")
    count = lax.axis_size("band")
    last = q_ref.shape[0] - 1
    times, rows, packed = lat_ref.shape
    depth = cin_ref.shape[0] // 27
    taps = 3 * depth
    width = packed // depth
    ch = cin_ref.shape[1]
    tiles = packed // 128
    per = 128 // depth
    start, arrive, sent = swap(
        place,
        count,
        sends,
        arrivals,
        [(lat_ref, below_ref, 0), (q_ref.at[last], qp_ref, 1)],
        [(lat_ref, above_ref, 2), (q_ref.at[0], qn_ref, 3)],
    )
    greet(place, count)
    start((0, 1))

    @pl.when(place == 0)
    def _():
        below_ref[...] = jnp.zeros_like(below_ref)
        pltpu.make_async_copy(q_ref.at[0], qp_ref, local_sem.at[0]).start()

    @pl.when(place == count - 1)
    def _():
        above_ref[...] = jnp.zeros_like(above_ref)
        pltpu.make_async_copy(q_ref.at[last], qn_ref, local_sem.at[1]).start()

    at_row = (0, taps, 128)
    win_ref[...] = jnp.zeros_like(win_ref)
    for dy in range(3):
        for dt in range(3):
            source = (dt * 3 + dy) * taps
            win_ref[dy, at_row[dt] : at_row[dt] + taps] = cin_ref[source : source + taps]

    ext_ref[:, :, :128] = jnp.zeros((times, 8, 128), jnp.float32)
    ext_ref[:, :, 128 + packed :] = jnp.zeros((times, 8, 128), jnp.float32)
    lane = lax.broadcasted_iota(jnp.int32, (8, 128), 1)
    sub = lax.broadcasted_iota(jnp.int32, (8, packed), 0)

    def spread(base):
        @pl.loop(0, tiles)
        def _(t):
            here = [ext_ref[dt, :, pl.ds(pl.multiple_of((t + 1) * 128, 128), 128)] for dt in range(3)]
            left = [ext_ref[dt, :, pl.ds(pl.multiple_of(t * 128, 128), 128)] for dt in range(3)]
            right = [ext_ref[dt, :, pl.ds(pl.multiple_of((t + 2) * 128, 128), 128)] for dt in range(3)]
            for j in range(per):
                moved = []
                for dt in range(3):
                    piece = here[dt]
                    if j == 0:
                        piece = jnp.where(lane >= 128 - depth, left[dt], piece)
                    if j == per - 1:
                        piece = jnp.where(lane < depth, right[dt], piece)
                    shift = (at_row[dt] - depth * (j - 1)) % 128
                    moved.append(pltpu.roll(piece, shift, 1) if shift else piece)
                both = jnp.where(lane < taps, moved[0], jnp.where(lane < 2 * taps, moved[1], 0.0))
                at = pl.ds(base * width + t * per + j, 8, stride=width)
                pair_ref[at, :] = both
                rest_ref[at, :] = jnp.where(lane < taps, moved[2], 0.0)

    x_at = lax.broadcasted_iota(jnp.int32, (width, ch), 0)

    def features(i, group, source_rows):
        total = jnp.zeros((group * width, ch), jnp.float32)
        for dy in range(3):
            at = [pl.ds(pl.multiple_of(source_rows(i + g + dy) * width, width), width) for g in range(group)]
            source = [jnp.concatenate([ref[here, :] for here in at], axis=0) for ref in (pair_ref, rest_ref)]
            source = jnp.concatenate(source, axis=1).astype(jnp.bfloat16)
            total += jnp.dot(source, win_ref[dy], preferred_element_type=jnp.float32)
        total = total + bin_ref[...][None]
        scale = lax.rsqrt(jnp.mean(total * total, axis=-1, keepdims=True) + 1e-06)
        value = total * scale * gain_ref[...][None]
        active = value / (1.0 + jnp.exp(-value))
        for g in range(group):
            row = i + g
            outside = ((row == 0) & (place == 0)) | ((row == rows + 1) & (place == count - 1))
            mine = jnp.where(outside, 0.0, active[g * width : (g + 1) * width])
            first_ref[row] = total[g * width : (g + 1) * width]
            at = pl.ds(pl.multiple_of(row * width, width), width)
            act_ref[at, 0:ch] = jnp.where(x_at == 0, 0.0, pltpu.roll(mine, 1, 0)).astype(jnp.bfloat16)
            act_ref[at, ch : 2 * ch] = mine.astype(jnp.bfloat16)
            act_ref[at, 2 * ch : 3 * ch] = jnp.where(x_at == width - 1, 0.0, pltpu.roll(mine, width - 1, 0)).astype(
                jnp.bfloat16
            )

    for dt in range(3):
        ext_ref[dt, :, 128 : 128 + packed] = lat_ref[dt].astype(jnp.float32)
    spread(2)
    group = 2 if rows % 2 == 0 else 1

    @pl.loop(0, (rows - 2) // group)
    def _(k):
        features(2 + k * group, group, lambda y: y)

    arrive((0,))
    for dt in range(3):
        ext_ref[dt, :, 128 : 128 + packed] = jnp.where(
            sub < 4, above_ref[dt].astype(jnp.float32), below_ref[dt].astype(jnp.float32)
        )
    spread(rows + 2)
    for i in (0, rows):
        features(i, 2, lambda y: y + rows + 8 if y < 2 else y)

    acts = pltpu.make_async_copy(act_ref, act_out, out_sem.at[0])
    firsts = pltpu.make_async_copy(first_ref, first_out, out_sem.at[1])
    acts.start()
    firsts.start()
    arrive((1,))
    sent((0, 1))

    @pl.when(place == 0)
    def _():
        pltpu.make_async_copy(q_ref.at[0], qp_ref, local_sem.at[0]).wait()

    @pl.when(place == count - 1)
    def _():
        pltpu.make_async_copy(q_ref.at[last], qn_ref, local_sem.at[1]).wait()

    acts.wait()
    firsts.wait()


def features(queries, latent, conv_in, bias_in, norm_gain):
    cols, wide = queries.shape[1:]
    times, rows, packed = latent.shape
    ch = conv_in.shape[1]
    width = packed // (conv_in.shape[0] // 27)
    vmem = pl.BlockSpec(memory_space=pltpu.VMEM)
    anywhere = pl.BlockSpec(memory_space=pl.ANY)
    return pl.pallas_call(
        features_kernel,
        out_shape=(
            jax.ShapeDtypeStruct((cols, wide), jnp.bfloat16),
            jax.ShapeDtypeStruct((cols, wide), jnp.bfloat16),
            jax.ShapeDtypeStruct(((rows + 2) * width, 3 * ch), jnp.bfloat16),
            jax.ShapeDtypeStruct((rows + 2, width, ch), jnp.float32),
        ),
        in_specs=[anywhere, vmem, vmem, vmem, vmem],
        out_specs=(anywhere,) * 4,
        scratch_shapes=[
            pltpu.VMEM(latent.shape, jnp.bfloat16),
            pltpu.VMEM(latent.shape, jnp.bfloat16),
            pltpu.VMEM((times, 8, packed + 256), jnp.float32),
            pltpu.VMEM(((rows + 10) * width, 128), jnp.float32),
            pltpu.VMEM(((rows + 10) * width, 128), jnp.float32),
            pltpu.VMEM((3, 256, ch), jnp.bfloat16),
            pltpu.VMEM((rows + 2, width, ch), jnp.float32),
            pltpu.VMEM(((rows + 2) * width, 3 * ch), jnp.bfloat16),
            pltpu.SemaphoreType.DMA((4,)),
            pltpu.SemaphoreType.DMA((4,)),
            pltpu.SemaphoreType.DMA((2,)),
            pltpu.SemaphoreType.DMA((2,)),
        ],
        compiler_params=pltpu.CompilerParams(
            collective_id=0, has_side_effects=True, vmem_limit_bytes=VMEM_BYTES
        ),
        name="features",
    )(queries, latent, conv_in, bias_in, norm_gain)


def decode_kernel(
    group, part_ref, op_ref, on_ref, lev_ref, act_in, first_in, wmid_in, bmid_ref, att_ref, dec_out,
    own_ref, below_ref, above_ref, far_ref, act_ref, first_ref, wmid_ref, dec_ref, sends, arrivals, loads, outs
):
    place = lax.axis_index("band")
    count = lax.axis_size("band")
    last = part_ref.shape[0] - 1
    cols, wide = op_ref.shape
    rows, width, ch = dec_ref.shape
    start, arrive, sent = swap(
        place,
        count,
        sends,
        arrivals,
        [(on_ref, below_ref, 0), (lev_ref.at[1], far_ref.at[0], 1)],
        [(op_ref, above_ref, 2), (lev_ref.at[0], far_ref.at[1], 3)],
    )
    fetch = [
        pltpu.make_async_copy(act_in, act_ref, loads.at[0]),
        pltpu.make_async_copy(wmid_in, wmid_ref, loads.at[1]),
        pltpu.make_async_copy(first_in, first_ref, loads.at[2]),
        pltpu.make_async_copy(part_ref.at[0], own_ref.at[0], loads.at[3]),
        pltpu.make_async_copy(part_ref.at[last], own_ref.at[1], loads.at[4]),
    ]
    for copy in fetch:
        copy.start()
    greet(place, count)
    start((0, 1))

    @pl.when(place == 0)
    def _():
        below_ref[...] = jnp.zeros_like(below_ref)
        far_ref[0] = jnp.zeros((cols, 128), jnp.float32)

    @pl.when(place == count - 1)
    def _():
        above_ref[...] = jnp.zeros_like(above_ref)
        far_ref[1] = jnp.zeros((cols, 128), jnp.float32)

    for copy in fetch:
        copy.wait()

    @pl.loop(0, rows // group)
    def _(g):
        total = jnp.zeros((group * width, ch), jnp.float32)
        for dy in range(3):
            at = pl.ds(pl.multiple_of((g * group + dy) * width, width), group * width)
            total += jnp.dot(
                act_ref[at, :], wmid_ref[dy * 3 * ch : (dy + 1) * 3 * ch, :], preferred_element_type=jnp.float32
            )
        total = total + bmid_ref[...][None]
        for y in range(group):
            here = g * group + y
            dec_ref[here] = (total[y * width : (y + 1) * width] + first_ref[here + 1]).astype(jnp.bfloat16)

    decoded = pltpu.make_async_copy(dec_ref, dec_out, outs.at[0])
    decoded.start()
    arrive((0, 1))
    lane = lax.broadcasted_iota(jnp.int32, (cols, 128), 1)
    shares = []
    for side, there in ((0, place > 0), (1, place < count - 1)):
        shares.append(jnp.where(there, 1.0 / (1.0 + jnp.exp2(lev_ref[2 + side] - far_ref[side])), 0.0))

    @pl.loop(0, wide // HD)
    def _(head):
        part = pl.ds(pl.multiple_of(head * HD, HD), HD)
        for side, far in ((0, below_ref), (1, above_ref)):
            weight = jnp.sum(jnp.where(lane == head, shares[side], 0.0), axis=-1, keepdims=True)
            mine = own_ref[side, :, part].astype(jnp.float32)
            other = far[:, part].astype(jnp.float32)
            own_ref[side, :, part] = (mine + (other - mine) * weight).astype(jnp.bfloat16)

    mixed = [
        pltpu.make_async_copy(own_ref.at[0], att_ref.at[0], outs.at[1]),
        pltpu.make_async_copy(own_ref.at[1], att_ref.at[last], outs.at[2]),
    ]
    for copy in mixed:
        copy.start()
    sent((0, 1))
    for copy in mixed:
        copy.wait()
    decoded.wait()


def decode(partial, o_prev, o_next, level, active, first, conv_mid, bias_mid):
    rows = first.shape[0] - 2
    width, ch = first.shape[1:]
    cols, wide = o_prev.shape
    group = next(size for size in (4, 2, 1) if rows % size == 0)
    vmem = pl.BlockSpec(memory_space=pltpu.VMEM)
    anywhere = pl.BlockSpec(memory_space=pl.ANY)
    return pl.pallas_call(
        functools.partial(decode_kernel, group),
        out_shape=(
            jax.ShapeDtypeStruct(partial.shape, jnp.bfloat16),
            jax.ShapeDtypeStruct((rows, width, ch), jnp.bfloat16),
        ),
        in_specs=[anywhere, anywhere, anywhere, vmem, anywhere, anywhere, anywhere, vmem],
        out_specs=(anywhere, anywhere),
        input_output_aliases={0: 0},
        scratch_shapes=[
            pltpu.VMEM((2, cols, wide), jnp.bfloat16),
            pltpu.VMEM((cols, wide), jnp.bfloat16),
            pltpu.VMEM((cols, wide), jnp.bfloat16),
            pltpu.VMEM((2, cols, 128), jnp.float32),
            pltpu.VMEM(active.shape, jnp.bfloat16),
            pltpu.VMEM(first.shape, jnp.float32),
            pltpu.VMEM(conv_mid.shape, jnp.bfloat16),
            pltpu.VMEM((rows, width, ch), jnp.bfloat16),
            pltpu.SemaphoreType.DMA((4,)),
            pltpu.SemaphoreType.DMA((4,)),
            pltpu.SemaphoreType.DMA((5,)),
            pltpu.SemaphoreType.DMA((3,)),
        ],
        compiler_params=pltpu.CompilerParams(
            collective_id=1, has_side_effects=True, vmem_limit_bytes=VMEM_BYTES
        ),
        name="decode",
    )(partial, o_prev, o_next, level, active, first, conv_mid, bias_mid)


def body(
    queries, kv_frames, frame_mask, col_shift, latent, conv_in, bias_in, norm_gain, conv_mid, bias_mid
):
    q_prev, q_next, active, first = features(queries, latent, conv_in, bias_in, norm_gain)
    partial, o_prev, o_next, level = attention(queries, kv_frames, frame_mask, col_shift, q_prev, q_next)
    return tuple(decode(partial, o_prev, o_next, level, active, first, conv_mid, bias_mid))


def solution(mesh):
    placed = (
        P(("groups", "band"), None, None),
        P("groups", None, "band", None, None),
        P("groups"),
        P("groups"),
        P("groups", "band", None),
        P(),
        P(),
        P(),
        P(),
        P(),
    )
    return jax.shard_map(
        body,
        mesh=mesh,
        in_specs=placed,
        out_specs=(P(("groups", "band"), None, None), P(("groups", "band"), None, None)),
        check_vma=False,
    )
```

```python
import functools
import math

import jax
import jax.numpy as jnp
from jax import lax
from jax.experimental import pallas as pl
from jax.experimental.pallas import tpu as pltpu
from jax.sharding import PartitionSpec as P

HD = 128
RC = 8
NEG = -1e30
MESH = pl.DeviceIdType.MESH
SCALE2 = math.log2(math.e) / math.sqrt(HD)
HEADS_PER_STEP = 4
EDGE_HEADS = 10
VMEM_BYTES = 56 * 2**20


def to_next(block, axis):
    count = lax.axis_size(axis)
    return lax.ppermute(block, axis, [(i, i + 1) for i in range(count - 1)])


def to_previous(block, axis):
    count = lax.axis_size(axis)
    return lax.ppermute(block, axis, [(i + 1, i) for i in range(count - 1)])


def key_bias(cols, padded, slots, shift, open_slots):
    lane = lax.broadcasted_iota(jnp.int32, (cols, padded), 1)
    query = lax.broadcasted_iota(jnp.int32, (cols, padded), 0)
    column = lane
    level = jnp.full((cols, padded), NEG, jnp.float32)
    for s in range(slots):
        inside = (lane >= s * cols) & (lane < (s + 1) * cols)
        level = jnp.where(inside, open_slots[s], level)
        column = jnp.where(lane >= s * cols, lane - s * cols, column)
    return jnp.where(jnp.abs(column - query - shift) <= RC, level, NEG)


def heads_per_step(heads, most):
    return next(size for size in range(min(most, heads), 0, -1) if heads % size == 0)


def over_frames(mask_ref, frames, run):
    open_frames = [jnp.where(mask_ref[f] == 1, 0.0, NEG) for f in range(frames - 1)] + [jnp.float32(0.0)]
    closed = jnp.int32(frames - 1)
    for f in reversed(range(frames - 1)):
        closed = jnp.where(mask_ref[f] == 1, closed, f)

    @pl.when(closed < frames - 1)
    def _():
        run(
            lambda s: jnp.where(s < closed, s, s + 1),
            [jnp.where(s < closed, open_frames[s], open_frames[s + 1]) for s in range(frames - 1)],
        )

    @pl.when(closed == frames - 1)
    def _():
        run(lambda s: s, open_frames)


def attend(total_rows, cols, shift_ref, bias_ref, plan, places, query_row, kv_row, emit, each, frame_of, open_slots):
    step = pl.program_id(0)
    slots = len(open_slots)
    span = slots * cols
    padded = -(-span // 128) * 128
    queries = sorted({r for _, seen in plan for r in seen})
    near = {r: [(k, seen.index(r)) for k, (_, seen) in enumerate(plan) if r in seen] for r in queries}

    @pl.when(step == 0)
    def _():
        for at, r in enumerate(queries):
            row = jnp.clip(places[r], 0, total_rows - 1)
            bias_ref[at, :, :padded] = key_bias(cols, padded, slots, shift_ref[row], open_slots)

    def stack(which, n, part):
        pieces = [kv_row(which, frame_of(s), n, slice(None), part) for s in range(slots)]
        if padded > span:
            pieces.append(kv_row(which, frame_of(0), n, slice(0, padded - span), part))
        return jnp.concatenate(pieces, axis=0)

    def score(j):
        part = pl.ds(j * HD, HD)
        found = []
        for n, seen in plan:
            query = jnp.concatenate([query_row(r, part) for r in seen], axis=0)
            found.append(
                lax.dot_general(query, stack(0, n, part), (((1,), (1,)), ((), ())), preferred_element_type=jnp.float32)
            )
        return found

    def soften(found):
        pieces = [[None] * len(seen) for _, seen in plan]
        totals, tops = {}, {}
        for row, r in enumerate(queries):
            bias = bias_ref[row, :, :padded]
            blocks = [found[k][d * cols : (d + 1) * cols] + bias for k, d in near[r]]
            top = jnp.max(functools.reduce(jnp.maximum, blocks), axis=-1, keepdims=True) * SCALE2
            weights = [jnp.exp2(block * SCALE2 - top) for block in blocks]
            totals[r] = jnp.sum(functools.reduce(jnp.add, weights), axis=-1, keepdims=True)
            tops[r] = top
            for (k, d), weight in zip(near[r], weights):
                pieces[k][d] = weight.astype(jnp.bfloat16)
        return [jnp.concatenate(piece, axis=0) for piece in pieces], totals, tops

    def finish(j, weights, totals, tops):
        part = pl.ds(j * HD, HD)
        sums = [
            jnp.dot(weights[k], stack(1, n, part), preferred_element_type=jnp.float32)
            for k, (n, _) in enumerate(plan)
        ]
        for r in queries:
            acc = functools.reduce(jnp.add, [sums[k][d * cols : (d + 1) * cols] for k, d in near[r]])
            emit(j, step * each + j, r, (acc * (1.0 / totals[r])).astype(jnp.bfloat16), tops[r], totals[r])

    ahead = score(0)
    for j in range(each):
        found = ahead
        if j + 1 < each:
            ahead = score(j + 1)
        finish(j, *soften(found))


def edge_kernel(
    total_rows, rows, each, shift_ref, mask_ref, qp_ref, qn_ref, kvf_ref, kvl_ref, op_ref, on_ref, bias_ref, level_ref
):
    step = pl.program_id(0)
    frames, cols = kvf_ref.shape[1], kvf_ref.shape[3]
    wide = op_ref.shape[1] - 3 * 128
    first_row = lax.axis_index("band") * rows
    lane = lax.broadcasted_iota(jnp.int32, (cols, 128), 1)
    sources, keys, targets = (qp_ref, qn_ref), (kvf_ref, kvl_ref), (op_ref, on_ref)

    @pl.when(step == 0)
    def _():
        level_ref[...] = jnp.zeros_like(level_ref)

    def emit(j, head, r, out, top, total):
        targets[r][:, pl.ds(pl.multiple_of(head * HD, HD), HD)] = out
        level_ref[r] = jnp.where(lane == head, top + jnp.log2(total), level_ref[r])

    over_frames(
        mask_ref,
        frames,
        functools.partial(
            attend,
            total_rows,
            cols,
            shift_ref,
            bias_ref,
            [(0, [0]), (1, [1])],
            [first_row - 1, first_row + rows],
            lambda r, part: sources[r][:, part],
            lambda which, f, n, some, part: keys[n][which, f, 0, some, part],
            emit,
            each,
        ),
    )

    @pl.when(step == pl.num_programs(0) - 1)
    def _():
        for side, o_ref in enumerate(targets):
            rest = level_ref[side]
            for k in range(3):
                piece = rest.astype(jnp.bfloat16)
                o_ref[:, wide + k * 128 : wide + (k + 1) * 128] = piece
                rest = rest - piece.astype(jnp.float32)


def main_kernel(total_rows, each, shift_ref, mask_ref, q_ref, kv_ref, out_ref, level_ref, bias_ref):
    step = pl.program_id(0)
    frames, rows, cols = kv_ref.shape[1], q_ref.shape[0], q_ref.shape[1]
    first_row = lax.axis_index("band") * rows
    lane = lax.broadcasted_iota(jnp.int32, (cols, 128), 1)

    @pl.when(step == 0)
    def _():
        level_ref[...] = jnp.zeros_like(level_ref)

    def emit(j, head, r, out, top, total):
        out_ref[r, :, j * HD : (j + 1) * HD] = out
        for side, edge in enumerate((0, rows - 1)):
            if r == edge:
                level_ref[side] = jnp.where(lane == head, top + jnp.log2(total), level_ref[side])

    over_frames(
        mask_ref,
        frames,
        functools.partial(
            attend,
            total_rows,
            cols,
            shift_ref,
            bias_ref,
            [(n, list(range(max(n - 1, 0), min(n + 2, rows)))) for n in range(rows)],
            [first_row + r for r in range(rows)],
            lambda r, part: q_ref[r, :, part],
            lambda which, f, n, some, part: kv_ref[which, f, n, some, part],
            emit,
            each,
        ),
    )


def combine_kernel(own_ref, lev_ref, op_ref, on_ref, out_ref):
    side = pl.program_id(0)
    place = lax.axis_index("band")
    count = lax.axis_size("band")
    cols, lanes = own_ref.shape[1], own_ref.shape[2]
    wide = op_ref.shape[1] - 3 * 128
    lane = lax.broadcasted_iota(jnp.int32, (cols, 128), 1)

    def mix(o_ref, there):
        other = sum(o_ref[:, wide + k * 128 : wide + (k + 1) * 128].astype(jnp.float32) for k in range(3))
        share = jnp.where(there, 1.0 / (1.0 + jnp.exp2(lev_ref[side] - other)), 0.0)
        for j in range(lanes // HD):
            weight = jnp.sum(jnp.where(lane == j, share, 0.0), axis=-1, keepdims=True)
            here = own_ref[0, :, j * HD : (j + 1) * HD].astype(jnp.float32)
            far = o_ref[:, j * HD : (j + 1) * HD].astype(jnp.float32)
            out_ref[0, :, j * HD : (j + 1) * HD] = (here + (far - here) * weight).astype(jnp.bfloat16)

    @pl.when(side == 0)
    def _():
        mix(op_ref, place > 0)

    @pl.when(side == 1)
    def _():
        mix(on_ref, place < count - 1)


def fixed(shape):
    return pl.BlockSpec(shape, lambda *_: (0,) * len(shape))


def lanes(shape, row=None):
    lead = (0,) * (len(shape) - 1) if row is None else (0,) * (len(shape) - 3) + (row, 0)
    return pl.BlockSpec(shape, lambda h: lead + (h,))


def edge_attention(kv_frames, frame_mask, col_shift, q_prev, q_next):
    frames, rows, cols, wide = kv_frames.shape[1:]
    heads = wide // HD
    each = heads_per_step(heads, EDGE_HEADS)
    smem = pl.BlockSpec(memory_space=pltpu.SMEM)
    packed = wide + 3 * 128
    padded = -(-frames * cols // 128) * 128
    return pl.pallas_call(
        functools.partial(edge_kernel, col_shift.shape[0], rows, each),
        grid=(heads // each,),
        out_shape=(jax.ShapeDtypeStruct((cols, packed), jnp.bfloat16),) * 2,
        in_specs=[
            smem,
            smem,
            lanes((cols, each * HD)),
            lanes((cols, each * HD)),
            lanes((2, frames, 1, cols, each * HD), 0),
            lanes((2, frames, 1, cols, each * HD), rows - 1),
        ],
        out_specs=(fixed((cols, packed)),) * 2,
        scratch_shapes=[
            pltpu.VMEM((2, cols, padded), jnp.float32),
            pltpu.VMEM((2, cols, 128), jnp.float32),
        ],
        compiler_params=pltpu.CompilerParams(vmem_limit_bytes=VMEM_BYTES),
        cost_estimate=pl.CostEstimate(
            flops=8 * cols * frames * cols * wide,
            bytes_accessed=4 * frames * cols * wide * 2,
            transcendentals=2 * heads * cols * frames * cols,
        ),
        name="edge_attention",
    )(col_shift, frame_mask, q_prev, q_next, kv_frames, kv_frames)


def main_attention(queries, kv_frames, frame_mask, col_shift):
    rows, cols, wide = queries.shape
    frames = kv_frames.shape[1]
    heads = wide // HD
    each = heads_per_step(heads, HEADS_PER_STEP)
    smem = pl.BlockSpec(memory_space=pltpu.SMEM)
    padded = -(-frames * cols // 128) * 128
    return pl.pallas_call(
        functools.partial(main_kernel, col_shift.shape[0], each),
        grid=(heads // each,),
        out_shape=(
            jax.ShapeDtypeStruct(queries.shape, jnp.bfloat16),
            jax.ShapeDtypeStruct((2, cols, 128), jnp.float32),
        ),
        in_specs=[smem, smem, lanes((rows, cols, each * HD)), lanes((2, frames, rows, cols, each * HD))],
        out_specs=(lanes((rows, cols, each * HD)), fixed((2, cols, 128))),
        scratch_shapes=[pltpu.VMEM((rows, cols, padded), jnp.float32)],
        compiler_params=pltpu.CompilerParams(vmem_limit_bytes=VMEM_BYTES),
        cost_estimate=pl.CostEstimate(
            flops=4 * rows * cols * 3 * frames * cols * wide,
            bytes_accessed=2 * rows * frames * cols * wide * 2,
            transcendentals=rows * heads * cols * 3 * frames * cols,
        ),
        name="main_attention",
    )(col_shift, frame_mask, queries, kv_frames)


def combine(partial, level, back_prev, back_next):
    rows, cols, wide = partial.shape
    edge = pl.BlockSpec((1, cols, wide), lambda s: (s * (rows - 1), 0, 0))
    return pl.pallas_call(
        combine_kernel,
        grid=(2,),
        out_shape=jax.ShapeDtypeStruct(partial.shape, jnp.bfloat16),
        in_specs=[edge, fixed(level.shape), fixed(back_prev.shape), fixed(back_next.shape)],
        out_specs=edge,
        input_output_aliases={0: 0},
        compiler_params=pltpu.CompilerParams(vmem_limit_bytes=VMEM_BYTES),
        name="combine",
    )(partial, level, back_prev, back_next)


def greet(place, count):
    barrier = pltpu.get_barrier_semaphore()

    @pl.when(place > 0)
    def _():
        pl.semaphore_signal(barrier, 1, device_id={"band": place - 1}, device_id_type=MESH)

    @pl.when(place < count - 1)
    def _():
        pl.semaphore_signal(barrier, 1, device_id={"band": place + 1}, device_id_type=MESH)

    pl.semaphore_wait(barrier, jnp.where(place > 0, 1, 0) + jnp.where(place < count - 1, 1, 0))


def swap(place, count, sends, arrivals, up, down):
    def make(triple, other):
        source, target, at = triple
        return pltpu.make_async_remote_copy(
            src_ref=source,
            dst_ref=target,
            send_sem=sends.at[at],
            recv_sem=arrivals.at[at],
            device_id={"band": other},
            device_id_type=MESH,
        )

    ups = [make(triple, jnp.minimum(place + 1, count - 1)) for triple in up]
    downs = [make(triple, jnp.maximum(place - 1, 0)) for triple in down]

    def start(which):
        @pl.when(place < count - 1)
        def _():
            for at in which:
                ups[at].start()

        @pl.when(place > 0)
        def _():
            for at in which:
                downs[at].start()

    def arrive(which):
        @pl.when(place > 0)
        def _():
            for at in which:
                ups[at].wait_recv()

        @pl.when(place < count - 1)
        def _():
            for at in which:
                downs[at].wait_recv()

    def sent(which):
        @pl.when(place < count - 1)
        def _():
            for at in which:
                ups[at].wait_send()

        @pl.when(place > 0)
        def _():
            for at in which:
                downs[at].wait_send()

    return start, arrive, sent


def decoder_kernel(
    q_ref, lat_ref, cin_ref, wmid_in, bin_ref, gain_ref, bmid_ref, qp_ref, qn_ref, dec_out,
    high_ref, low_ref, below_ref, above_ref, ext_ref, pair_ref, rest_ref, win_ref, wmid_ref, first_ref, act_ref, dec_ref,
    sends, arrivals, local_sem, load_sem, out_sem
):
    place = lax.axis_index("band")
    count = lax.axis_size("band")
    last = q_ref.shape[0] - 1
    times, rows, packed = lat_ref.shape
    depth = cin_ref.shape[0] // 27
    taps = 3 * depth
    width = packed // depth
    ch = cin_ref.shape[1]
    tiles = packed // 128
    per = 128 // depth
    start, arrive, sent = swap(
        place,
        count,
        sends,
        arrivals,
        [(high_ref, below_ref, 0), (q_ref.at[last], qp_ref, 1)],
        [(low_ref, above_ref, 2), (q_ref.at[0], qn_ref, 3)],
    )
    middle = pltpu.make_async_copy(wmid_in, wmid_ref, load_sem.at[0])
    middle.start()
    sub = lax.broadcasted_iota(jnp.int32, (8, packed), 0)

    def gather(target, shifts):
        rows_of = [pltpu.roll(lat_ref[dt].astype(jnp.float32), shifts[dt], 0) for dt in range(3)]
        target[...] = jnp.where(sub < 2, rows_of[0], jnp.where(sub < 4, rows_of[1], rows_of[2])).astype(jnp.bfloat16)

    gather(high_ref, [2, 4, 6])
    gather(low_ref, [0, 2, 4])
    greet(place, count)
    start((0, 1))

    @pl.when(place == 0)
    def _():
        below_ref[...] = jnp.zeros_like(below_ref)
        pltpu.make_async_copy(q_ref.at[0], qp_ref, local_sem.at[0]).start()

    @pl.when(place == count - 1)
    def _():
        above_ref[...] = jnp.zeros_like(above_ref)
        pltpu.make_async_copy(q_ref.at[last], qn_ref, local_sem.at[1]).start()

    at_row = (0, taps, 128)
    win_ref[...] = jnp.zeros_like(win_ref)
    for dy in range(3):
        for dt in range(3):
            source = (dt * 3 + dy) * taps
            win_ref[dy, at_row[dt] : at_row[dt] + taps] = cin_ref[source : source + taps]

    ext_ref[:, :, :128] = jnp.zeros((times, 8, 128), jnp.float32)
    ext_ref[:, :, 128 + packed :] = jnp.zeros((times, 8, 128), jnp.float32)
    lane = lax.broadcasted_iota(jnp.int32, (8, 128), 1)

    def spread(base):
        @pl.loop(0, tiles)
        def _(t):
            here = [ext_ref[dt, :, pl.ds(pl.multiple_of((t + 1) * 128, 128), 128)] for dt in range(3)]
            left = [ext_ref[dt, :, pl.ds(pl.multiple_of(t * 128, 128), 128)] for dt in range(3)]
            right = [ext_ref[dt, :, pl.ds(pl.multiple_of((t + 2) * 128, 128), 128)] for dt in range(3)]
            for j in range(per):
                moved = []
                for dt in range(3):
                    piece = here[dt]
                    if j == 0:
                        piece = jnp.where(lane >= 128 - depth, left[dt], piece)
                    if j == per - 1:
                        piece = jnp.where(lane < depth, right[dt], piece)
                    shift = (at_row[dt] - depth * (j - 1)) % 128
                    moved.append(pltpu.roll(piece, shift, 1) if shift else piece)
                both = jnp.where(lane < taps, moved[0], jnp.where(lane < 2 * taps, moved[1], 0.0))
                at = pl.ds(base * width + t * per + j, 8, stride=width)
                pair_ref[at, :] = both
                rest_ref[at, :] = jnp.where(lane < taps, moved[2], 0.0)

    x_at = lax.broadcasted_iota(jnp.int32, (width, ch), 0)

    def features(i, group, source_rows):
        total = jnp.zeros((group * width, ch), jnp.float32)
        for dy in range(3):
            at = [pl.ds(pl.multiple_of(source_rows(i + g + dy) * width, width), width) for g in range(group)]
            source = [jnp.concatenate([ref[here, :] for here in at], axis=0) for ref in (pair_ref, rest_ref)]
            source = jnp.concatenate(source, axis=1).astype(jnp.bfloat16)
            total += jnp.dot(source, win_ref[dy], preferred_element_type=jnp.float32)
        total = total + bin_ref[...][None]
        scale = lax.rsqrt(jnp.mean(total * total, axis=-1, keepdims=True) + 1e-06)
        value = total * scale * gain_ref[...][None]
        active = value / (1.0 + jnp.exp(-value))
        for g in range(group):
            row = i + g
            outside = ((row == 0) & (place == 0)) | ((row == rows + 1) & (place == count - 1))
            mine = jnp.where(outside, 0.0, active[g * width : (g + 1) * width])
            first_ref[row] = total[g * width : (g + 1) * width]
            at = pl.ds(pl.multiple_of(row * width, width), width)
            act_ref[at, 0:ch] = jnp.where(x_at == 0, 0.0, pltpu.roll(mine, 1, 0)).astype(jnp.bfloat16)
            act_ref[at, ch : 2 * ch] = mine.astype(jnp.bfloat16)
            act_ref[at, 2 * ch : 3 * ch] = jnp.where(x_at == width - 1, 0.0, pltpu.roll(mine, width - 1, 0)).astype(
                jnp.bfloat16
            )

    for dt in range(3):
        ext_ref[dt, :, 128 : 128 + packed] = lat_ref[dt].astype(jnp.float32)
    spread(2)
    group = 2 if rows % 2 == 0 else 1

    @pl.loop(0, (rows - 2) // group)
    def _(k):
        features(2 + k * group, group, lambda y: y)

    arrive((0,))
    for dt in range(3):
        up = pltpu.roll(above_ref[...].astype(jnp.float32), (8 - 2 * dt) % 8, 0)
        down = pltpu.roll(below_ref[...].astype(jnp.float32), 6 - 2 * dt, 0)
        ext_ref[dt, :, 128 : 128 + packed] = jnp.where(sub < 4, up, down)
    spread(rows + 2)
    for i in (0, rows):
        features(i, 2, lambda y: y + rows + 8 if y < 2 else y)

    middle.wait()
    many = next(size for size in (4, 2, 1) if rows % size == 0)

    @pl.loop(0, rows // many)
    def _(g):
        total = jnp.zeros((many * width, ch), jnp.float32)
        for dy in range(3):
            at = pl.ds(pl.multiple_of((g * many + dy) * width, width), many * width)
            total += jnp.dot(
                act_ref[at, :], wmid_ref[dy * 3 * ch : (dy + 1) * 3 * ch, :], preferred_element_type=jnp.float32
            )
        total = total + bmid_ref[...][None]
        for y in range(many):
            here = g * many + y
            dec_ref[here] = (total[y * width : (y + 1) * width] + first_ref[here + 1]).astype(jnp.bfloat16)

    decoded = pltpu.make_async_copy(dec_ref, dec_out, out_sem.at[0])
    decoded.start()
    arrive((1,))
    sent((0, 1))

    @pl.when(place == 0)
    def _():
        pltpu.make_async_copy(q_ref.at[0], qp_ref, local_sem.at[0]).wait()

    @pl.when(place == count - 1)
    def _():
        pltpu.make_async_copy(q_ref.at[last], qn_ref, local_sem.at[1]).wait()

    decoded.wait()


def decoder(queries, latent, conv_in, bias_in, norm_gain, conv_mid, bias_mid):
    cols, wide = queries.shape[1:]
    times, rows, packed = latent.shape
    ch = conv_in.shape[1]
    width = packed // (conv_in.shape[0] // 27)
    vmem = pl.BlockSpec(memory_space=pltpu.VMEM)
    anywhere = pl.BlockSpec(memory_space=pl.ANY)
    return pl.pallas_call(
        decoder_kernel,
        out_shape=(
            jax.ShapeDtypeStruct((cols, wide), jnp.bfloat16),
            jax.ShapeDtypeStruct((cols, wide), jnp.bfloat16),
            jax.ShapeDtypeStruct((rows, width, ch), jnp.bfloat16),
        ),
        in_specs=[anywhere, vmem, vmem, anywhere, vmem, vmem, vmem],
        out_specs=(anywhere,) * 3,
        scratch_shapes=[
            *[pltpu.VMEM((8, packed), jnp.bfloat16)] * 4,
            pltpu.VMEM((times, 8, packed + 256), jnp.float32),
            pltpu.VMEM(((rows + 10) * width, 128), jnp.float32),
            pltpu.VMEM(((rows + 10) * width, 128), jnp.float32),
            pltpu.VMEM((3, 256, ch), jnp.bfloat16),
            pltpu.VMEM(conv_mid.shape, jnp.bfloat16),
            pltpu.VMEM((rows + 2, width, ch), jnp.float32),
            pltpu.VMEM(((rows + 2) * width, 3 * ch), jnp.bfloat16),
            pltpu.VMEM((rows, width, ch), jnp.bfloat16),
            pltpu.SemaphoreType.DMA((4,)),
            pltpu.SemaphoreType.DMA((4,)),
            pltpu.SemaphoreType.DMA((2,)),
            pltpu.SemaphoreType.DMA((1,)),
            pltpu.SemaphoreType.DMA((1,)),
        ],
        compiler_params=pltpu.CompilerParams(
            collective_id=0, has_side_effects=True, vmem_limit_bytes=VMEM_BYTES
        ),
        name="decoder",
    )(queries, latent, conv_in, conv_mid, bias_in, norm_gain, bias_mid)


def body(
    queries, kv_frames, frame_mask, col_shift, latent, conv_in, bias_in, norm_gain, conv_mid, bias_mid
):
    q_prev, q_next, decoded = decoder(queries, latent, conv_in, bias_in, norm_gain, conv_mid, bias_mid)
    o_prev, o_next = edge_attention(kv_frames, frame_mask, col_shift, q_prev, q_next)
    back_prev = to_next(o_next, "band")
    back_next = to_previous(o_prev, "band")
    partial, level = main_attention(queries, kv_frames, frame_mask, col_shift)
    return (combine(partial, level, back_prev, back_next), decoded)


def solution(mesh):
    placed = (
        P(("groups", "band"), None, None),
        P("groups", None, "band", None, None),
        P("groups"),
        P("groups"),
        P("groups", "band", None),
        P(),
        P(),
        P(),
        P(),
        P(),
    )
    return jax.shard_map(
        body,
        mesh=mesh,
        in_specs=placed,
        out_specs=(P(("groups", "band"), None, None), P(("groups", "band"), None, None)),
        check_vma=False,
    )
```

```python
import functools
import math

import jax
import jax.numpy as jnp
from jax import lax
from jax.experimental import pallas as pl
from jax.experimental.pallas import tpu as pltpu
from jax.sharding import PartitionSpec as P

HD = 128
RC = 8
NEG = -1e30
MESH = pl.DeviceIdType.MESH
SCALE2 = math.log2(math.e) / math.sqrt(HD)
HEADS_PER_STEP = 5
EDGE_HEADS = 10
VMEM_BYTES = 56 * 2**20


def to_next(block, axis):
    count = lax.axis_size(axis)
    return lax.ppermute(block, axis, [(i, i + 1) for i in range(count - 1)])


def to_previous(block, axis):
    count = lax.axis_size(axis)
    return lax.ppermute(block, axis, [(i + 1, i) for i in range(count - 1)])


def key_bias(cols, padded, slots, shift, open_slots):
    lane = lax.broadcasted_iota(jnp.int32, (cols, padded), 1)
    query = lax.broadcasted_iota(jnp.int32, (cols, padded), 0)
    column = lane
    level = jnp.full((cols, padded), NEG, jnp.float32)
    for s in range(slots):
        inside = (lane >= s * cols) & (lane < (s + 1) * cols)
        level = jnp.where(inside, open_slots[s], level)
        column = jnp.where(lane >= s * cols, lane - s * cols, column)
    return jnp.where(jnp.abs(column - query - shift) <= RC, level, NEG)


def heads_per_step(heads, most):
    return next(size for size in range(min(most, heads), 0, -1) if heads % size == 0)


def over_frames(mask_ref, frames, run):
    open_frames = [jnp.where(mask_ref[f] == 1, 0.0, NEG) for f in range(frames - 1)] + [jnp.float32(0.0)]
    closed = jnp.int32(frames - 1)
    for f in reversed(range(frames - 1)):
        closed = jnp.where(mask_ref[f] == 1, closed, f)

    @pl.when(closed < frames - 1)
    def _():
        run(
            lambda s: jnp.where(s < closed, s, s + 1),
            [jnp.where(s < closed, open_frames[s], open_frames[s + 1]) for s in range(frames - 1)],
        )

    @pl.when(closed == frames - 1)
    def _():
        run(lambda s: s, open_frames)


def attend(total_rows, cols, shift_ref, bias_ref, plan, places, query_row, kv_row, emit, each, ahead, frame_of, open_slots):
    step = pl.program_id(0)
    slots = len(open_slots)
    span = slots * cols
    padded = -(-span // 128) * 128
    queries = sorted({r for _, seen in plan for r in seen})
    near = {r: [(k, seen.index(r)) for k, (_, seen) in enumerate(plan) if r in seen] for r in queries}

    @pl.when(step == 0)
    def _():
        for at, r in enumerate(queries):
            row = jnp.clip(places[r], 0, total_rows - 1)
            bias_ref[at, :, :padded] = key_bias(cols, padded, slots, shift_ref[row], open_slots)

    def stack(which, n, part):
        pieces = [kv_row(which, frame_of(s), n, slice(None), part) for s in range(slots)]
        if padded > span:
            pieces.append(kv_row(which, frame_of(0), n, slice(0, padded - span), part))
        return jnp.concatenate(pieces, axis=0)

    def score(j):
        part = pl.ds(j * HD, HD)
        found = []
        for n, seen in plan:
            query = jnp.concatenate([query_row(r, part) for r in seen], axis=0)
            found.append(
                lax.dot_general(query, stack(0, n, part), (((1,), (1,)), ((), ())), preferred_element_type=jnp.float32)
            )
        return found

    def soften(found):
        pieces = [[None] * len(seen) for _, seen in plan]
        totals, tops = {}, {}
        for row, r in enumerate(queries):
            bias = bias_ref[row, :, :padded]
            blocks = [found[k][d * cols : (d + 1) * cols] + bias for k, d in near[r]]
            top = jnp.max(functools.reduce(jnp.maximum, blocks), axis=-1, keepdims=True) * SCALE2
            weights = [jnp.exp2(block * SCALE2 - top) for block in blocks]
            totals[r] = jnp.sum(functools.reduce(jnp.add, weights), axis=-1, keepdims=True)
            tops[r] = top
            for (k, d), weight in zip(near[r], weights):
                pieces[k][d] = weight.astype(jnp.bfloat16)
        return [jnp.concatenate(piece, axis=0) for piece in pieces], totals, tops

    def finish(j, weights, totals, tops):
        part = pl.ds(j * HD, HD)
        sums = [
            jnp.dot(weights[k], stack(1, n, part), preferred_element_type=jnp.float32)
            for k, (n, _) in enumerate(plan)
        ]
        for r in queries:
            acc = functools.reduce(jnp.add, [sums[k][d * cols : (d + 1) * cols] for k, d in near[r]])
            emit(j, step * each + j, r, (acc * (1.0 / totals[r])).astype(jnp.bfloat16), tops[r], totals[r])

    found, soft = {}, {}
    for j in range(each + ahead[0]):
        if j < each:
            found[j] = score(j)
        at = j - ahead[1]
        if 0 <= at < each:
            soft[at] = soften(found.pop(at))
        if j >= ahead[0]:
            finish(j - ahead[0], *soft.pop(j - ahead[0]))


def edge_kernel(
    total_rows, rows, each, shift_ref, mask_ref, qp_ref, qn_ref, kvf_ref, kvl_ref, op_ref, on_ref, bias_ref, level_ref
):
    step = pl.program_id(0)
    frames, cols = kvf_ref.shape[1], kvf_ref.shape[3]
    wide = op_ref.shape[1] - 3 * 128
    first_row = lax.axis_index("band") * rows
    lane = lax.broadcasted_iota(jnp.int32, (cols, 128), 1)
    sources, keys, targets = (qp_ref, qn_ref), (kvf_ref, kvl_ref), (op_ref, on_ref)

    @pl.when(step == 0)
    def _():
        level_ref[...] = jnp.zeros_like(level_ref)

    def emit(j, head, r, out, top, total):
        targets[r][:, pl.ds(pl.multiple_of(head * HD, HD), HD)] = out
        level_ref[r] = jnp.where(lane == head, top + jnp.log2(total), level_ref[r])

    over_frames(
        mask_ref,
        frames,
        functools.partial(
            attend,
            total_rows,
            cols,
            shift_ref,
            bias_ref,
            [(0, [0]), (1, [1])],
            [first_row - 1, first_row + rows],
            lambda r, part: sources[r][:, part],
            lambda which, f, n, some, part: keys[n][which, f, 0, some, part],
            emit,
            each,
            (3, 1),
        ),
    )

    @pl.when(step == pl.num_programs(0) - 1)
    def _():
        for side, o_ref in enumerate(targets):
            rest = level_ref[side]
            for k in range(3):
                piece = rest.astype(jnp.bfloat16)
                o_ref[:, wide + k * 128 : wide + (k + 1) * 128] = piece
                rest = rest - piece.astype(jnp.float32)


def main_kernel(total_rows, each, shift_ref, mask_ref, q_ref, kv_ref, out_ref, level_ref, bias_ref):
    step = pl.program_id(0)
    frames, rows, cols = kv_ref.shape[1], q_ref.shape[0], q_ref.shape[1]
    first_row = lax.axis_index("band") * rows
    lane = lax.broadcasted_iota(jnp.int32, (cols, 128), 1)

    @pl.when(step == 0)
    def _():
        level_ref[...] = jnp.zeros_like(level_ref)

    def emit(j, head, r, out, top, total):
        out_ref[r, :, j * HD : (j + 1) * HD] = out
        for side, edge in enumerate((0, rows - 1)):
            if r == edge:
                level_ref[side] = jnp.where(lane == head, top + jnp.log2(total), level_ref[side])

    over_frames(
        mask_ref,
        frames,
        functools.partial(
            attend,
            total_rows,
            cols,
            shift_ref,
            bias_ref,
            [(n, list(range(max(n - 1, 0), min(n + 2, rows)))) for n in range(rows)],
            [first_row + r for r in range(rows)],
            lambda r, part: q_ref[r, :, part],
            lambda which, f, n, some, part: kv_ref[which, f, n, some, part],
            emit,
            each,
            (1, 1),
        ),
    )


def combine_kernel(own_ref, lev_ref, op_ref, on_ref, out_ref):
    side = pl.program_id(0)
    place = lax.axis_index("band")
    count = lax.axis_size("band")
    cols, lanes = own_ref.shape[1], own_ref.shape[2]
    wide = op_ref.shape[1] - 3 * 128
    lane = lax.broadcasted_iota(jnp.int32, (cols, 128), 1)

    def mix(o_ref, there):
        other = sum(o_ref[:, wide + k * 128 : wide + (k + 1) * 128].astype(jnp.float32) for k in range(3))
        share = jnp.where(there, 1.0 / (1.0 + jnp.exp2(lev_ref[side] - other)), 0.0)
        for j in range(lanes // HD):
            weight = jnp.sum(jnp.where(lane == j, share, 0.0), axis=-1, keepdims=True)
            here = own_ref[0, :, j * HD : (j + 1) * HD].astype(jnp.float32)
            far = o_ref[:, j * HD : (j + 1) * HD].astype(jnp.float32)
            out_ref[0, :, j * HD : (j + 1) * HD] = (here + (far - here) * weight).astype(jnp.bfloat16)

    @pl.when(side == 0)
    def _():
        mix(op_ref, place > 0)

    @pl.when(side == 1)
    def _():
        mix(on_ref, place < count - 1)


def fixed(shape):
    return pl.BlockSpec(shape, lambda *_: (0,) * len(shape))


def lanes(shape, row=None):
    lead = (0,) * (len(shape) - 1) if row is None else (0,) * (len(shape) - 3) + (row, 0)
    return pl.BlockSpec(shape, lambda h: lead + (h,))


def edge_attention(kv_frames, frame_mask, col_shift, q_prev, q_next):
    frames, rows, cols, wide = kv_frames.shape[1:]
    heads = wide // HD
    each = heads_per_step(heads, EDGE_HEADS)
    smem = pl.BlockSpec(memory_space=pltpu.SMEM)
    packed = wide + 3 * 128
    padded = -(-frames * cols // 128) * 128
    return pl.pallas_call(
        functools.partial(edge_kernel, col_shift.shape[0], rows, each),
        grid=(heads // each,),
        out_shape=(jax.ShapeDtypeStruct((cols, packed), jnp.bfloat16),) * 2,
        in_specs=[
            smem,
            smem,
            lanes((cols, each * HD)),
            lanes((cols, each * HD)),
            lanes((2, frames, 1, cols, each * HD), 0),
            lanes((2, frames, 1, cols, each * HD), rows - 1),
        ],
        out_specs=(fixed((cols, packed)),) * 2,
        scratch_shapes=[
            pltpu.VMEM((2, cols, padded), jnp.float32),
            pltpu.VMEM((2, cols, 128), jnp.float32),
        ],
        compiler_params=pltpu.CompilerParams(vmem_limit_bytes=VMEM_BYTES),
        cost_estimate=pl.CostEstimate(
            flops=8 * cols * frames * cols * wide,
            bytes_accessed=4 * frames * cols * wide * 2,
            transcendentals=2 * heads * cols * frames * cols,
        ),
        name="edge_attention",
    )(col_shift, frame_mask, q_prev, q_next, kv_frames, kv_frames)


def main_attention(queries, kv_frames, frame_mask, col_shift):
    rows, cols, wide = queries.shape
    frames = kv_frames.shape[1]
    heads = wide // HD
    each = heads_per_step(heads, HEADS_PER_STEP)
    smem = pl.BlockSpec(memory_space=pltpu.SMEM)
    padded = -(-frames * cols // 128) * 128
    return pl.pallas_call(
        functools.partial(main_kernel, col_shift.shape[0], each),
        grid=(heads // each,),
        out_shape=(
            jax.ShapeDtypeStruct(queries.shape, jnp.bfloat16),
            jax.ShapeDtypeStruct((2, cols, 128), jnp.float32),
        ),
        in_specs=[smem, smem, lanes((rows, cols, each * HD)), lanes((2, frames, rows, cols, each * HD))],
        out_specs=(lanes((rows, cols, each * HD)), fixed((2, cols, 128))),
        scratch_shapes=[pltpu.VMEM((rows, cols, padded), jnp.float32)],
        compiler_params=pltpu.CompilerParams(vmem_limit_bytes=VMEM_BYTES),
        cost_estimate=pl.CostEstimate(
            flops=4 * rows * cols * 3 * frames * cols * wide,
            bytes_accessed=2 * rows * frames * cols * wide * 2,
            transcendentals=rows * heads * cols * 3 * frames * cols,
        ),
        name="main_attention",
    )(col_shift, frame_mask, queries, kv_frames)


def combine(partial, level, back_prev, back_next):
    rows, cols, wide = partial.shape
    edge = pl.BlockSpec((1, cols, wide), lambda s: (s * (rows - 1), 0, 0))
    return pl.pallas_call(
        combine_kernel,
        grid=(2,),
        out_shape=jax.ShapeDtypeStruct(partial.shape, jnp.bfloat16),
        in_specs=[edge, fixed(level.shape), fixed(back_prev.shape), fixed(back_next.shape)],
        out_specs=edge,
        input_output_aliases={0: 0},
        compiler_params=pltpu.CompilerParams(vmem_limit_bytes=VMEM_BYTES),
        name="combine",
    )(partial, level, back_prev, back_next)


def hail(place, count):
    barrier = pltpu.get_barrier_semaphore()

    @pl.when(place > 0)
    def _():
        pl.semaphore_signal(barrier, 1, device_id={"band": place - 1}, device_id_type=MESH)

    @pl.when(place < count - 1)
    def _():
        pl.semaphore_signal(barrier, 1, device_id={"band": place + 1}, device_id_type=MESH)


def meet(place, count):
    barrier = pltpu.get_barrier_semaphore()
    pl.semaphore_wait(barrier, jnp.where(place > 0, 1, 0) + jnp.where(place < count - 1, 1, 0))


def swap(place, count, sends, arrivals, up, down):
    def make(triple, other):
        source, target, at = triple
        return pltpu.make_async_remote_copy(
            src_ref=source,
            dst_ref=target,
            send_sem=sends.at[at],
            recv_sem=arrivals.at[at],
            device_id={"band": other},
            device_id_type=MESH,
        )

    ups = [make(triple, jnp.minimum(place + 1, count - 1)) for triple in up]
    downs = [make(triple, jnp.maximum(place - 1, 0)) for triple in down]

    def start(which):
        @pl.when(place < count - 1)
        def _():
            for at in which:
                ups[at].start()

        @pl.when(place > 0)
        def _():
            for at in which:
                downs[at].start()

    def arrive(which):
        @pl.when(place > 0)
        def _():
            for at in which:
                ups[at].wait_recv()

        @pl.when(place < count - 1)
        def _():
            for at in which:
                downs[at].wait_recv()

    def sent(which):
        @pl.when(place < count - 1)
        def _():
            for at in which:
                ups[at].wait_send()

        @pl.when(place > 0)
        def _():
            for at in which:
                downs[at].wait_send()

    return start, arrive, sent


def decoder_kernel(
    q_ref, lat_ref, cin_ref, wmid_in, bin_ref, gain_ref, bmid_ref, qp_ref, qn_ref, dec_out,
    high_ref, low_ref, below_ref, above_ref, ext_ref, pair_ref, rest_ref, win_ref, wmid_ref, first_ref, act_ref, dec_ref,
    sends, arrivals, local_sem, load_sem, out_sem
):
    place = lax.axis_index("band")
    count = lax.axis_size("band")
    last = q_ref.shape[0] - 1
    times, rows, packed = lat_ref.shape
    depth = cin_ref.shape[0] // 27
    taps = 3 * depth
    width = packed // depth
    ch = cin_ref.shape[1]
    tiles = packed // 128
    per = 128 // depth
    start, arrive, sent = swap(
        place,
        count,
        sends,
        arrivals,
        [(high_ref, below_ref, 0), (q_ref.at[last], qp_ref, 1)],
        [(low_ref, above_ref, 2), (q_ref.at[0], qn_ref, 3)],
    )
    hail(place, count)
    middle = pltpu.make_async_copy(wmid_in, wmid_ref, load_sem.at[0])
    middle.start()
    sub = lax.broadcasted_iota(jnp.int32, (8, packed), 0)

    def gather(target, shifts):
        rows_of = [pltpu.roll(lat_ref[dt].astype(jnp.float32), shifts[dt], 0) for dt in range(3)]
        target[...] = jnp.where(sub < 2, rows_of[0], jnp.where(sub < 4, rows_of[1], rows_of[2])).astype(jnp.bfloat16)

    gather(high_ref, [2, 4, 6])
    gather(low_ref, [0, 2, 4])
    at_row = (0, taps, 128)
    win_ref[...] = jnp.zeros_like(win_ref)
    for dy in range(3):
        for dt in range(3):
            source = (dt * 3 + dy) * taps
            win_ref[dy, at_row[dt] : at_row[dt] + taps] = cin_ref[source : source + taps]

    ext_ref[:, :, :128] = jnp.zeros((times, 8, 128), jnp.float32)
    ext_ref[:, :, 128 + packed :] = jnp.zeros((times, 8, 128), jnp.float32)
    lane = lax.broadcasted_iota(jnp.int32, (8, 128), 1)

    def spread(base):
        @pl.loop(0, tiles)
        def _(t):
            here = [ext_ref[dt, :, pl.ds(pl.multiple_of((t + 1) * 128, 128), 128)] for dt in range(3)]
            left = [ext_ref[dt, :, pl.ds(pl.multiple_of(t * 128, 128), 128)] for dt in range(3)]
            right = [ext_ref[dt, :, pl.ds(pl.multiple_of((t + 2) * 128, 128), 128)] for dt in range(3)]
            for j in range(per):
                moved = []
                for dt in range(3):
                    piece = here[dt]
                    if j == 0:
                        piece = jnp.where(lane >= 128 - depth, left[dt], piece)
                    if j == per - 1:
                        piece = jnp.where(lane < depth, right[dt], piece)
                    shift = (at_row[dt] - depth * (j - 1)) % 128
                    moved.append(pltpu.roll(piece, shift, 1) if shift else piece)
                both = jnp.where(lane < taps, moved[0], jnp.where(lane < 2 * taps, moved[1], 0.0))
                at = pl.ds(base * width + t * per + j, 8, stride=width)
                pair_ref[at, :] = both
                rest_ref[at, :] = jnp.where(lane < taps, moved[2], 0.0)

    x_at = lax.broadcasted_iota(jnp.int32, (width, ch), 0)

    def place_of(y):
        return y + rows + 8 if y < 2 else y

    def convolve(i, group):
        total = jnp.zeros((group * width, ch), jnp.float32)
        for dy in range(3):
            at = [place_of(i + g + dy) * width for g in range(group)]
            source = [jnp.concatenate([ref[here : here + width, :] for here in at], axis=0) for ref in (pair_ref, rest_ref)]
            source = jnp.concatenate(source, axis=1).astype(jnp.bfloat16)
            total += jnp.dot(source, win_ref[dy], preferred_element_type=jnp.float32)
        return total + bin_ref[...][None]

    def activate(i, group, total):
        scale = lax.rsqrt(jnp.mean(total * total, axis=-1, keepdims=True) + 1e-06)
        value = total * scale * gain_ref[...][None]
        active = value / (1.0 + jnp.exp(-value))
        for g in range(group):
            row = i + g
            mine = active[g * width : (g + 1) * width]
            if row == 0:
                mine = jnp.where(place == 0, 0.0, mine)
            if row == rows + 1:
                mine = jnp.where(place == count - 1, 0.0, mine)
            first_ref[row] = total[g * width : (g + 1) * width]
            at = slice(row * width, (row + 1) * width)
            act_ref[at, 0:ch] = jnp.where(x_at == 0, 0.0, pltpu.roll(mine, 1, 0)).astype(jnp.bfloat16)
            act_ref[at, ch : 2 * ch] = mine.astype(jnp.bfloat16)
            act_ref[at, 2 * ch : 3 * ch] = jnp.where(x_at == width - 1, 0.0, pltpu.roll(mine, width - 1, 0)).astype(
                jnp.bfloat16
            )

    def decode(at, many):
        total = jnp.zeros((many * width, ch), jnp.float32)
        for dy in range(3):
            total += jnp.dot(
                act_ref[(at + dy) * width : (at + dy + many) * width, :],
                wmid_ref[dy * 3 * ch : (dy + 1) * 3 * ch, :],
                preferred_element_type=jnp.float32,
            )
        total = total + bmid_ref[...][None]
        for y in range(many):
            dec_ref[at + y] = (total[y * width : (y + 1) * width] + first_ref[at + y + 1]).astype(jnp.bfloat16)

    group = 2 if rows % 2 == 0 else 1
    for dt in range(3):
        ext_ref[dt, :, 128 : 128 + packed] = lat_ref[dt].astype(jnp.float32)
    spread(2)
    meet(place, count)
    start((0, 1))

    @pl.when(place == 0)
    def _():
        below_ref[...] = jnp.zeros_like(below_ref)
        pltpu.make_async_copy(q_ref.at[0], qp_ref, local_sem.at[0]).start()

    @pl.when(place == count - 1)
    def _():
        above_ref[...] = jnp.zeros_like(above_ref)
        pltpu.make_async_copy(q_ref.at[last], qn_ref, local_sem.at[1]).start()

    order = list(range(2, rows, group)) + [0, rows]
    size = {i: group for i in order}
    size[0] = size[rows] = 2
    done, ready = set(), []
    spans = [(at, group) for at in range(0, rows, group)]
    middle_waited = False
    total = convolve(order[0], size[order[0]])
    for k, i in enumerate(order):
        here = total
        if k + 1 < len(order):
            if order[k + 1] == 0:
                arrive((0,))
                for dt in range(3):
                    up = pltpu.roll(above_ref[...].astype(jnp.float32), (8 - 2 * dt) % 8, 0)
                    down = pltpu.roll(below_ref[...].astype(jnp.float32), 6 - 2 * dt, 0)
                    ext_ref[dt, :, 128 : 128 + packed] = jnp.where(sub < 4, up, down)
                spread(rows + 2)
                middle.wait()
                middle_waited = True
            total = convolve(order[k + 1], size[order[k + 1]])
        if middle_waited:
            ready = [span for span in spans if set(range(span[0], span[0] + span[1] + 2)) <= done]
            for span in ready[:1]:
                spans.remove(span)
                decode(*span)
        activate(i, size[i], here)
        done |= set(range(i, i + size[i]))
    for span in spans:
        decode(*span)

    decoded = pltpu.make_async_copy(dec_ref, dec_out, out_sem.at[0])
    decoded.start()
    arrive((1,))
    sent((0, 1))

    @pl.when(place == 0)
    def _():
        pltpu.make_async_copy(q_ref.at[0], qp_ref, local_sem.at[0]).wait()

    @pl.when(place == count - 1)
    def _():
        pltpu.make_async_copy(q_ref.at[last], qn_ref, local_sem.at[1]).wait()

    decoded.wait()


def decoder(queries, latent, conv_in, bias_in, norm_gain, conv_mid, bias_mid):
    cols, wide = queries.shape[1:]
    times, rows, packed = latent.shape
    ch = conv_in.shape[1]
    width = packed // (conv_in.shape[0] // 27)
    vmem = pl.BlockSpec(memory_space=pltpu.VMEM)
    anywhere = pl.BlockSpec(memory_space=pl.ANY)
    return pl.pallas_call(
        decoder_kernel,
        out_shape=(
            jax.ShapeDtypeStruct((cols, wide), jnp.bfloat16),
            jax.ShapeDtypeStruct((cols, wide), jnp.bfloat16),
            jax.ShapeDtypeStruct((rows, width, ch), jnp.bfloat16),
        ),
        in_specs=[anywhere, vmem, vmem, anywhere, vmem, vmem, vmem],
        out_specs=(anywhere,) * 3,
        scratch_shapes=[
            *[pltpu.VMEM((8, packed), jnp.bfloat16)] * 4,
            pltpu.VMEM((times, 8, packed + 256), jnp.float32),
            pltpu.VMEM(((rows + 10) * width, 128), jnp.float32),
            pltpu.VMEM(((rows + 10) * width, 128), jnp.float32),
            pltpu.VMEM((3, 256, ch), jnp.bfloat16),
            pltpu.VMEM(conv_mid.shape, jnp.bfloat16),
            pltpu.VMEM((rows + 2, width, ch), jnp.float32),
            pltpu.VMEM(((rows + 2) * width, 3 * ch), jnp.bfloat16),
            pltpu.VMEM((rows, width, ch), jnp.bfloat16),
            pltpu.SemaphoreType.DMA((4,)),
            pltpu.SemaphoreType.DMA((4,)),
            pltpu.SemaphoreType.DMA((2,)),
            pltpu.SemaphoreType.DMA((1,)),
            pltpu.SemaphoreType.DMA((1,)),
        ],
        compiler_params=pltpu.CompilerParams(
            collective_id=0, has_side_effects=True, vmem_limit_bytes=VMEM_BYTES
        ),
        name="decoder",
    )(queries, latent, conv_in, conv_mid, bias_in, norm_gain, bias_mid)


def body(
    queries, kv_frames, frame_mask, col_shift, latent, conv_in, bias_in, norm_gain, conv_mid, bias_mid
):
    q_prev, q_next, decoded = decoder(queries, latent, conv_in, bias_in, norm_gain, conv_mid, bias_mid)
    o_prev, o_next = edge_attention(kv_frames, frame_mask, col_shift, q_prev, q_next)
    back_prev = to_next(o_next, "band")
    back_next = to_previous(o_prev, "band")
    partial, level = main_attention(queries, kv_frames, frame_mask, col_shift)
    return (combine(partial, level, back_prev, back_next), decoded)


def solution(mesh):
    placed = (
        P(("groups", "band"), None, None),
        P("groups", None, "band", None, None),
        P("groups"),
        P("groups"),
        P("groups", "band", None),
        P(),
        P(),
        P(),
        P(),
        P(),
    )
    return jax.shard_map(
        body,
        mesh=mesh,
        in_specs=placed,
        out_specs=(P(("groups", "band"), None, None), P(("groups", "band"), None, None)),
        check_vma=False,
    )
```

```python
import functools
import math

import jax
import jax.numpy as jnp
from jax import lax
from jax.experimental import pallas as pl
from jax.experimental.pallas import tpu as pltpu
from jax.sharding import PartitionSpec as P

HD = 128
RC = 8
NEG = -1e30
MESH = pl.DeviceIdType.MESH
SCALE2 = math.log2(math.e) / math.sqrt(HD)
HEADS_PER_STEP = 5
EDGE_HEADS = 10
VMEM_BYTES = 56 * 2**20


def to_next(block, axis):
    count = lax.axis_size(axis)
    return lax.ppermute(block, axis, [(i, i + 1) for i in range(count - 1)])


def to_previous(block, axis):
    count = lax.axis_size(axis)
    return lax.ppermute(block, axis, [(i + 1, i) for i in range(count - 1)])


def key_bias(cols, padded, slots, shift, open_slots):
    lane = lax.broadcasted_iota(jnp.int32, (cols, padded), 1)
    query = lax.broadcasted_iota(jnp.int32, (cols, padded), 0)
    column = lane
    level = jnp.full((cols, padded), NEG, jnp.float32)
    for s in range(slots):
        inside = (lane >= s * cols) & (lane < (s + 1) * cols)
        level = jnp.where(inside, open_slots[s], level)
        column = jnp.where(lane >= s * cols, lane - s * cols, column)
    return jnp.where(jnp.abs(column - query - shift) <= RC, level, NEG)


def heads_per_step(heads, most):
    return next(size for size in range(min(most, heads), 0, -1) if heads % size == 0)


def over_frames(mask_ref, frames, run):
    open_frames = [jnp.where(mask_ref[f] == 1, 0.0, NEG) for f in range(frames - 1)] + [jnp.float32(0.0)]
    closed = jnp.int32(frames - 1)
    for f in reversed(range(frames - 1)):
        closed = jnp.where(mask_ref[f] == 1, closed, f)

    @pl.when(closed < frames - 1)
    def _():
        run(
            lambda s: jnp.where(s < closed, s, s + 1),
            [jnp.where(s < closed, open_frames[s], open_frames[s + 1]) for s in range(frames - 1)],
        )

    @pl.when(closed == frames - 1)
    def _():
        run(lambda s: s, open_frames)


def attend(total_rows, cols, shift_ref, bias_ref, plan, places, query_row, kv_row, emit, each, ahead, frame_of, open_slots):
    step = pl.program_id(0)
    slots = len(open_slots)
    span = slots * cols
    padded = -(-span // 128) * 128
    queries = sorted({r for _, seen in plan for r in seen})
    near = {r: [(k, seen.index(r)) for k, (_, seen) in enumerate(plan) if r in seen] for r in queries}

    @pl.when(step == 0)
    def _():
        for at, r in enumerate(queries):
            row = jnp.clip(places[r], 0, total_rows - 1)
            bias_ref[at, :, :padded] = key_bias(cols, padded, slots, shift_ref[row], open_slots)

    def stack(which, n, part):
        pieces = [kv_row(which, frame_of(s), n, slice(None), part) for s in range(slots)]
        if padded > span:
            pieces.append(kv_row(which, frame_of(0), n, slice(0, padded - span), part))
        return jnp.concatenate(pieces, axis=0)

    def score(j):
        part = pl.ds(j * HD, HD)
        found = []
        for n, seen in plan:
            query = jnp.concatenate([query_row(r, part) for r in seen], axis=0)
            found.append(
                lax.dot_general(query, stack(0, n, part), (((1,), (1,)), ((), ())), preferred_element_type=jnp.float32)
            )
        return found

    def soften(found):
        pieces = [[None] * len(seen) for _, seen in plan]
        totals, tops = {}, {}
        for row, r in enumerate(queries):
            bias = bias_ref[row, :, :padded]
            blocks = [found[k][d * cols : (d + 1) * cols] + bias for k, d in near[r]]
            top = jnp.max(functools.reduce(jnp.maximum, blocks), axis=-1, keepdims=True) * SCALE2
            weights = [jnp.exp2(block * SCALE2 - top) for block in blocks]
            totals[r] = jnp.sum(functools.reduce(jnp.add, weights), axis=-1, keepdims=True)
            tops[r] = top
            for (k, d), weight in zip(near[r], weights):
                pieces[k][d] = weight.astype(jnp.bfloat16)
        return [jnp.concatenate(piece, axis=0) for piece in pieces], totals, tops

    def finish(j, weights, totals, tops):
        part = pl.ds(j * HD, HD)
        sums = [
            jnp.dot(weights[k], stack(1, n, part), preferred_element_type=jnp.float32)
            for k, (n, _) in enumerate(plan)
        ]
        for r in queries:
            acc = functools.reduce(jnp.add, [sums[k][d * cols : (d + 1) * cols] for k, d in near[r]])
            emit(j, step * each + j, r, (acc * (1.0 / totals[r])).astype(jnp.bfloat16), tops[r], totals[r])

    found, soft = {}, {}
    for j in range(each + ahead[0]):
        if j < each:
            found[j] = score(j)
        at = j - ahead[1]
        if 0 <= at < each:
            soft[at] = soften(found.pop(at))
        if j >= ahead[0]:
            finish(j - ahead[0], *soft.pop(j - ahead[0]))


def edge_kernel(
    total_rows, rows, each, shift_ref, mask_ref, qp_ref, qn_ref, kvf_ref, kvl_ref, op_ref, on_ref, bias_ref, level_ref
):
    step = pl.program_id(0)
    frames, cols = kvf_ref.shape[1], kvf_ref.shape[3]
    wide = op_ref.shape[1] - 3 * 128
    first_row = lax.axis_index("band") * rows
    lane = lax.broadcasted_iota(jnp.int32, (cols, 128), 1)
    sources, keys, targets = (qp_ref, qn_ref), (kvf_ref, kvl_ref), (op_ref, on_ref)

    @pl.when(step == 0)
    def _():
        level_ref[...] = jnp.zeros_like(level_ref)

    def emit(j, head, r, out, top, total):
        targets[r][:, pl.ds(pl.multiple_of(head * HD, HD), HD)] = out
        level_ref[r] = jnp.where(lane == head, top + jnp.log2(total), level_ref[r])

    over_frames(
        mask_ref,
        frames,
        functools.partial(
            attend,
            total_rows,
            cols,
            shift_ref,
            bias_ref,
            [(0, [0]), (1, [1])],
            [first_row - 1, first_row + rows],
            lambda r, part: sources[r][:, part],
            lambda which, f, n, some, part: keys[n][which, f, 0, some, part],
            emit,
            each,
            (3, 1),
        ),
    )

    @pl.when(step == pl.num_programs(0) - 1)
    def _():
        for side, o_ref in enumerate(targets):
            rest = level_ref[side]
            for k in range(3):
                piece = rest.astype(jnp.bfloat16)
                o_ref[:, wide + k * 128 : wide + (k + 1) * 128] = piece
                rest = rest - piece.astype(jnp.float32)


def main_kernel(
    total_rows, each, shift_ref, mask_ref, q_ref, kv_ref, dec_ref, out_ref, level_ref, dec_out, bias_ref, sem
):
    step = pl.program_id(0)
    frames, rows, cols = kv_ref.shape[1], q_ref.shape[0], q_ref.shape[1]
    first_row = lax.axis_index("band") * rows
    lane = lax.broadcasted_iota(jnp.int32, (cols, 128), 1)

    decoded = pltpu.make_async_copy(dec_ref, dec_out, sem)

    @pl.when(step == 0)
    def _():
        decoded.start()
        level_ref[...] = jnp.zeros_like(level_ref)

    def emit(j, head, r, out, top, total):
        out_ref[r, :, j * HD : (j + 1) * HD] = out
        for side, edge in enumerate((0, rows - 1)):
            if r == edge:
                level_ref[side] = jnp.where(lane == head, top + jnp.log2(total), level_ref[side])

    over_frames(
        mask_ref,
        frames,
        functools.partial(
            attend,
            total_rows,
            cols,
            shift_ref,
            bias_ref,
            [(n, list(range(max(n - 1, 0), min(n + 2, rows)))) for n in range(rows)],
            [first_row + r for r in range(rows)],
            lambda r, part: q_ref[r, :, part],
            lambda which, f, n, some, part: kv_ref[which, f, n, some, part],
            emit,
            each,
            (1, 1),
        ),
    )

    @pl.when(step == pl.num_programs(0) - 1)
    def _():
        decoded.wait()


def combine_kernel(own_ref, lev_ref, op_in, on_in, out_ref, op_ref, on_ref, sems):
    side = pl.program_id(0)
    place = lax.axis_index("band")
    count = lax.axis_size("band")
    cols, lanes = own_ref.shape[1], own_ref.shape[2]
    wide = op_ref.shape[1] - 3 * 128
    lane = lax.broadcasted_iota(jnp.int32, (cols, 128), 1)

    copies = [pltpu.make_async_copy(op_in, op_ref, sems.at[0]), pltpu.make_async_copy(on_in, on_ref, sems.at[1])]

    def mix(o_ref, there):
        other = sum(o_ref[:, wide + k * 128 : wide + (k + 1) * 128].astype(jnp.float32) for k in range(3))
        share = jnp.where(there, 1.0 / (1.0 + jnp.exp2(lev_ref[side] - other)), 0.0)
        for j in range(lanes // HD):
            weight = jnp.sum(jnp.where(lane == j, share, 0.0), axis=-1, keepdims=True)
            here = own_ref[0, :, j * HD : (j + 1) * HD].astype(jnp.float32)
            far = o_ref[:, j * HD : (j + 1) * HD].astype(jnp.float32)
            out_ref[0, :, j * HD : (j + 1) * HD] = (here + (far - here) * weight).astype(jnp.bfloat16)

    @pl.when(side == 0)
    def _():
        copies[0].start()
        copies[1].start()
        copies[0].wait()
        mix(op_ref, place > 0)

    @pl.when(side == 1)
    def _():
        copies[1].wait()
        mix(on_ref, place < count - 1)


def fixed(shape):
    return pl.BlockSpec(shape, lambda *_: (0,) * len(shape))


def lanes(shape, row=None):
    lead = (0,) * (len(shape) - 1) if row is None else (0,) * (len(shape) - 3) + (row, 0)
    return pl.BlockSpec(shape, lambda h: lead + (h,))


def edge_attention(kv_frames, frame_mask, col_shift, q_prev, q_next):
    frames, rows, cols, wide = kv_frames.shape[1:]
    heads = wide // HD
    each = heads_per_step(heads, EDGE_HEADS)
    smem = pl.BlockSpec(memory_space=pltpu.SMEM)
    packed = wide + 3 * 128
    padded = -(-frames * cols // 128) * 128
    return pl.pallas_call(
        functools.partial(edge_kernel, col_shift.shape[0], rows, each),
        grid=(heads // each,),
        out_shape=(jax.ShapeDtypeStruct((cols, packed), jnp.bfloat16),) * 2,
        in_specs=[
            smem,
            smem,
            lanes((cols, each * HD)),
            lanes((cols, each * HD)),
            lanes((2, frames, 1, cols, each * HD), 0),
            lanes((2, frames, 1, cols, each * HD), rows - 1),
        ],
        out_specs=(fixed((cols, packed)),) * 2,
        scratch_shapes=[
            pltpu.VMEM((2, cols, padded), jnp.float32),
            pltpu.VMEM((2, cols, 128), jnp.float32),
        ],
        compiler_params=pltpu.CompilerParams(vmem_limit_bytes=VMEM_BYTES),
        cost_estimate=pl.CostEstimate(
            flops=8 * cols * frames * cols * wide,
            bytes_accessed=4 * frames * cols * wide * 2,
            transcendentals=2 * heads * cols * frames * cols,
        ),
        name="edge_attention",
    )(col_shift, frame_mask, q_prev, q_next, kv_frames, kv_frames)


def main_attention(queries, kv_frames, frame_mask, col_shift, decoded):
    rows, cols, wide = queries.shape
    frames = kv_frames.shape[1]
    heads = wide // HD
    each = heads_per_step(heads, HEADS_PER_STEP)
    anywhere = pl.BlockSpec(memory_space=pl.ANY)
    smem = pl.BlockSpec(memory_space=pltpu.SMEM)
    padded = -(-frames * cols // 128) * 128
    return pl.pallas_call(
        functools.partial(main_kernel, col_shift.shape[0], each),
        grid=(heads // each,),
        out_shape=(
            jax.ShapeDtypeStruct(queries.shape, jnp.bfloat16),
            jax.ShapeDtypeStruct((2, cols, 128), jnp.float32),
            jax.ShapeDtypeStruct(decoded.shape, decoded.dtype),
        ),
        in_specs=[smem, smem, lanes((rows, cols, each * HD)), lanes((2, frames, rows, cols, each * HD)), anywhere],
        out_specs=(lanes((rows, cols, each * HD)), fixed((2, cols, 128)), anywhere),
        scratch_shapes=[pltpu.VMEM((rows, cols, padded), jnp.float32), pltpu.SemaphoreType.DMA(())],
        compiler_params=pltpu.CompilerParams(vmem_limit_bytes=VMEM_BYTES),
        cost_estimate=pl.CostEstimate(
            flops=4 * rows * cols * 3 * frames * cols * wide,
            bytes_accessed=2 * rows * frames * cols * wide * 2,
            transcendentals=rows * heads * cols * 3 * frames * cols,
        ),
        name="main_attention",
    )(col_shift, frame_mask, queries, kv_frames, decoded)


def combine(partial, level, back_prev, back_next):
    rows, cols, wide = partial.shape
    anywhere = pl.BlockSpec(memory_space=pl.ANY)
    edge = pl.BlockSpec((1, cols, wide), lambda s: (s * (rows - 1), 0, 0))
    return pl.pallas_call(
        combine_kernel,
        grid=(2,),
        out_shape=jax.ShapeDtypeStruct(partial.shape, jnp.bfloat16),
        in_specs=[edge, fixed(level.shape), anywhere, anywhere],
        out_specs=edge,
        input_output_aliases={0: 0},
        scratch_shapes=[
            pltpu.VMEM(back_prev.shape, jnp.bfloat16),
            pltpu.VMEM(back_next.shape, jnp.bfloat16),
            pltpu.SemaphoreType.DMA((2,)),
        ],
        compiler_params=pltpu.CompilerParams(vmem_limit_bytes=16 * 2**20),
        name="combine",
    )(partial, level, back_prev, back_next)


def hail(place, count):
    barrier = pltpu.get_barrier_semaphore()

    @pl.when(place > 0)
    def _():
        pl.semaphore_signal(barrier, 1, device_id={"band": place - 1}, device_id_type=MESH)

    @pl.when(place < count - 1)
    def _():
        pl.semaphore_signal(barrier, 1, device_id={"band": place + 1}, device_id_type=MESH)


def meet(place, count):
    barrier = pltpu.get_barrier_semaphore()
    pl.semaphore_wait(barrier, jnp.where(place > 0, 1, 0) + jnp.where(place < count - 1, 1, 0))


def swap(place, count, sends, arrivals, up, down):
    def make(triple, other):
        source, target, at = triple
        return pltpu.make_async_remote_copy(
            src_ref=source,
            dst_ref=target,
            send_sem=sends.at[at],
            recv_sem=arrivals.at[at],
            device_id={"band": other},
            device_id_type=MESH,
        )

    ups = [make(triple, jnp.minimum(place + 1, count - 1)) for triple in up]
    downs = [make(triple, jnp.maximum(place - 1, 0)) for triple in down]

    def start(which):
        @pl.when(place < count - 1)
        def _():
            for at in which:
                ups[at].start()

        @pl.when(place > 0)
        def _():
            for at in which:
                downs[at].start()

    def arrive(which):
        @pl.when(place > 0)
        def _():
            for at in which:
                ups[at].wait_recv()

        @pl.when(place < count - 1)
        def _():
            for at in which:
                downs[at].wait_recv()

    def sent(which):
        @pl.when(place < count - 1)
        def _():
            for at in which:
                ups[at].wait_send()

        @pl.when(place > 0)
        def _():
            for at in which:
                downs[at].wait_send()

    return start, arrive, sent


def decoder_kernel(
    q_ref, lat_in, cin_in, wmid_in, bin_in, gain_in, bmid_in, qp_ref, qn_ref, dec_out,
    high_ref, low_ref, below_ref, above_ref, ext_ref, pair_ref, rest_ref, win_ref, wmid_ref, first_ref, act_ref, dec_ref,
    lat_ref, cin_ref, bin_ref, gain_ref, bmid_ref,
    sends, arrivals, local_sem, load_sem, out_sem
):
    place = lax.axis_index("band")
    count = lax.axis_size("band")
    last = q_ref.shape[0] - 1
    hail(place, count)
    named = [
        (lat_in, lat_ref), (cin_in, cin_ref), (bin_in, bin_ref), (gain_in, gain_ref), (bmid_in, bmid_ref),
        (wmid_in, wmid_ref),
    ]
    loads = [pltpu.make_async_copy(source, target, load_sem.at[k]) for k, (source, target) in enumerate(named)]
    for load in loads:
        load.start()
    middle = loads.pop()
    times, rows, packed = lat_ref.shape
    depth = cin_ref.shape[0] // 27
    taps = 3 * depth
    width = packed // depth
    ch = cin_ref.shape[1]
    tiles = packed // 128
    per = 128 // depth
    start, arrive, sent = swap(
        place,
        count,
        sends,
        arrivals,
        [(high_ref, below_ref, 0), (q_ref.at[last], qp_ref, 1)],
        [(low_ref, above_ref, 2), (q_ref.at[0], qn_ref, 3)],
    )
    sub = lax.broadcasted_iota(jnp.int32, (8, packed), 0)

    def gather(target, shifts):
        rows_of = [pltpu.roll(lat_ref[dt].astype(jnp.float32), shifts[dt], 0) for dt in range(3)]
        target[...] = jnp.where(sub < 2, rows_of[0], jnp.where(sub < 4, rows_of[1], rows_of[2])).astype(jnp.bfloat16)

    loads[0].wait()
    gather(high_ref, [2, 4, 6])
    gather(low_ref, [0, 2, 4])
    meet(place, count)
    start((0, 1))

    @pl.when(place == 0)
    def _():
        below_ref[...] = jnp.zeros_like(below_ref)
        pltpu.make_async_copy(q_ref.at[0], qp_ref, local_sem.at[0]).start()

    @pl.when(place == count - 1)
    def _():
        above_ref[...] = jnp.zeros_like(above_ref)
        pltpu.make_async_copy(q_ref.at[last], qn_ref, local_sem.at[1]).start()

    at_row = (0, taps, 128)
    ext_ref[:, :, :128] = jnp.zeros((times, 8, 128), jnp.float32)
    ext_ref[:, :, 128 + packed :] = jnp.zeros((times, 8, 128), jnp.float32)
    lane = lax.broadcasted_iota(jnp.int32, (8, 128), 1)

    def spread(base):
        @pl.loop(0, tiles)
        def _(t):
            here = [ext_ref[dt, :, pl.ds(pl.multiple_of((t + 1) * 128, 128), 128)] for dt in range(3)]
            left = [ext_ref[dt, :, pl.ds(pl.multiple_of(t * 128, 128), 128)] for dt in range(3)]
            right = [ext_ref[dt, :, pl.ds(pl.multiple_of((t + 2) * 128, 128), 128)] for dt in range(3)]
            for j in range(per):
                moved = []
                for dt in range(3):
                    piece = here[dt]
                    if j == 0:
                        piece = jnp.where(lane >= 128 - depth, left[dt], piece)
                    if j == per - 1:
                        piece = jnp.where(lane < depth, right[dt], piece)
                    shift = (at_row[dt] - depth * (j - 1)) % 128
                    moved.append(pltpu.roll(piece, shift, 1) if shift else piece)
                both = jnp.where(lane < taps, moved[0], jnp.where(lane < 2 * taps, moved[1], 0.0))
                at = pl.ds(base * width + t * per + j, 8, stride=width)
                pair_ref[at, :] = both
                rest_ref[at, :] = jnp.where(lane < taps, moved[2], 0.0)

    x_at = lax.broadcasted_iota(jnp.int32, (width, ch), 0)

    def place_of(y):
        return y + rows + 8 if y < 2 else y

    def convolve(i, group):
        total = jnp.zeros((group * width, ch), jnp.float32)
        for dy in range(3):
            at = [place_of(i + g + dy) * width for g in range(group)]
            source = [jnp.concatenate([ref[here : here + width, :] for here in at], axis=0) for ref in (pair_ref, rest_ref)]
            source = jnp.concatenate(source, axis=1).astype(jnp.bfloat16)
            total += jnp.dot(source, win_ref[dy], preferred_element_type=jnp.float32)
        return total + bin_ref[...][None]

    def activate(i, group, total):
        scale = lax.rsqrt(jnp.mean(total * total, axis=-1, keepdims=True) + 1e-06)
        value = total * scale * gain_ref[...][None]
        active = value / (1.0 + jnp.exp(-value))
        for g in range(group):
            row = i + g
            mine = active[g * width : (g + 1) * width]
            if row == 0:
                mine = jnp.where(place == 0, 0.0, mine)
            if row == rows + 1:
                mine = jnp.where(place == count - 1, 0.0, mine)
            first_ref[row] = total[g * width : (g + 1) * width]
            at = slice(row * width, (row + 1) * width)
            act_ref[at, 0:ch] = jnp.where(x_at == 0, 0.0, pltpu.roll(mine, 1, 0)).astype(jnp.bfloat16)
            act_ref[at, ch : 2 * ch] = mine.astype(jnp.bfloat16)
            act_ref[at, 2 * ch : 3 * ch] = jnp.where(x_at == width - 1, 0.0, pltpu.roll(mine, width - 1, 0)).astype(
                jnp.bfloat16
            )

    def decode(at, many):
        source = [act_ref[(at + dy) * width : (at + dy + many) * width, :] for dy in range(3)]
        total = jnp.dot(jnp.concatenate(source, axis=1), wmid_ref[...], preferred_element_type=jnp.float32)
        total = total + bmid_ref[...][None]
        for y in range(many):
            dec_ref[at + y] = (total[y * width : (y + 1) * width] + first_ref[at + y + 1]).astype(jnp.bfloat16)
        some = pl.ds(at, many)
        store = pltpu.make_async_copy(dec_ref.at[some], dec_out.at[some], out_sem.at[at // many])
        store.start()
        stores.append(store)

    stores = []
    group = 2 if rows % 2 == 0 else 1
    for dt in range(3):
        ext_ref[dt, :, 128 : 128 + packed] = lat_ref[dt].astype(jnp.float32)
    spread(2)
    for load in loads[1:]:
        load.wait()
    win_ref[...] = jnp.zeros_like(win_ref)
    for dy in range(3):
        for dt in range(3):
            source = (dt * 3 + dy) * taps
            win_ref[dy, at_row[dt] : at_row[dt] + taps] = cin_ref[source : source + taps]
    order = list(range(2, rows, group)) + [0, rows]
    size = {i: group for i in order}
    size[0] = size[rows] = 2
    done, ready = set(), []
    spans = [(at, group) for at in range(0, rows, group)]
    middle_waited = False
    total = convolve(order[0], size[order[0]])
    for k, i in enumerate(order):
        here = total
        if k + 1 < len(order):
            if order[k + 1] == 0:
                arrive((0,))
                for dt in range(3):
                    up = pltpu.roll(above_ref[...].astype(jnp.float32), (8 - 2 * dt) % 8, 0)
                    down = pltpu.roll(below_ref[...].astype(jnp.float32), 6 - 2 * dt, 0)
                    ext_ref[dt, :, 128 : 128 + packed] = jnp.where(sub < 4, up, down)
                spread(rows + 2)
                middle.wait()
                middle_waited = True
            total = convolve(order[k + 1], size[order[k + 1]])
        if middle_waited:
            ready = [span for span in spans if set(range(span[0], span[0] + span[1] + 2)) <= done]
            for span in ready[:1]:
                spans.remove(span)
                decode(*span)
        activate(i, size[i], here)
        done |= set(range(i, i + size[i]))
    for span in spans:
        decode(*span)

    arrive((1,))
    sent((0, 1))

    @pl.when(place == 0)
    def _():
        pltpu.make_async_copy(q_ref.at[0], qp_ref, local_sem.at[0]).wait()

    @pl.when(place == count - 1)
    def _():
        pltpu.make_async_copy(q_ref.at[last], qn_ref, local_sem.at[1]).wait()

    for store in stores:
        store.wait()


def decoder(queries, latent, conv_in, bias_in, norm_gain, conv_mid, bias_mid):
    cols, wide = queries.shape[1:]
    times, rows, packed = latent.shape
    ch = conv_in.shape[1]
    width = packed // (conv_in.shape[0] // 27)
    anywhere = pl.BlockSpec(memory_space=pl.ANY)
    return pl.pallas_call(
        decoder_kernel,
        out_shape=(
            jax.ShapeDtypeStruct((cols, wide), jnp.bfloat16),
            jax.ShapeDtypeStruct((cols, wide), jnp.bfloat16),
            jax.ShapeDtypeStruct((rows, width, ch), jnp.bfloat16),
        ),
        in_specs=[anywhere] * 7,
        out_specs=(anywhere,) * 3,
        scratch_shapes=[
            *[pltpu.VMEM((8, packed), jnp.bfloat16)] * 4,
            pltpu.VMEM((times, 8, packed + 256), jnp.float32),
            pltpu.VMEM(((rows + 10) * width, 128), jnp.float32),
            pltpu.VMEM(((rows + 10) * width, 128), jnp.float32),
            pltpu.VMEM((3, 256, ch), jnp.bfloat16),
            pltpu.VMEM(conv_mid.shape, jnp.bfloat16),
            pltpu.VMEM((rows + 2, width, ch), jnp.float32),
            pltpu.VMEM(((rows + 2) * width, 3 * ch), jnp.bfloat16),
            pltpu.VMEM((rows, width, ch), jnp.bfloat16),
            pltpu.VMEM(latent.shape, jnp.bfloat16),
            pltpu.VMEM(conv_in.shape, jnp.bfloat16),
            *[pltpu.VMEM((ch,), jnp.float32)] * 3,
            pltpu.SemaphoreType.DMA((4,)),
            pltpu.SemaphoreType.DMA((4,)),
            pltpu.SemaphoreType.DMA((2,)),
            pltpu.SemaphoreType.DMA((6,)),
            pltpu.SemaphoreType.DMA((rows,)),
        ],
        compiler_params=pltpu.CompilerParams(
            collective_id=0, has_side_effects=True, vmem_limit_bytes=VMEM_BYTES
        ),
        name="decoder",
    )(queries, latent, conv_in, conv_mid, bias_in, norm_gain, bias_mid)


def body(
    queries, kv_frames, frame_mask, col_shift, latent, conv_in, bias_in, norm_gain, conv_mid, bias_mid
):
    q_prev, q_next, decoded = decoder(queries, latent, conv_in, bias_in, norm_gain, conv_mid, bias_mid)
    o_prev, o_next = edge_attention(kv_frames, frame_mask, col_shift, q_prev, q_next)
    back_prev = to_next(o_next, "band")
    back_next = to_previous(o_prev, "band")
    partial, level, decoded = main_attention(queries, kv_frames, frame_mask, col_shift, decoded)
    return (combine(partial, level, back_prev, back_next), decoded)


def solution(mesh):
    placed = (
        P(("groups", "band"), None, None),
        P("groups", None, "band", None, None),
        P("groups"),
        P("groups"),
        P("groups", "band", None),
        P(),
        P(),
        P(),
        P(),
        P(),
    )
    return jax.shard_map(
        body,
        mesh=mesh,
        in_specs=placed,
        out_specs=(P(("groups", "band"), None, None), P(("groups", "band"), None, None)),
        check_vma=False,
    )
```

```python
import functools
import math

import jax
import jax.numpy as jnp
from jax import lax
from jax.experimental import pallas as pl
from jax.experimental.pallas import tpu as pltpu
from jax.sharding import PartitionSpec as P

HD = 128
RC = 8
NEG = -1e30
MESH = pl.DeviceIdType.MESH
SCALE2 = math.log2(math.e) / math.sqrt(HD)
HEADS_PER_STEP = 5
EDGE_HEADS = 10
VMEM_BYTES = 56 * 2**20


def to_next(block, axis):
    count = lax.axis_size(axis)
    return lax.ppermute(block, axis, [(i, i + 1) for i in range(count - 1)])


def to_previous(block, axis):
    count = lax.axis_size(axis)
    return lax.ppermute(block, axis, [(i + 1, i) for i in range(count - 1)])


def key_bias(cols, padded, slots, shift, open_slots):
    lane = lax.broadcasted_iota(jnp.int32, (cols, padded), 1)
    query = lax.broadcasted_iota(jnp.int32, (cols, padded), 0)
    column = lane
    level = jnp.full((cols, padded), NEG, jnp.float32)
    for s in range(slots):
        inside = (lane >= s * cols) & (lane < (s + 1) * cols)
        level = jnp.where(inside, open_slots[s], level)
        column = jnp.where(lane >= s * cols, lane - s * cols, column)
    return jnp.where(jnp.abs(column - query - shift) <= RC, level, NEG)


def heads_per_step(heads, most):
    return next(size for size in range(min(most, heads), 0, -1) if heads % size == 0)


def over_frames(mask_ref, frames, run):
    open_frames = [jnp.where(mask_ref[f] == 1, 0.0, NEG) for f in range(frames - 1)] + [jnp.float32(0.0)]
    closed = jnp.int32(frames - 1)
    for f in reversed(range(frames - 1)):
        closed = jnp.where(mask_ref[f] == 1, closed, f)

    @pl.when(closed < frames - 1)
    def _():
        run(
            lambda s: jnp.where(s < closed, s, s + 1),
            [jnp.where(s < closed, open_frames[s], open_frames[s + 1]) for s in range(frames - 1)],
        )

    @pl.when(closed == frames - 1)
    def _():
        run(lambda s: s, open_frames)


def attend(total_rows, cols, shift_ref, bias_ref, plan, places, query_row, kv_row, emit, each, ahead, frame_of, open_slots):
    step = pl.program_id(0)
    slots = len(open_slots)
    span = slots * cols
    padded = -(-span // 128) * 128
    queries = sorted({r for _, seen in plan for r in seen})
    near = {r: [(k, seen.index(r)) for k, (_, seen) in enumerate(plan) if r in seen] for r in queries}

    @pl.when(step == 0)
    def _():
        for at, r in enumerate(queries):
            row = jnp.clip(places[r], 0, total_rows - 1)
            bias_ref[at, :, :padded] = key_bias(cols, padded, slots, shift_ref[row], open_slots)

    def stack(which, n, part):
        pieces = [kv_row(which, frame_of(s), n, slice(None), part) for s in range(slots)]
        if padded > span:
            pieces.append(kv_row(which, frame_of(0), n, slice(0, padded - span), part))
        return jnp.concatenate(pieces, axis=0)

    def score(j):
        part = pl.ds(j * HD, HD)
        found = []
        for n, seen in plan:
            query = jnp.concatenate([query_row(r, part) for r in seen], axis=0)
            found.append(
                lax.dot_general(query, stack(0, n, part), (((1,), (1,)), ((), ())), preferred_element_type=jnp.float32)
            )
        return found

    def soften(found):
        pieces = [[None] * len(seen) for _, seen in plan]
        totals, tops = {}, {}
        for row, r in enumerate(queries):
            bias = bias_ref[row, :, :padded]
            blocks = [found[k][d * cols : (d + 1) * cols] + bias for k, d in near[r]]
            top = jnp.max(functools.reduce(jnp.maximum, blocks), axis=-1, keepdims=True) * SCALE2
            weights = [jnp.exp2(block * SCALE2 - top) for block in blocks]
            totals[r] = jnp.sum(functools.reduce(jnp.add, weights), axis=-1, keepdims=True)
            tops[r] = top
            for (k, d), weight in zip(near[r], weights):
                pieces[k][d] = weight.astype(jnp.bfloat16)
        return [jnp.concatenate(piece, axis=0) for piece in pieces], totals, tops

    def finish(j, weights, totals, tops):
        part = pl.ds(j * HD, HD)
        sums = [
            jnp.dot(weights[k], stack(1, n, part), preferred_element_type=jnp.float32)
            for k, (n, _) in enumerate(plan)
        ]
        for r in queries:
            acc = functools.reduce(jnp.add, [sums[k][d * cols : (d + 1) * cols] for k, d in near[r]])
            emit(j, step * each + j, r, (acc * (1.0 / totals[r])).astype(jnp.bfloat16), tops[r], totals[r])

    found, soft = {}, {}
    for j in range(each + ahead[0]):
        if j < each:
            found[j] = score(j)
        at = j - ahead[1]
        if 0 <= at < each:
            soft[at] = soften(found.pop(at))
        if j >= ahead[0]:
            finish(j - ahead[0], *soft.pop(j - ahead[0]))


def edge_kernel(
    total_rows, rows, each, shift_ref, mask_ref, qp_ref, qn_ref, kvf_ref, kvl_ref, op_ref, on_ref, bias_ref, level_ref
):
    step = pl.program_id(0)
    frames, cols = kvf_ref.shape[1], kvf_ref.shape[3]
    wide = op_ref.shape[1] - 3 * 128
    first_row = lax.axis_index("band") * rows
    lane = lax.broadcasted_iota(jnp.int32, (cols, 128), 1)
    sources, keys, targets = (qp_ref, qn_ref), (kvf_ref, kvl_ref), (op_ref, on_ref)

    @pl.when(step == 0)
    def _():
        level_ref[...] = jnp.zeros_like(level_ref)

    def emit(j, head, r, out, top, total):
        targets[r][:, pl.ds(pl.multiple_of(head * HD, HD), HD)] = out
        level_ref[r] = jnp.where(lane == head, top + jnp.log2(total), level_ref[r])

    over_frames(
        mask_ref,
        frames,
        functools.partial(
            attend,
            total_rows,
            cols,
            shift_ref,
            bias_ref,
            [(0, [0]), (1, [1])],
            [first_row - 1, first_row + rows],
            lambda r, part: sources[r][:, part],
            lambda which, f, n, some, part: keys[n][which, f, 0, some, part],
            emit,
            each,
            (3, 1),
        ),
    )

    @pl.when(step == pl.num_programs(0) - 1)
    def _():
        for side, o_ref in enumerate(targets):
            rest = level_ref[side]
            for k in range(3):
                piece = rest.astype(jnp.bfloat16)
                o_ref[:, wide + k * 128 : wide + (k + 1) * 128] = piece
                rest = rest - piece.astype(jnp.float32)


def main_kernel(
    total_rows, each, shift_ref, mask_ref, q_ref, kv_ref, dec_ref, out_ref, level_ref, dec_out, bias_ref, held_ref, sems
):
    step = pl.program_id(0)
    frames, rows, cols = kv_ref.shape[1], q_ref.shape[0], q_ref.shape[1]
    first_row = lax.axis_index("band") * rows
    lane = lax.broadcasted_iota(jnp.int32, (cols, 128), 1)

    fetch = pltpu.make_async_copy(dec_ref, held_ref, sems.at[0])
    store = pltpu.make_async_copy(held_ref, dec_out, sems.at[1])
    final = pl.num_programs(0) - 1

    @pl.when(step == 0)
    def _():
        fetch.start()
        level_ref[...] = jnp.zeros_like(level_ref)

    def emit(j, head, r, out, top, total):
        out_ref[r, :, j * HD : (j + 1) * HD] = out
        for side, edge in enumerate((0, rows - 1)):
            if r == edge:
                level_ref[side] = jnp.where(lane == head, top + jnp.log2(total), level_ref[side])

    over_frames(
        mask_ref,
        frames,
        functools.partial(
            attend,
            total_rows,
            cols,
            shift_ref,
            bias_ref,
            [(n, list(range(max(n - 1, 0), min(n + 2, rows)))) for n in range(rows)],
            [first_row + r for r in range(rows)],
            lambda r, part: q_ref[r, :, part],
            lambda which, f, n, some, part: kv_ref[which, f, n, some, part],
            emit,
            each,
            (1, 1),
        ),
    )

    @pl.when(step == jnp.minimum(1, final))
    def _():
        fetch.wait()
        store.start()

    @pl.when(step == final)
    def _():
        store.wait()


def combine_kernel(own_in, lev_in, op_in, on_in, out_ref, own_ref, lev_ref, op_ref, on_ref, loads, stores):
    place = lax.axis_index("band")
    count = lax.axis_size("band")
    cols, wide = own_ref.shape[1:]
    last = own_in.shape[0] - 1
    pairs = [
        (lev_in, lev_ref), (op_in, op_ref), (own_in.at[0], own_ref.at[0]), (on_in, on_ref), (own_in.at[last], own_ref.at[1])
    ]
    copies = [pltpu.make_async_copy(source, target, loads.at[k]) for k, (source, target) in enumerate(pairs)]
    for copy in copies:
        copy.start()
    outs = []
    copies[0].wait()
    for side, (o_ref, there, edge) in enumerate(((op_ref, place > 0, 0), (on_ref, place < count - 1, last))):
        copies[1 + 2 * side].wait()
        copies[2 + 2 * side].wait()
        other = sum(o_ref[:, wide + k * 128 : wide + (k + 1) * 128].astype(jnp.float32) for k in range(3))
        share = jnp.where(there, 1.0 / (1.0 + jnp.exp2(lev_ref[side] - other)), 0.0)
        for j in range(wide // HD):
            part = slice(j * HD, (j + 1) * HD)
            here = own_ref[side, :, part].astype(jnp.float32)
            far = o_ref[:, part].astype(jnp.float32)
            own_ref[side, :, part] = (here + (far - here) * share[:, j : j + 1]).astype(jnp.bfloat16)
        out = pltpu.make_async_copy(own_ref.at[side], out_ref.at[edge], stores.at[side])
        out.start()
        outs.append(out)
    for out in outs:
        out.wait()


def fixed(shape):
    return pl.BlockSpec(shape, lambda *_: (0,) * len(shape))


def lanes(shape, row=None):
    lead = (0,) * (len(shape) - 1) if row is None else (0,) * (len(shape) - 3) + (row, 0)
    return pl.BlockSpec(shape, lambda h: lead + (h,))


def edge_attention(kv_frames, frame_mask, col_shift, q_prev, q_next):
    frames, rows, cols, wide = kv_frames.shape[1:]
    heads = wide // HD
    each = heads_per_step(heads, EDGE_HEADS)
    smem = pl.BlockSpec(memory_space=pltpu.SMEM)
    packed = wide + 3 * 128
    padded = -(-frames * cols // 128) * 128
    return pl.pallas_call(
        functools.partial(edge_kernel, col_shift.shape[0], rows, each),
        grid=(heads // each,),
        out_shape=(jax.ShapeDtypeStruct((cols, packed), jnp.bfloat16),) * 2,
        in_specs=[
            smem,
            smem,
            lanes((cols, each * HD)),
            lanes((cols, each * HD)),
            lanes((2, frames, 1, cols, each * HD), 0),
            lanes((2, frames, 1, cols, each * HD), rows - 1),
        ],
        out_specs=(fixed((cols, packed)),) * 2,
        scratch_shapes=[
            pltpu.VMEM((2, cols, padded), jnp.float32),
            pltpu.VMEM((2, cols, 128), jnp.float32),
        ],
        compiler_params=pltpu.CompilerParams(vmem_limit_bytes=VMEM_BYTES),
        cost_estimate=pl.CostEstimate(
            flops=8 * cols * frames * cols * wide,
            bytes_accessed=4 * frames * cols * wide * 2,
            transcendentals=2 * heads * cols * frames * cols,
        ),
        name="edge_attention",
    )(col_shift, frame_mask, q_prev, q_next, kv_frames, kv_frames)


def main_attention(queries, kv_frames, frame_mask, col_shift, decoded):
    rows, cols, wide = queries.shape
    frames = kv_frames.shape[1]
    heads = wide // HD
    each = heads_per_step(heads, HEADS_PER_STEP)
    anywhere = pl.BlockSpec(memory_space=pl.ANY)
    smem = pl.BlockSpec(memory_space=pltpu.SMEM)
    padded = -(-frames * cols // 128) * 128
    return pl.pallas_call(
        functools.partial(main_kernel, col_shift.shape[0], each),
        grid=(heads // each,),
        out_shape=(
            jax.ShapeDtypeStruct(queries.shape, jnp.bfloat16),
            jax.ShapeDtypeStruct((2, cols, 128), jnp.float32),
            jax.ShapeDtypeStruct(decoded.shape, decoded.dtype),
        ),
        in_specs=[smem, smem, lanes((rows, cols, each * HD)), lanes((2, frames, rows, cols, each * HD)), anywhere],
        out_specs=(lanes((rows, cols, each * HD)), fixed((2, cols, 128)), anywhere),
        scratch_shapes=[
            pltpu.VMEM((rows, cols, padded), jnp.float32),
            pltpu.VMEM(decoded.shape, decoded.dtype),
            pltpu.SemaphoreType.DMA((2,)),
        ],
        compiler_params=pltpu.CompilerParams(vmem_limit_bytes=VMEM_BYTES),
        cost_estimate=pl.CostEstimate(
            flops=4 * rows * cols * 3 * frames * cols * wide,
            bytes_accessed=2 * rows * frames * cols * wide * 2,
            transcendentals=rows * heads * cols * 3 * frames * cols,
        ),
        name="main_attention",
    )(col_shift, frame_mask, queries, kv_frames, decoded)


def combine(partial, level, back_prev, back_next):
    rows, cols, wide = partial.shape
    anywhere = pl.BlockSpec(memory_space=pl.ANY)
    return pl.pallas_call(
        combine_kernel,
        out_shape=jax.ShapeDtypeStruct(partial.shape, jnp.bfloat16),
        in_specs=[anywhere, pl.BlockSpec(memory_space=pltpu.HBM), anywhere, anywhere],
        out_specs=anywhere,
        input_output_aliases={0: 0},
        scratch_shapes=[
            pltpu.VMEM((2, cols, wide), jnp.bfloat16),
            pltpu.VMEM(level.shape, jnp.float32),
            pltpu.VMEM(back_prev.shape, jnp.bfloat16),
            pltpu.VMEM(back_next.shape, jnp.bfloat16),
            pltpu.SemaphoreType.DMA((5,)),
            pltpu.SemaphoreType.DMA((2,)),
        ],
        compiler_params=pltpu.CompilerParams(vmem_limit_bytes=16 * 2**20),
        name="combine",
    )(partial, level, back_prev, back_next)


def hail(place, count):
    barrier = pltpu.get_barrier_semaphore()

    @pl.when(place > 0)
    def _():
        pl.semaphore_signal(barrier, 1, device_id={"band": place - 1}, device_id_type=MESH)

    @pl.when(place < count - 1)
    def _():
        pl.semaphore_signal(barrier, 1, device_id={"band": place + 1}, device_id_type=MESH)


def meet(place, count):
    barrier = pltpu.get_barrier_semaphore()
    pl.semaphore_wait(barrier, jnp.where(place > 0, 1, 0) + jnp.where(place < count - 1, 1, 0))


def swap(place, count, sends, arrivals, up, down):
    def make(triple, other):
        source, target, at = triple
        return pltpu.make_async_remote_copy(
            src_ref=source,
            dst_ref=target,
            send_sem=sends.at[at],
            recv_sem=arrivals.at[at],
            device_id={"band": other},
            device_id_type=MESH,
        )

    ups = [make(triple, jnp.minimum(place + 1, count - 1)) for triple in up]
    downs = [make(triple, jnp.maximum(place - 1, 0)) for triple in down]

    def start(which):
        @pl.when(place < count - 1)
        def _():
            for at in which:
                ups[at].start()

        @pl.when(place > 0)
        def _():
            for at in which:
                downs[at].start()

    def arrive(which):
        @pl.when(place > 0)
        def _():
            for at in which:
                ups[at].wait_recv()

        @pl.when(place < count - 1)
        def _():
            for at in which:
                downs[at].wait_recv()

    def sent(which):
        @pl.when(place < count - 1)
        def _():
            for at in which:
                ups[at].wait_send()

        @pl.when(place > 0)
        def _():
            for at in which:
                downs[at].wait_send()

    return start, arrive, sent


def decoder_kernel(
    q_ref, lat_in, cin_in, wmid_in, bin_in, gain_in, bmid_in, qp_ref, qn_ref, dec_out,
    high_ref, low_ref, below_ref, above_ref, ext_ref, pair_ref, rest_ref, win_ref, wmid_ref, first_ref, act_ref, dec_ref,
    lat_ref, cin_ref, bin_ref, gain_ref, bmid_ref,
    sends, arrivals, local_sem, load_sem, out_sem
):
    place = lax.axis_index("band")
    count = lax.axis_size("band")
    last = q_ref.shape[0] - 1
    hail(place, count)
    named = [
        (lat_in, lat_ref), (cin_in, cin_ref), (bin_in, bin_ref), (gain_in, gain_ref), (bmid_in, bmid_ref),
        (wmid_in, wmid_ref),
    ]
    loads = [pltpu.make_async_copy(source, target, load_sem.at[k]) for k, (source, target) in enumerate(named)]
    for load in loads:
        load.start()
    middle = loads.pop()
    times, rows, packed = lat_ref.shape
    depth = cin_ref.shape[0] // 27
    taps = 3 * depth
    width = packed // depth
    ch = cin_ref.shape[1]
    tiles = packed // 128
    per = 128 // depth
    start, arrive, sent = swap(
        place,
        count,
        sends,
        arrivals,
        [(high_ref, below_ref, 0), (q_ref.at[last], qp_ref, 1)],
        [(low_ref, above_ref, 2), (q_ref.at[0], qn_ref, 3)],
    )
    sub = lax.broadcasted_iota(jnp.int32, (8, packed), 0)

    def gather(target, shifts):
        rows_of = [pltpu.roll(lat_ref[dt].astype(jnp.float32), shifts[dt], 0) for dt in range(3)]
        target[...] = jnp.where(sub < 2, rows_of[0], jnp.where(sub < 4, rows_of[1], rows_of[2])).astype(jnp.bfloat16)

    loads[0].wait()
    gather(high_ref, [2, 4, 6])
    gather(low_ref, [0, 2, 4])
    meet(place, count)
    start((0, 1))

    @pl.when(place == 0)
    def _():
        below_ref[...] = jnp.zeros_like(below_ref)
        pltpu.make_async_copy(q_ref.at[0], qp_ref, local_sem.at[0]).start()

    @pl.when(place == count - 1)
    def _():
        above_ref[...] = jnp.zeros_like(above_ref)
        pltpu.make_async_copy(q_ref.at[last], qn_ref, local_sem.at[1]).start()

    at_row = (0, taps, 128)
    ext_ref[:, :, :128] = jnp.zeros((times, 8, 128), jnp.float32)
    ext_ref[:, :, 128 + packed :] = jnp.zeros((times, 8, 128), jnp.float32)
    lane = lax.broadcasted_iota(jnp.int32, (8, 128), 1)

    def spread(base):
        @pl.loop(0, tiles, unroll=tiles)
        def _(t):
            here = [ext_ref[dt, :, pl.ds(pl.multiple_of((t + 1) * 128, 128), 128)] for dt in range(3)]
            left = [ext_ref[dt, :, pl.ds(pl.multiple_of(t * 128, 128), 128)] for dt in range(3)]
            right = [ext_ref[dt, :, pl.ds(pl.multiple_of((t + 2) * 128, 128), 128)] for dt in range(3)]
            for j in range(per):
                moved = []
                for dt in range(3):
                    piece = here[dt]
                    if j == 0:
                        piece = jnp.where(lane >= 128 - depth, left[dt], piece)
                    if j == per - 1:
                        piece = jnp.where(lane < depth, right[dt], piece)
                    shift = (at_row[dt] - depth * (j - 1)) % 128
                    moved.append(pltpu.roll(piece, shift, 1) if shift else piece)
                both = jnp.where(lane < taps, moved[0], jnp.where(lane < 2 * taps, moved[1], 0.0))
                at = pl.ds(base * width + t * per + j, 8, stride=width)
                pair_ref[at, :] = both
                rest_ref[at, :] = jnp.where(lane < taps, moved[2], 0.0)

    x_at = lax.broadcasted_iota(jnp.int32, (width, ch), 0)

    def place_of(y):
        return y + rows + 8 if y < 2 else y

    def convolve(i, group):
        total = jnp.zeros((group * width, ch), jnp.float32)
        for dy in range(3):
            at = [place_of(i + g + dy) * width for g in range(group)]
            source = [jnp.concatenate([ref[here : here + width, :] for here in at], axis=0) for ref in (pair_ref, rest_ref)]
            source = jnp.concatenate(source, axis=1).astype(jnp.bfloat16)
            total += jnp.dot(source, win_ref[dy], preferred_element_type=jnp.float32)
        return total + bin_ref[...][None]

    def activate(i, group, total):
        scale = lax.rsqrt(jnp.mean(total * total, axis=-1, keepdims=True) + 1e-06)
        value = total * scale * gain_ref[...][None]
        half = 0.5 * value
        active = half + half * jnp.tanh(half)
        for g in range(group):
            row = i + g
            mine = active[g * width : (g + 1) * width]
            if row == 0:
                mine = jnp.where(place == 0, 0.0, mine)
            if row == rows + 1:
                mine = jnp.where(place == count - 1, 0.0, mine)
            first_ref[row] = total[g * width : (g + 1) * width]
            at = slice(row * width, (row + 1) * width)
            act_ref[at, 0:ch] = jnp.where(x_at == 0, 0.0, pltpu.roll(mine, 1, 0)).astype(jnp.bfloat16)
            act_ref[at, ch : 2 * ch] = mine.astype(jnp.bfloat16)
            act_ref[at, 2 * ch : 3 * ch] = jnp.where(x_at == width - 1, 0.0, pltpu.roll(mine, width - 1, 0)).astype(
                jnp.bfloat16
            )

    def decode(at, many):
        source = [act_ref[(at + dy) * width : (at + dy + many) * width, :] for dy in range(3)]
        total = jnp.dot(jnp.concatenate(source, axis=1), wmid_ref[...], preferred_element_type=jnp.float32)
        total = total + bmid_ref[...][None]
        for y in range(many):
            dec_ref[at + y] = (total[y * width : (y + 1) * width] + first_ref[at + y + 1]).astype(jnp.bfloat16)
        some = pl.ds(at, many)
        store = pltpu.make_async_copy(dec_ref.at[some], dec_out.at[some], out_sem.at[at // many])
        store.start()
        stores.append(store)

    stores = []
    group = 2 if rows % 2 == 0 else 1
    for dt in range(3):
        ext_ref[dt, :, 128 : 128 + packed] = lat_ref[dt].astype(jnp.float32)
    spread(2)
    for load in loads[1:]:
        load.wait()
    win_ref[...] = jnp.zeros_like(win_ref)
    for dy in range(3):
        for dt in range(3):
            source = (dt * 3 + dy) * taps
            win_ref[dy, at_row[dt] : at_row[dt] + taps] = cin_ref[source : source + taps]
    order = list(range(2, rows, group)) + [0, rows]
    size = {i: group for i in order}
    size[0] = size[rows] = 2
    done, ready = set(), []
    spans = [(at, group) for at in range(0, rows, group)]
    middle_waited = False
    total = convolve(order[0], size[order[0]])
    for k, i in enumerate(order):
        here = total
        if k + 1 < len(order):
            if order[k + 1] == 0:
                arrive((0,))
                for dt in range(3):
                    up = pltpu.roll(above_ref[...].astype(jnp.float32), (8 - 2 * dt) % 8, 0)
                    down = pltpu.roll(below_ref[...].astype(jnp.float32), 6 - 2 * dt, 0)
                    ext_ref[dt, :, 128 : 128 + packed] = jnp.where(sub < 4, up, down)
                spread(rows + 2)
                middle.wait()
                middle_waited = True
            total = convolve(order[k + 1], size[order[k + 1]])
        if middle_waited:
            ready = [span for span in spans if set(range(span[0], span[0] + span[1] + 2)) <= done]
            for span in ready[:1]:
                spans.remove(span)
                decode(*span)
        activate(i, size[i], here)
        done |= set(range(i, i + size[i]))
    for span in spans:
        decode(*span)

    arrive((1,))
    sent((0, 1))

    @pl.when(place == 0)
    def _():
        pltpu.make_async_copy(q_ref.at[0], qp_ref, local_sem.at[0]).wait()

    @pl.when(place == count - 1)
    def _():
        pltpu.make_async_copy(q_ref.at[last], qn_ref, local_sem.at[1]).wait()

    for store in stores:
        store.wait()


def decoder(queries, latent, conv_in, bias_in, norm_gain, conv_mid, bias_mid):
    cols, wide = queries.shape[1:]
    times, rows, packed = latent.shape
    ch = conv_in.shape[1]
    width = packed // (conv_in.shape[0] // 27)
    anywhere = pl.BlockSpec(memory_space=pl.ANY)
    return pl.pallas_call(
        decoder_kernel,
        out_shape=(
            jax.ShapeDtypeStruct((cols, wide), jnp.bfloat16),
            jax.ShapeDtypeStruct((cols, wide), jnp.bfloat16),
            jax.ShapeDtypeStruct((rows, width, ch), jnp.bfloat16),
        ),
        in_specs=[anywhere] * 7,
        out_specs=(anywhere,) * 3,
        scratch_shapes=[
            *[pltpu.VMEM((8, packed), jnp.bfloat16)] * 4,
            pltpu.VMEM((times, 8, packed + 256), jnp.float32),
            pltpu.VMEM(((rows + 10) * width, 128), jnp.float32),
            pltpu.VMEM(((rows + 10) * width, 128), jnp.float32),
            pltpu.VMEM((3, 256, ch), jnp.bfloat16),
            pltpu.VMEM(conv_mid.shape, jnp.bfloat16),
            pltpu.VMEM((rows + 2, width, ch), jnp.float32),
            pltpu.VMEM(((rows + 2) * width, 3 * ch), jnp.bfloat16),
            pltpu.VMEM((rows, width, ch), jnp.bfloat16),
            pltpu.VMEM(latent.shape, jnp.bfloat16),
            pltpu.VMEM(conv_in.shape, jnp.bfloat16),
            *[pltpu.VMEM((ch,), jnp.float32)] * 3,
            pltpu.SemaphoreType.DMA((4,)),
            pltpu.SemaphoreType.DMA((4,)),
            pltpu.SemaphoreType.DMA((2,)),
            pltpu.SemaphoreType.DMA((6,)),
            pltpu.SemaphoreType.DMA((rows,)),
        ],
        compiler_params=pltpu.CompilerParams(
            collective_id=0, has_side_effects=True, vmem_limit_bytes=VMEM_BYTES
        ),
        name="decoder",
    )(queries, latent, conv_in, conv_mid, bias_in, norm_gain, bias_mid)


def body(
    queries, kv_frames, frame_mask, col_shift, latent, conv_in, bias_in, norm_gain, conv_mid, bias_mid
):
    q_prev, q_next, decoded = decoder(queries, latent, conv_in, bias_in, norm_gain, conv_mid, bias_mid)
    o_prev, o_next = edge_attention(kv_frames, frame_mask, col_shift, q_prev, q_next)
    back_prev = to_next(o_next, "band")
    back_next = to_previous(o_prev, "band")
    partial, level, decoded = main_attention(queries, kv_frames, frame_mask, col_shift, decoded)
    return (combine(partial, level, back_prev, back_next), decoded)


def solution(mesh):
    placed = (
        P(("groups", "band"), None, None),
        P("groups", None, "band", None, None),
        P("groups"),
        P("groups"),
        P("groups", "band", None),
        P(),
        P(),
        P(),
        P(),
        P(),
    )
    return jax.shard_map(
        body,
        mesh=mesh,
        in_specs=placed,
        out_specs=(P(("groups", "band"), None, None), P(("groups", "band"), None, None)),
        check_vma=False,
    )
```

```python
import functools
import math

import jax
import jax.numpy as jnp
from jax import lax
from jax.experimental import pallas as pl
from jax.experimental.pallas import tpu as pltpu
from jax.sharding import PartitionSpec as P

HD = 128
RC = 8
NEG = -1e30
MESH = pl.DeviceIdType.MESH
SCALE2 = math.log2(math.e) / math.sqrt(HD)
HEADS_PER_STEP = 5
EDGE_HEADS = 10
VMEM_BYTES = 56 * 2**20
COMBINE_BYTES = 48 * 2**20
LEVEL_BYTES = 24 * 2**20


def to_next(block, axis):
    count = lax.axis_size(axis)
    return lax.ppermute(block, axis, [(i, i + 1) for i in range(count - 1)])


def to_previous(block, axis):
    count = lax.axis_size(axis)
    return lax.ppermute(block, axis, [(i + 1, i) for i in range(count - 1)])


def key_bias(cols, padded, slots, shift, open_slots):
    lane = lax.broadcasted_iota(jnp.int32, (cols, padded), 1)
    query = lax.broadcasted_iota(jnp.int32, (cols, padded), 0)
    column = lane
    level = jnp.full((cols, padded), NEG, jnp.float32)
    for s in range(slots):
        inside = (lane >= s * cols) & (lane < (s + 1) * cols)
        level = jnp.where(inside, open_slots[s], level)
        column = jnp.where(lane >= s * cols, lane - s * cols, column)
    return jnp.where(jnp.abs(column - query - shift) <= RC, level, NEG)


def heads_per_step(heads, most):
    return next(size for size in range(min(most, heads), 0, -1) if heads % size == 0)


def over_frames(mask_ref, frames, run):
    open_frames = [jnp.where(mask_ref[f] == 1, 0.0, NEG) for f in range(frames - 1)] + [jnp.float32(0.0)]
    closed = jnp.int32(frames - 1)
    for f in reversed(range(frames - 1)):
        closed = jnp.where(mask_ref[f] == 1, closed, f)

    @pl.when(closed < frames - 1)
    def _():
        run(
            lambda s: jnp.where(s < closed, s, s + 1),
            [jnp.where(s < closed, open_frames[s], open_frames[s + 1]) for s in range(frames - 1)],
        )

    @pl.when(closed == frames - 1)
    def _():
        run(lambda s: s, open_frames)


def attend(total_rows, cols, shift_ref, bias_ref, plan, places, query_row, kv_row, emit, each, ahead, frame_of, open_slots):
    step = pl.program_id(0)
    slots = len(open_slots)
    span = slots * cols
    padded = -(-span // 128) * 128
    queries = sorted({r for _, seen in plan for r in seen})
    near = {r: [(k, seen.index(r)) for k, (_, seen) in enumerate(plan) if r in seen] for r in queries}

    @pl.when(step == 0)
    def _():
        for at, r in enumerate(queries):
            row = jnp.clip(places[r], 0, total_rows - 1)
            bias_ref[at, :, :padded] = key_bias(cols, padded, slots, shift_ref[row], open_slots)

    def stack(which, n, part):
        pieces = [kv_row(which, frame_of(s), n, slice(None), part) for s in range(slots)]
        if padded > span:
            pieces.append(kv_row(which, frame_of(0), n, slice(0, padded - span), part))
        return jnp.concatenate(pieces, axis=0)

    def score(j):
        part = pl.ds(j * HD, HD)
        found = []
        for n, seen in plan:
            query = jnp.concatenate([query_row(r, part) for r in seen], axis=0)
            found.append(
                lax.dot_general(query, stack(0, n, part), (((1,), (1,)), ((), ())), preferred_element_type=jnp.float32)
            )
        return found

    def soften(found):
        pieces = [[None] * len(seen) for _, seen in plan]
        totals, tops = {}, {}
        for row, r in enumerate(queries):
            bias = bias_ref[row, :, :padded]
            blocks = [found[k][d * cols : (d + 1) * cols] + bias for k, d in near[r]]
            top = jnp.max(functools.reduce(jnp.maximum, blocks), axis=-1, keepdims=True) * SCALE2
            weights = [jnp.exp2(block * SCALE2 - top) for block in blocks]
            tops[r] = top
            for (k, d), weight in zip(near[r], weights):
                pieces[k][d] = weight.astype(jnp.bfloat16)
        return [jnp.concatenate(piece, axis=0) for piece in pieces], totals, tops

    def finish(j, weights, totals, tops):
        part = pl.ds(j * HD, HD)
        ones = jnp.ones((padded, HD), jnp.bfloat16)
        sums = [
            jnp.dot(
                weights[k],
                jnp.concatenate([stack(1, n, part), ones], axis=1),
                preferred_element_type=jnp.float32,
            )
            for k, (n, _) in enumerate(plan)
        ]
        for r in queries:
            acc = functools.reduce(jnp.add, [sums[k][d * cols : (d + 1) * cols] for k, d in near[r]])
            total = acc[:, HD:]
            emit(j, step * each + j, r, (acc[:, :HD] * (1.0 / total)).astype(jnp.bfloat16), tops[r], total)

    found, soft = {}, {}
    for j in range(each + ahead[0]):
        if j < each:
            found[j] = score(j)
        at = j - ahead[1]
        if 0 <= at < each:
            soft[at] = soften(found.pop(at))
        if j >= ahead[0]:
            finish(j - ahead[0], *soft.pop(j - ahead[0]))


def edge_kernel(
    total_rows, rows, each, shift_ref, mask_ref, qp_ref, qn_ref, kvf_ref, kvl_ref, op_ref, on_ref, bias_ref, level_ref
):
    step = pl.program_id(0)
    frames, cols = kvf_ref.shape[1], kvf_ref.shape[3]
    wide = op_ref.shape[1] - 3 * 128
    first_row = lax.axis_index("band") * rows
    lane = lax.broadcasted_iota(jnp.int32, (cols, 128), 1)
    sources, keys, targets = (qp_ref, qn_ref), (kvf_ref, kvl_ref), (op_ref, on_ref)

    @pl.when(step == 0)
    def _():
        level_ref[...] = jnp.zeros_like(level_ref)

    def emit(j, head, r, out, top, total):
        targets[r][:, pl.ds(pl.multiple_of(head * HD, HD), HD)] = out
        level_ref[r] = jnp.where(lane == head, top + jnp.log2(total), level_ref[r])

    over_frames(
        mask_ref,
        frames,
        functools.partial(
            attend,
            total_rows,
            cols,
            shift_ref,
            bias_ref,
            [(0, [0]), (1, [1])],
            [first_row - 1, first_row + rows],
            lambda r, part: sources[r][:, part],
            lambda which, f, n, some, part: keys[n][which, f, 0, some, part],
            emit,
            each,
            (3, 1),
        ),
    )

    @pl.when(step == pl.num_programs(0) - 1)
    def _():
        for side, o_ref in enumerate(targets):
            rest = level_ref[side]
            for k in range(3):
                piece = rest.astype(jnp.bfloat16)
                o_ref[:, wide + k * 128 : wide + (k + 1) * 128] = piece
                rest = rest - piece.astype(jnp.float32)


def main_kernel(
    total_rows, each, shift_ref, mask_ref, q_ref, kv_ref, dec_ref, out_ref, level_out, dec_out, bias_ref, held_ref, level_ref, sems
):
    step = pl.program_id(0)
    frames, rows, cols = kv_ref.shape[1], q_ref.shape[0], q_ref.shape[1]
    first_row = lax.axis_index("band") * rows
    lane = lax.broadcasted_iota(jnp.int32, (cols, 128), 1)

    fetch = pltpu.make_async_copy(dec_ref, held_ref, sems.at[0])
    store = pltpu.make_async_copy(held_ref, dec_out, sems.at[1])
    final = pl.num_programs(0) - 1

    @pl.when(step == 0)
    def _():
        fetch.start()
        level_ref[...] = jnp.zeros_like(level_ref)

    def emit(j, head, r, out, top, total):
        out_ref[r, :, j * HD : (j + 1) * HD] = out
        for side, edge in enumerate((0, rows - 1)):
            if r == edge:
                level_ref[side] = jnp.where(lane == head, top + jnp.log2(total), level_ref[side])

    over_frames(
        mask_ref,
        frames,
        functools.partial(
            attend,
            total_rows,
            cols,
            shift_ref,
            bias_ref,
            [(n, list(range(max(n - 1, 0), min(n + 2, rows)))) for n in range(rows)],
            [first_row + r for r in range(rows)],
            lambda r, part: q_ref[r, :, part],
            lambda which, f, n, some, part: kv_ref[which, f, n, some, part],
            emit,
            each,
            (1, 1),
        ),
    )

    @pl.when(step == jnp.minimum(1, final))
    def _():
        fetch.wait()
        store.start()

    @pl.when(step == final)
    def _():
        levels = pltpu.make_async_copy(level_ref, level_out.at[pl.ds(0, 2)], sems.at[2])
        levels.start()
        store.wait()
        levels.wait()


def combine_kernel(own_in, lev_in, op_in, on_in, out_ref, own_ref, lev_ref, op_ref, on_ref, loads, stores):
    place = lax.axis_index("band")
    count = lax.axis_size("band")
    cols, wide = own_ref.shape[1:]
    last = own_in.shape[0] - 1
    heads = wide // HD
    chunks = next(size for size in (4, 2, 1) if heads % size == 0)
    some = wide // chunks
    rows_of = ((0, 0), (1, last))
    copies = [
        pltpu.make_async_copy(source, target, loads.at[k])
        for k, (source, target) in enumerate(((lev_in.at[pl.ds(0, 2)], lev_ref), (op_in, op_ref), (on_in, on_ref)))
    ]
    owns, outs = [], []
    for side, row in rows_of:
        for c in range(chunks):
            part = pl.ds(c * some, some)
            at = side * chunks + c
            owns.append(pltpu.make_async_copy(own_in.at[row, :, part], own_ref.at[side, :, part], loads.at[3 + at]))
            outs.append(pltpu.make_async_copy(own_ref.at[side, :, part], out_ref.at[row, :, part], stores.at[at]))
    for copy in copies[:2] + owns[:chunks] + copies[2:] + owns[chunks:]:
        copy.start()
    copies[0].wait()
    for side, (o_ref, there) in enumerate(((op_ref, place > 0), (on_ref, place < count - 1))):
        copies[1 + side].wait()
        other = sum(o_ref[:, wide + k * 128 : wide + (k + 1) * 128].astype(jnp.float32) for k in range(3))
        share = jnp.where(there, 1.0 / (1.0 + jnp.exp2(lev_ref[side] - other)), 0.0)
        for c in range(chunks):
            owns[side * chunks + c].wait()
            for j in range(c * (heads // chunks), (c + 1) * (heads // chunks)):
                part = slice(j * HD, (j + 1) * HD)
                here = own_ref[side, :, part].astype(jnp.float32)
                far = o_ref[:, part].astype(jnp.float32)
                own_ref[side, :, part] = (here + (far - here) * share[:, j : j + 1]).astype(jnp.bfloat16)
            outs[side * chunks + c].start()
    for out in outs:
        out.wait()


def fixed(shape):
    return pl.BlockSpec(shape, lambda *_: (0,) * len(shape))


def lanes(shape, row=None):
    lead = (0,) * (len(shape) - 1) if row is None else (0,) * (len(shape) - 3) + (row, 0)
    return pl.BlockSpec(shape, lambda h: lead + (h,))


def edge_attention(kv_frames, frame_mask, col_shift, q_prev, q_next):
    frames, rows, cols, wide = kv_frames.shape[1:]
    heads = wide // HD
    each = heads_per_step(heads, EDGE_HEADS)
    smem = pl.BlockSpec(memory_space=pltpu.SMEM)
    packed = wide + 3 * 128
    padded = -(-frames * cols // 128) * 128
    return pl.pallas_call(
        functools.partial(edge_kernel, col_shift.shape[0], rows, each),
        grid=(heads // each,),
        out_shape=(jax.ShapeDtypeStruct((cols, packed), jnp.bfloat16),) * 2,
        in_specs=[
            smem,
            smem,
            lanes((cols, each * HD)),
            lanes((cols, each * HD)),
            lanes((2, frames, 1, cols, each * HD), 0),
            lanes((2, frames, 1, cols, each * HD), rows - 1),
        ],
        out_specs=(fixed((cols, packed)),) * 2,
        scratch_shapes=[
            pltpu.VMEM((2, cols, padded), jnp.float32),
            pltpu.VMEM((2, cols, 128), jnp.float32),
        ],
        compiler_params=pltpu.CompilerParams(vmem_limit_bytes=VMEM_BYTES),
        cost_estimate=pl.CostEstimate(
            flops=8 * cols * frames * cols * wide,
            bytes_accessed=4 * frames * cols * wide * 2,
            transcendentals=2 * heads * cols * frames * cols,
        ),
        name="edge_attention",
    )(col_shift, frame_mask, q_prev, q_next, kv_frames, kv_frames)


def main_attention(queries, kv_frames, frame_mask, col_shift, decoded):
    rows, cols, wide = queries.shape
    frames = kv_frames.shape[1]
    heads = wide // HD
    each = heads_per_step(heads, HEADS_PER_STEP)
    anywhere = pl.BlockSpec(memory_space=pl.ANY)
    smem = pl.BlockSpec(memory_space=pltpu.SMEM)
    padded = -(-frames * cols // 128) * 128
    return pl.pallas_call(
        functools.partial(main_kernel, col_shift.shape[0], each),
        grid=(heads // each,),
        out_shape=(
            jax.ShapeDtypeStruct(queries.shape, jnp.bfloat16),
            jax.ShapeDtypeStruct((LEVEL_BYTES // (cols * 512), cols, 128), jnp.float32),
            jax.ShapeDtypeStruct(decoded.shape, decoded.dtype),
        ),
        in_specs=[smem, smem, lanes((rows, cols, each * HD)), lanes((2, frames, rows, cols, each * HD)), anywhere],
        out_specs=(lanes((rows, cols, each * HD)), anywhere, anywhere),
        scratch_shapes=[
            pltpu.VMEM((rows, cols, padded), jnp.float32),
            pltpu.VMEM(decoded.shape, decoded.dtype),
            pltpu.VMEM((2, cols, 128), jnp.float32),
            pltpu.SemaphoreType.DMA((3,)),
        ],
        compiler_params=pltpu.CompilerParams(vmem_limit_bytes=VMEM_BYTES),
        cost_estimate=pl.CostEstimate(
            flops=4 * rows * cols * 3 * frames * cols * wide,
            bytes_accessed=2 * rows * frames * cols * wide * 2,
            transcendentals=rows * heads * cols * 3 * frames * cols,
        ),
        name="main_attention",
    )(col_shift, frame_mask, queries, kv_frames, decoded)


def combine(partial, level, back_prev, back_next):
    rows, cols, wide = partial.shape
    anywhere = pl.BlockSpec(memory_space=pl.ANY)
    return pl.pallas_call(
        combine_kernel,
        out_shape=jax.ShapeDtypeStruct(partial.shape, jnp.bfloat16),
        in_specs=[anywhere] * 4,
        out_specs=anywhere,
        input_output_aliases={0: 0},
        scratch_shapes=[
            pltpu.VMEM((2, cols, wide), jnp.bfloat16),
            pltpu.VMEM((2, cols, 128), jnp.float32),
            pltpu.VMEM(back_prev.shape, jnp.bfloat16),
            pltpu.VMEM(back_next.shape, jnp.bfloat16),
            pltpu.SemaphoreType.DMA((11,)),
            pltpu.SemaphoreType.DMA((8,)),
        ],
        compiler_params=pltpu.CompilerParams(vmem_limit_bytes=COMBINE_BYTES),
        name="combine",
    )(partial, level, back_prev, back_next)


def hail(place, count):
    barrier = pltpu.get_barrier_semaphore()

    @pl.when(place > 0)
    def _():
        pl.semaphore_signal(barrier, 1, device_id={"band": place - 1}, device_id_type=MESH)

    @pl.when(place < count - 1)
    def _():
        pl.semaphore_signal(barrier, 1, device_id={"band": place + 1}, device_id_type=MESH)


def meet(place, count):
    barrier = pltpu.get_barrier_semaphore()
    pl.semaphore_wait(barrier, jnp.where(place > 0, 1, 0) + jnp.where(place < count - 1, 1, 0))


def swap(place, count, sends, arrivals, up, down):
    def make(triple, other):
        source, target, at = triple
        return pltpu.make_async_remote_copy(
            src_ref=source,
            dst_ref=target,
            send_sem=sends.at[at],
            recv_sem=arrivals.at[at],
            device_id={"band": other},
            device_id_type=MESH,
        )

    ups = [make(triple, jnp.minimum(place + 1, count - 1)) for triple in up]
    downs = [make(triple, jnp.maximum(place - 1, 0)) for triple in down]

    def start(which):
        @pl.when(place < count - 1)
        def _():
            for at in which:
                ups[at].start()

        @pl.when(place > 0)
        def _():
            for at in which:
                downs[at].start()

    def arrive(which):
        @pl.when(place > 0)
        def _():
            for at in which:
                ups[at].wait_recv()

        @pl.when(place < count - 1)
        def _():
            for at in which:
                downs[at].wait_recv()

    def sent(which):
        @pl.when(place < count - 1)
        def _():
            for at in which:
                ups[at].wait_send()

        @pl.when(place > 0)
        def _():
            for at in which:
                downs[at].wait_send()

    return start, arrive, sent


def decoder_kernel(
    q_ref, lat_in, cin_in, wmid_in, bin_in, gain_in, bmid_in, qp_ref, qn_ref, dec_out,
    high_ref, low_ref, below_ref, above_ref, ext_ref, pair_ref, rest_ref, win_ref, wmid_ref, first_ref, act_ref, dec_ref,
    lat_ref, cin_ref, bin_ref, gain_ref, bmid_ref,
    sends, arrivals, local_sem, load_sem, out_sem
):
    place = lax.axis_index("band")
    count = lax.axis_size("band")
    last = q_ref.shape[0] - 1
    hail(place, count)
    named = [
        (lat_in, lat_ref), (cin_in, cin_ref), (bin_in, bin_ref), (gain_in, gain_ref), (bmid_in, bmid_ref),
        (wmid_in, wmid_ref),
    ]
    loads = [pltpu.make_async_copy(source, target, load_sem.at[k]) for k, (source, target) in enumerate(named)]
    for load in loads:
        load.start()
    middle = loads.pop()
    times, rows, packed = lat_ref.shape
    depth = cin_ref.shape[0] // 27
    taps = 3 * depth
    width = packed // depth
    ch = cin_ref.shape[1]
    tiles = packed // 128
    per = 128 // depth
    start, arrive, sent = swap(
        place,
        count,
        sends,
        arrivals,
        [(high_ref, below_ref, 0), (q_ref.at[last], qp_ref, 1)],
        [(low_ref, above_ref, 2), (q_ref.at[0], qn_ref, 3)],
    )
    meet(place, count)
    start((1,))

    @pl.when(place == 0)
    def _():
        below_ref[...] = jnp.zeros_like(below_ref)
        pltpu.make_async_copy(q_ref.at[0], qp_ref, local_sem.at[0]).start()

    @pl.when(place == count - 1)
    def _():
        above_ref[...] = jnp.zeros_like(above_ref)
        pltpu.make_async_copy(q_ref.at[last], qn_ref, local_sem.at[1]).start()

    sub = lax.broadcasted_iota(jnp.int32, (8, packed), 0)

    def gather(target, shifts):
        rows_of = [pltpu.roll(lat_ref[dt].astype(jnp.float32), shifts[dt], 0) for dt in range(3)]
        target[...] = jnp.where(sub < 2, rows_of[0], jnp.where(sub < 4, rows_of[1], rows_of[2])).astype(jnp.bfloat16)

    loads[0].wait()
    gather(high_ref, [2, 4, 6])
    gather(low_ref, [0, 2, 4])
    start((0,))

    at_row = (0, taps, 128)
    ext_ref[:, :, :128] = jnp.zeros((times, 8, 128), jnp.float32)
    ext_ref[:, :, 128 + packed :] = jnp.zeros((times, 8, 128), jnp.float32)
    lane = lax.broadcasted_iota(jnp.int32, (8, 128), 1)

    def spread(base):
        @pl.loop(0, tiles, unroll=tiles)
        def _(t):
            here = [ext_ref[dt, :, pl.ds(pl.multiple_of((t + 1) * 128, 128), 128)] for dt in range(3)]
            left = [ext_ref[dt, :, pl.ds(pl.multiple_of(t * 128, 128), 128)] for dt in range(3)]
            right = [ext_ref[dt, :, pl.ds(pl.multiple_of((t + 2) * 128, 128), 128)] for dt in range(3)]
            for j in range(per):
                moved = []
                for dt in range(3):
                    piece = here[dt]
                    if j == 0:
                        piece = jnp.where(lane >= 128 - depth, left[dt], piece)
                    if j == per - 1:
                        piece = jnp.where(lane < depth, right[dt], piece)
                    shift = (at_row[dt] - depth * (j - 1)) % 128
                    moved.append(pltpu.roll(piece, shift, 1) if shift else piece)
                both = jnp.where(lane < taps, moved[0], jnp.where(lane < 2 * taps, moved[1], 0.0))
                at = pl.ds(base * width + t * per + j, 8, stride=width)
                pair_ref[at, :] = both
                rest_ref[at, :] = jnp.where(lane < taps, moved[2], 0.0)

    x_at = lax.broadcasted_iota(jnp.int32, (width, ch), 0)

    def place_of(y):
        return y + rows + 8 if y < 2 else y

    def convolve(i, group):
        total = jnp.zeros((group * width, ch), jnp.float32)
        for dy in range(3):
            at = [place_of(i + g + dy) * width for g in range(group)]
            source = [jnp.concatenate([ref[here : here + width, :] for here in at], axis=0) for ref in (pair_ref, rest_ref)]
            source = jnp.concatenate(source, axis=1).astype(jnp.bfloat16)
            total += jnp.dot(source, win_ref[dy], preferred_element_type=jnp.float32)
        return total + bin_ref[...][None]

    def activate(i, group, total):
        scale = lax.rsqrt(jnp.mean(total * total, axis=-1, keepdims=True) + 1e-06)
        value = total * scale * gain_ref[...][None]
        half = 0.5 * value
        active = half + half * jnp.tanh(half)
        for g in range(group):
            row = i + g
            mine = active[g * width : (g + 1) * width]
            if row == 0:
                mine = jnp.where(place == 0, 0.0, mine)
            if row == rows + 1:
                mine = jnp.where(place == count - 1, 0.0, mine)
            first_ref[row] = total[g * width : (g + 1) * width]
            at = slice(row * width, (row + 1) * width)
            act_ref[at, 0:ch] = jnp.where(x_at == 0, 0.0, pltpu.roll(mine, 1, 0)).astype(jnp.bfloat16)
            act_ref[at, ch : 2 * ch] = mine.astype(jnp.bfloat16)
            act_ref[at, 2 * ch : 3 * ch] = jnp.where(x_at == width - 1, 0.0, pltpu.roll(mine, width - 1, 0)).astype(
                jnp.bfloat16
            )

    def decode(at, many):
        source = [act_ref[(at + dy) * width : (at + dy + many) * width, :] for dy in range(3)]
        total = jnp.dot(jnp.concatenate(source, axis=1), wmid_ref[...], preferred_element_type=jnp.float32)
        total = total + bmid_ref[...][None]
        for y in range(many):
            dec_ref[at + y] = (total[y * width : (y + 1) * width] + first_ref[at + y + 1]).astype(jnp.bfloat16)
        some = pl.ds(at, many)
        store = pltpu.make_async_copy(dec_ref.at[some], dec_out.at[some], out_sem.at[at // many])
        store.start()
        stores.append(store)

    stores = []
    group = 2 if rows % 2 == 0 else 1
    for dt in range(3):
        ext_ref[dt, :, 128 : 128 + packed] = lat_ref[dt].astype(jnp.float32)
    spread(2)
    for load in loads[1:]:
        load.wait()
    win_ref[...] = jnp.zeros_like(win_ref)
    for dy in range(3):
        for dt in range(3):
            source = (dt * 3 + dy) * taps
            win_ref[dy, at_row[dt] : at_row[dt] + taps] = cin_ref[source : source + taps]
    order = list(range(2, rows, group)) + [0, rows]
    size = {i: group for i in order}
    size[0] = size[rows] = 2
    done, ready = set(), []
    spans = [(at, group) for at in range(0, rows, group)]
    middle_waited = False
    total = convolve(order[0], size[order[0]])
    for k, i in enumerate(order):
        here = total
        if k + 1 < len(order):
            if order[k + 1] == 0:
                arrive((0,))
                for dt in range(3):
                    up = pltpu.roll(above_ref[...].astype(jnp.float32), (8 - 2 * dt) % 8, 0)
                    down = pltpu.roll(below_ref[...].astype(jnp.float32), 6 - 2 * dt, 0)
                    ext_ref[dt, :, 128 : 128 + packed] = jnp.where(sub < 4, up, down)
                spread(rows + 2)
                middle.wait()
                middle_waited = True
            total = convolve(order[k + 1], size[order[k + 1]])
        if middle_waited:
            ready = [span for span in spans if set(range(span[0], span[0] + span[1] + 2)) <= done]
            for span in ready[:1]:
                spans.remove(span)
                decode(*span)
        activate(i, size[i], here)
        done |= set(range(i, i + size[i]))
    for span in spans:
        decode(*span)

    arrive((1,))
    sent((0, 1))

    @pl.when(place == 0)
    def _():
        pltpu.make_async_copy(q_ref.at[0], qp_ref, local_sem.at[0]).wait()

    @pl.when(place == count - 1)
    def _():
        pltpu.make_async_copy(q_ref.at[last], qn_ref, local_sem.at[1]).wait()

    for store in stores:
        store.wait()


def decoder(queries, latent, conv_in, bias_in, norm_gain, conv_mid, bias_mid):
    cols, wide = queries.shape[1:]
    times, rows, packed = latent.shape
    ch = conv_in.shape[1]
    width = packed // (conv_in.shape[0] // 27)
    anywhere = pl.BlockSpec(memory_space=pl.ANY)
    return pl.pallas_call(
        decoder_kernel,
        out_shape=(
            jax.ShapeDtypeStruct((cols, wide), jnp.bfloat16),
            jax.ShapeDtypeStruct((cols, wide), jnp.bfloat16),
            jax.ShapeDtypeStruct((rows, width, ch), jnp.bfloat16),
        ),
        in_specs=[anywhere] * 7,
        out_specs=(anywhere,) * 3,
        scratch_shapes=[
            *[pltpu.VMEM((8, packed), jnp.bfloat16)] * 4,
            pltpu.VMEM((times, 8, packed + 256), jnp.float32),
            pltpu.VMEM(((rows + 10) * width, 128), jnp.float32),
            pltpu.VMEM(((rows + 10) * width, 128), jnp.float32),
            pltpu.VMEM((3, 256, ch), jnp.bfloat16),
            pltpu.VMEM(conv_mid.shape, jnp.bfloat16),
            pltpu.VMEM((rows + 2, width, ch), jnp.float32),
            pltpu.VMEM(((rows + 2) * width, 3 * ch), jnp.bfloat16),
            pltpu.VMEM((rows, width, ch), jnp.bfloat16),
            pltpu.VMEM(latent.shape, jnp.bfloat16),
            pltpu.VMEM(conv_in.shape, jnp.bfloat16),
            *[pltpu.VMEM((ch,), jnp.float32)] * 3,
            pltpu.SemaphoreType.DMA((4,)),
            pltpu.SemaphoreType.DMA((4,)),
            pltpu.SemaphoreType.DMA((2,)),
            pltpu.SemaphoreType.DMA((6,)),
            pltpu.SemaphoreType.DMA((rows,)),
        ],
        compiler_params=pltpu.CompilerParams(
            collective_id=0, has_side_effects=True, vmem_limit_bytes=VMEM_BYTES
        ),
        name="decoder",
    )(queries, latent, conv_in, conv_mid, bias_in, norm_gain, bias_mid)


def body(
    queries, kv_frames, frame_mask, col_shift, latent, conv_in, bias_in, norm_gain, conv_mid, bias_mid
):
    q_prev, q_next, decoded = decoder(queries, latent, conv_in, bias_in, norm_gain, conv_mid, bias_mid)
    o_prev, o_next = edge_attention(kv_frames, frame_mask, col_shift, q_prev, q_next)
    back_prev = to_next(o_next, "band")
    back_next = to_previous(o_prev, "band")
    partial, level, decoded = main_attention(queries, kv_frames, frame_mask, col_shift, decoded)
    return (combine(partial, level, back_prev, back_next), decoded)


def solution(mesh):
    placed = (
        P(("groups", "band"), None, None),
        P("groups", None, "band", None, None),
        P("groups"),
        P("groups"),
        P("groups", "band", None),
        P(),
        P(),
        P(),
        P(),
        P(),
    )
    return jax.shard_map(
        body,
        mesh=mesh,
        in_specs=placed,
        out_specs=(P(("groups", "band"), None, None), P(("groups", "band"), None, None)),
        check_vma=False,
    )
```

```python
import functools
import math

import jax
import jax.numpy as jnp
from jax import lax
from jax.experimental import pallas as pl
from jax.experimental.pallas import tpu as pltpu
from jax.sharding import PartitionSpec as P

HD = 128
RC = 8
NEG = -1e30
MESH = pl.DeviceIdType.MESH
SCALE2 = math.log2(math.e) / math.sqrt(HD)
HEADS_PER_STEP = 5
EDGE_HEADS = 10
VMEM_BYTES = 56 * 2**20
COMBINE_BYTES = 48 * 2**20
LEVEL_BYTES = 24 * 2**20


def to_next(block, axis):
    count = lax.axis_size(axis)
    return lax.ppermute(block, axis, [(i, i + 1) for i in range(count - 1)])


def to_previous(block, axis):
    count = lax.axis_size(axis)
    return lax.ppermute(block, axis, [(i + 1, i) for i in range(count - 1)])


def key_bias(cols, padded, slots, shift, open_slots):
    lane = lax.broadcasted_iota(jnp.int32, (cols, padded), 1)
    query = lax.broadcasted_iota(jnp.int32, (cols, padded), 0)
    column = lane
    level = jnp.full((cols, padded), NEG, jnp.float32)
    for s in range(slots):
        inside = (lane >= s * cols) & (lane < (s + 1) * cols)
        level = jnp.where(inside, open_slots[s], level)
        column = jnp.where(lane >= s * cols, lane - s * cols, column)
    return jnp.where(jnp.abs(column - query - shift) <= RC, level, NEG)


def heads_per_step(heads, most):
    return next(size for size in range(min(most, heads), 0, -1) if heads % size == 0)


def over_frames(mask_ref, frames, run):
    open_frames = [jnp.where(mask_ref[f] == 1, 0.0, NEG) for f in range(frames - 1)] + [jnp.float32(0.0)]
    closed = jnp.int32(frames - 1)
    for f in reversed(range(frames - 1)):
        closed = jnp.where(mask_ref[f] == 1, closed, f)

    @pl.when(closed < frames - 1)
    def _():
        run(
            lambda s: jnp.where(s < closed, s, s + 1),
            [jnp.where(s < closed, open_frames[s], open_frames[s + 1]) for s in range(frames - 1)],
        )

    @pl.when(closed == frames - 1)
    def _():
        run(lambda s: s, open_frames)


def attend(total_rows, cols, shift_ref, bias_ref, plan, places, query_row, kv_row, emit, each, ahead, frame_of, open_slots):
    step = pl.program_id(0)
    slots = len(open_slots)
    span = slots * cols
    padded = -(-span // 128) * 128
    queries = sorted({r for _, seen in plan for r in seen})
    near = {r: [(k, seen.index(r)) for k, (_, seen) in enumerate(plan) if r in seen] for r in queries}

    @pl.when(step == 0)
    def _():
        for at, r in enumerate(queries):
            row = jnp.clip(places[r], 0, total_rows - 1)
            bias_ref[at, :, :padded] = key_bias(cols, padded, slots, shift_ref[row], open_slots)

    def stack(which, n, part):
        pieces = [kv_row(which, frame_of(s), n, slice(None), part) for s in range(slots)]
        if padded > span:
            pieces.append(kv_row(which, frame_of(0), n, slice(0, padded - span), part))
        return jnp.concatenate(pieces, axis=0)

    def score(j):
        part = pl.ds(j * HD, HD)
        found = []
        for n, seen in plan:
            query = jnp.concatenate([query_row(r, part) for r in seen], axis=0)
            found.append(
                lax.dot_general(query, stack(0, n, part), (((1,), (1,)), ((), ())), preferred_element_type=jnp.float32)
            )
        return found

    def soften(found):
        pieces = [[None] * len(seen) for _, seen in plan]
        totals, tops = {}, {}
        for row, r in enumerate(queries):
            bias = bias_ref[row, :, :padded]
            blocks = [found[k][d * cols : (d + 1) * cols] + bias for k, d in near[r]]
            top = jnp.max(functools.reduce(jnp.maximum, blocks), axis=-1, keepdims=True) * SCALE2
            weights = [jnp.exp2(block * SCALE2 - top) for block in blocks]
            tops[r] = top
            for (k, d), weight in zip(near[r], weights):
                pieces[k][d] = weight.astype(jnp.bfloat16)
        return [jnp.concatenate(piece, axis=0) for piece in pieces], totals, tops

    def finish(j, weights, totals, tops):
        part = pl.ds(j * HD, HD)
        ones = jnp.ones((padded, HD), jnp.bfloat16)
        sums = [
            jnp.dot(
                weights[k],
                jnp.concatenate([stack(1, n, part), ones], axis=1),
                preferred_element_type=jnp.float32,
            )
            for k, (n, _) in enumerate(plan)
        ]
        for r in queries:
            acc = functools.reduce(jnp.add, [sums[k][d * cols : (d + 1) * cols] for k, d in near[r]])
            total = acc[:, HD:]
            emit(j, step * each + j, r, (acc[:, :HD] * (1.0 / total)).astype(jnp.bfloat16), tops[r], total)

    found, soft = {}, {}
    for j in range(each + ahead[0]):
        if j < each:
            found[j] = score(j)
        at = j - ahead[1]
        if 0 <= at < each:
            soft[at] = soften(found.pop(at))
        if j >= ahead[0]:
            finish(j - ahead[0], *soft.pop(j - ahead[0]))


def edge_kernel(
    total_rows, rows, each, shift_ref, mask_ref, qp_ref, qn_ref, kvf_ref, kvl_ref, op_ref, on_ref, bias_ref, level_ref
):
    step = pl.program_id(0)
    frames, cols = kvf_ref.shape[1], kvf_ref.shape[3]
    wide = op_ref.shape[1] - 3 * 128
    first_row = lax.axis_index("band") * rows
    lane = lax.broadcasted_iota(jnp.int32, (cols, 128), 1)
    sources, keys, targets = (qp_ref, qn_ref), (kvf_ref, kvl_ref), (op_ref, on_ref)

    @pl.when(step == 0)
    def _():
        level_ref[...] = jnp.zeros_like(level_ref)

    def emit(j, head, r, out, top, total):
        targets[r][:, pl.ds(pl.multiple_of(head * HD, HD), HD)] = out
        level_ref[r] = jnp.where(lane == head, top + jnp.log2(total), level_ref[r])

    over_frames(
        mask_ref,
        frames,
        functools.partial(
            attend,
            total_rows,
            cols,
            shift_ref,
            bias_ref,
            [(0, [0]), (1, [1])],
            [first_row - 1, first_row + rows],
            lambda r, part: sources[r][:, part],
            lambda which, f, n, some, part: keys[n][which, f, 0, some, part],
            emit,
            each,
            (3, 1),
        ),
    )

    @pl.when(step == pl.num_programs(0) - 1)
    def _():
        for side, o_ref in enumerate(targets):
            rest = level_ref[side]
            for k in range(3):
                piece = rest.astype(jnp.bfloat16)
                o_ref[:, wide + k * 128 : wide + (k + 1) * 128] = piece
                rest = rest - piece.astype(jnp.float32)


def main_kernel(
    total_rows, each, shift_ref, mask_ref, q_ref, kv_ref, dec_ref, out_ref, level_ref, dec_out, bias_ref, held_ref, sems
):
    step = pl.program_id(0)
    frames, rows, cols = kv_ref.shape[1], q_ref.shape[0], q_ref.shape[1]
    first_row = lax.axis_index("band") * rows
    lane = lax.broadcasted_iota(jnp.int32, (cols, 128), 1)

    fetch = pltpu.make_async_copy(dec_ref, held_ref, sems.at[0])
    store = pltpu.make_async_copy(held_ref, dec_out, sems.at[1])
    final = pl.num_programs(0) - 1

    @pl.when(step == 0)
    def _():
        fetch.start()
        level_ref[...] = jnp.zeros_like(level_ref)

    def emit(j, head, r, out, top, total):
        out_ref[r, :, j * HD : (j + 1) * HD] = out
        for side, edge in enumerate((0, rows - 1)):
            if r == edge:
                level_ref[side] = jnp.where(lane == head, top + jnp.log2(total), level_ref[side])

    over_frames(
        mask_ref,
        frames,
        functools.partial(
            attend,
            total_rows,
            cols,
            shift_ref,
            bias_ref,
            [(n, list(range(max(n - 1, 0), min(n + 2, rows)))) for n in range(rows)],
            [first_row + r for r in range(rows)],
            lambda r, part: q_ref[r, :, part],
            lambda which, f, n, some, part: kv_ref[which, f, n, some, part],
            emit,
            each,
            (1, 1),
        ),
    )

    @pl.when(step == jnp.minimum(1, final))
    def _():
        fetch.wait()
        store.start()

    @pl.when(step == final)
    def _():
        store.wait()


def combine_kernel(own_in, lev_in, op_in, on_in, out_ref, own_ref, lev_ref, op_ref, on_ref, loads, stores):
    place = lax.axis_index("band")
    count = lax.axis_size("band")
    cols, wide = own_ref.shape[1:]
    last = own_in.shape[0] - 1
    heads = wide // HD
    chunks = next(size for size in (4, 2, 1) if heads % size == 0)
    some = wide // chunks
    rows_of = ((0, 0), (1, last))
    copies = [
        pltpu.make_async_copy(source, target, loads.at[k])
        for k, (source, target) in enumerate(((lev_in.at[pl.ds(0, 2)], lev_ref), (op_in, op_ref), (on_in, on_ref)))
    ]
    owns, outs = [], []
    for side, row in rows_of:
        for c in range(chunks):
            part = pl.ds(c * some, some)
            at = side * chunks + c
            owns.append(pltpu.make_async_copy(own_in.at[row, :, part], own_ref.at[side, :, part], loads.at[3 + at]))
            outs.append(pltpu.make_async_copy(own_ref.at[side, :, part], out_ref.at[row, :, part], stores.at[at]))
    for copy in copies[:2] + owns[:chunks] + copies[2:] + owns[chunks:]:
        copy.start()
    copies[0].wait()
    for side, (o_ref, there) in enumerate(((op_ref, place > 0), (on_ref, place < count - 1))):
        copies[1 + side].wait()
        other = sum(o_ref[:, wide + k * 128 : wide + (k + 1) * 128].astype(jnp.float32) for k in range(3))
        share = jnp.where(there, 1.0 / (1.0 + jnp.exp2(lev_ref[side] - other)), 0.0)
        for c in range(chunks):
            owns[side * chunks + c].wait()
            for j in range(c * (heads // chunks), (c + 1) * (heads // chunks)):
                part = slice(j * HD, (j + 1) * HD)
                here = own_ref[side, :, part].astype(jnp.float32)
                far = o_ref[:, part].astype(jnp.float32)
                own_ref[side, :, part] = (here + (far - here) * share[:, j : j + 1]).astype(jnp.bfloat16)
            outs[side * chunks + c].start()
    for out in outs:
        out.wait()


def fixed(shape):
    return pl.BlockSpec(shape, lambda *_: (0,) * len(shape))


def lanes(shape, row=None):
    lead = (0,) * (len(shape) - 1) if row is None else (0,) * (len(shape) - 3) + (row, 0)
    return pl.BlockSpec(shape, lambda h: lead + (h,))


def edge_attention(kv_frames, frame_mask, col_shift, q_prev, q_next):
    frames, rows, cols, wide = kv_frames.shape[1:]
    heads = wide // HD
    each = heads_per_step(heads, EDGE_HEADS)
    smem = pl.BlockSpec(memory_space=pltpu.SMEM)
    packed = wide + 3 * 128
    padded = -(-frames * cols // 128) * 128
    return pl.pallas_call(
        functools.partial(edge_kernel, col_shift.shape[0], rows, each),
        grid=(heads // each,),
        out_shape=(jax.ShapeDtypeStruct((cols, packed), jnp.bfloat16),) * 2,
        in_specs=[
            smem,
            smem,
            lanes((cols, each * HD)),
            lanes((cols, each * HD)),
            lanes((2, frames, 1, cols, each * HD), 0),
            lanes((2, frames, 1, cols, each * HD), rows - 1),
        ],
        out_specs=(fixed((cols, packed)),) * 2,
        scratch_shapes=[
            pltpu.VMEM((2, cols, padded), jnp.float32),
            pltpu.VMEM((2, cols, 128), jnp.float32),
        ],
        compiler_params=pltpu.CompilerParams(vmem_limit_bytes=VMEM_BYTES),
        cost_estimate=pl.CostEstimate(
            flops=8 * cols * frames * cols * wide,
            bytes_accessed=4 * frames * cols * wide * 2,
            transcendentals=2 * heads * cols * frames * cols,
        ),
        name="edge_attention",
    )(col_shift, frame_mask, q_prev, q_next, kv_frames, kv_frames)


def main_attention(queries, kv_frames, frame_mask, col_shift, decoded):
    rows, cols, wide = queries.shape
    frames = kv_frames.shape[1]
    heads = wide // HD
    each = heads_per_step(heads, HEADS_PER_STEP)
    anywhere = pl.BlockSpec(memory_space=pl.ANY)
    smem = pl.BlockSpec(memory_space=pltpu.SMEM)
    padded = -(-frames * cols // 128) * 128
    return pl.pallas_call(
        functools.partial(main_kernel, col_shift.shape[0], each),
        grid=(heads // each,),
        out_shape=(
            jax.ShapeDtypeStruct(queries.shape, jnp.bfloat16),
            jax.ShapeDtypeStruct((LEVEL_BYTES // (cols * 512), cols, 128), jnp.float32),
            jax.ShapeDtypeStruct(decoded.shape, decoded.dtype),
        ),
        in_specs=[smem, smem, lanes((rows, cols, each * HD)), lanes((2, frames, rows, cols, each * HD)), anywhere],
        out_specs=(lanes((rows, cols, each * HD)), fixed((2, cols, 128)), anywhere),
        scratch_shapes=[
            pltpu.VMEM((rows, cols, padded), jnp.float32),
            pltpu.VMEM(decoded.shape, decoded.dtype),
            pltpu.SemaphoreType.DMA((2,)),
        ],
        compiler_params=pltpu.CompilerParams(vmem_limit_bytes=VMEM_BYTES),
        cost_estimate=pl.CostEstimate(
            flops=4 * rows * cols * 3 * frames * cols * wide,
            bytes_accessed=2 * rows * frames * cols * wide * 2,
            transcendentals=rows * heads * cols * 3 * frames * cols,
        ),
        name="main_attention",
    )(col_shift, frame_mask, queries, kv_frames, decoded)


def combine(partial, level, back_prev, back_next):
    rows, cols, wide = partial.shape
    anywhere = pl.BlockSpec(memory_space=pl.ANY)
    return pl.pallas_call(
        combine_kernel,
        out_shape=jax.ShapeDtypeStruct(partial.shape, jnp.bfloat16),
        in_specs=[anywhere] * 4,
        out_specs=anywhere,
        input_output_aliases={0: 0},
        scratch_shapes=[
            pltpu.VMEM((2, cols, wide), jnp.bfloat16),
            pltpu.VMEM((2, cols, 128), jnp.float32),
            pltpu.VMEM(back_prev.shape, jnp.bfloat16),
            pltpu.VMEM(back_next.shape, jnp.bfloat16),
            pltpu.SemaphoreType.DMA((11,)),
            pltpu.SemaphoreType.DMA((8,)),
        ],
        compiler_params=pltpu.CompilerParams(vmem_limit_bytes=COMBINE_BYTES),
        name="combine",
    )(partial, level, back_prev, back_next)


def hail(place, count):
    barrier = pltpu.get_barrier_semaphore()

    @pl.when(place > 0)
    def _():
        pl.semaphore_signal(barrier, 1, device_id={"band": place - 1}, device_id_type=MESH)

    @pl.when(place < count - 1)
    def _():
        pl.semaphore_signal(barrier, 1, device_id={"band": place + 1}, device_id_type=MESH)


def meet(place, count):
    barrier = pltpu.get_barrier_semaphore()
    pl.semaphore_wait(barrier, jnp.where(place > 0, 1, 0) + jnp.where(place < count - 1, 1, 0))


def swap(place, count, sends, arrivals, up, down):
    def make(triple, other):
        source, target, at = triple
        return pltpu.make_async_remote_copy(
            src_ref=source,
            dst_ref=target,
            send_sem=sends.at[at],
            recv_sem=arrivals.at[at],
            device_id={"band": other},
            device_id_type=MESH,
        )

    ups = [make(triple, jnp.minimum(place + 1, count - 1)) for triple in up]
    downs = [make(triple, jnp.maximum(place - 1, 0)) for triple in down]

    def start(which):
        @pl.when(place < count - 1)
        def _():
            for at in which:
                ups[at].start()

        @pl.when(place > 0)
        def _():
            for at in which:
                downs[at].start()

    def arrive(which):
        @pl.when(place > 0)
        def _():
            for at in which:
                ups[at].wait_recv()

        @pl.when(place < count - 1)
        def _():
            for at in which:
                downs[at].wait_recv()

    def sent(which):
        @pl.when(place < count - 1)
        def _():
            for at in which:
                ups[at].wait_send()

        @pl.when(place > 0)
        def _():
            for at in which:
                downs[at].wait_send()

    return start, arrive, sent


def decoder_kernel(
    q_ref, lat_in, cin_in, wmid_in, bin_in, gain_in, bmid_in, qp_ref, qn_ref, dec_out,
    high_ref, low_ref, below_ref, above_ref, ext_ref, pair_ref, rest_ref, win_ref, wmid_ref, first_ref, act_ref, dec_ref,
    lat_ref, cin_ref, bin_ref, gain_ref, bmid_ref,
    sends, arrivals, local_sem, load_sem, out_sem
):
    place = lax.axis_index("band")
    count = lax.axis_size("band")
    last = q_ref.shape[0] - 1
    hail(place, count)
    named = [
        (lat_in, lat_ref), (cin_in, cin_ref), (bin_in, bin_ref), (gain_in, gain_ref), (bmid_in, bmid_ref),
        (wmid_in, wmid_ref),
    ]
    loads = [pltpu.make_async_copy(source, target, load_sem.at[k]) for k, (source, target) in enumerate(named)]
    for load in loads:
        load.start()
    middle = loads.pop()
    times, rows, packed = lat_ref.shape
    depth = cin_ref.shape[0] // 27
    taps = 3 * depth
    width = packed // depth
    ch = cin_ref.shape[1]
    tiles = packed // 128
    per = 128 // depth
    start, arrive, sent = swap(
        place,
        count,
        sends,
        arrivals,
        [(high_ref, below_ref, 0), (q_ref.at[last], qp_ref, 1)],
        [(low_ref, above_ref, 2), (q_ref.at[0], qn_ref, 3)],
    )
    sub = lax.broadcasted_iota(jnp.int32, (8, packed), 0)

    def gather(target, shifts):
        rows_of = [pltpu.roll(lat_ref[dt].astype(jnp.float32), shifts[dt], 0) for dt in range(3)]
        target[...] = jnp.where(sub < 2, rows_of[0], jnp.where(sub < 4, rows_of[1], rows_of[2])).astype(jnp.bfloat16)

    loads[0].wait()
    gather(high_ref, [2, 4, 6])
    gather(low_ref, [0, 2, 4])
    meet(place, count)
    start((0, 1))

    @pl.when(place == 0)
    def _():
        below_ref[...] = jnp.zeros_like(below_ref)
        pltpu.make_async_copy(q_ref.at[0], qp_ref, local_sem.at[0]).start()

    @pl.when(place == count - 1)
    def _():
        above_ref[...] = jnp.zeros_like(above_ref)
        pltpu.make_async_copy(q_ref.at[last], qn_ref, local_sem.at[1]).start()

    at_row = (0, taps, 128)
    ext_ref[:, :, :128] = jnp.zeros((times, 8, 128), jnp.float32)
    ext_ref[:, :, 128 + packed :] = jnp.zeros((times, 8, 128), jnp.float32)
    lane = lax.broadcasted_iota(jnp.int32, (8, 128), 1)

    def spread(base):
        @pl.loop(0, tiles, unroll=tiles)
        def _(t):
            here = [ext_ref[dt, :, pl.ds(pl.multiple_of((t + 1) * 128, 128), 128)] for dt in range(3)]
            left = [ext_ref[dt, :, pl.ds(pl.multiple_of(t * 128, 128), 128)] for dt in range(3)]
            right = [ext_ref[dt, :, pl.ds(pl.multiple_of((t + 2) * 128, 128), 128)] for dt in range(3)]
            for j in range(per):
                moved = []
                for dt in range(3):
                    piece = here[dt]
                    if j == 0:
                        piece = jnp.where(lane >= 128 - depth, left[dt], piece)
                    if j == per - 1:
                        piece = jnp.where(lane < depth, right[dt], piece)
                    shift = (at_row[dt] - depth * (j - 1)) % 128
                    moved.append(pltpu.roll(piece, shift, 1) if shift else piece)
                both = jnp.where(lane < taps, moved[0], jnp.where(lane < 2 * taps, moved[1], 0.0))
                at = pl.ds(base * width + t * per + j, 8, stride=width)
                pair_ref[at, :] = both
                rest_ref[at, :] = jnp.where(lane < taps, moved[2], 0.0)

    x_at = lax.broadcasted_iota(jnp.int32, (width, ch), 0)

    def place_of(y):
        return y + rows + 8 if y < 2 else y

    def convolve(i, group):
        total = jnp.zeros((group * width, ch), jnp.float32)
        for dy in range(3):
            at = [place_of(i + g + dy) * width for g in range(group)]
            source = [jnp.concatenate([ref[here : here + width, :] for here in at], axis=0) for ref in (pair_ref, rest_ref)]
            source = jnp.concatenate(source, axis=1).astype(jnp.bfloat16)
            total += jnp.dot(source, win_ref[dy], preferred_element_type=jnp.float32)
        return total + bin_ref[...][None]

    def activate(i, group, total):
        scale = lax.rsqrt(jnp.mean(total * total, axis=-1, keepdims=True) + 1e-06)
        value = total * scale * gain_ref[...][None]
        half = 0.5 * value
        active = half + half * jnp.tanh(half)
        for g in range(group):
            row = i + g
            mine = active[g * width : (g + 1) * width]
            if row == 0:
                mine = jnp.where(place == 0, 0.0, mine)
            if row == rows + 1:
                mine = jnp.where(place == count - 1, 0.0, mine)
            first_ref[row] = total[g * width : (g + 1) * width]
            at = slice(row * width, (row + 1) * width)
            act_ref[at, 0:ch] = jnp.where(x_at == 0, 0.0, pltpu.roll(mine, 1, 0)).astype(jnp.bfloat16)
            act_ref[at, ch : 2 * ch] = mine.astype(jnp.bfloat16)
            act_ref[at, 2 * ch : 3 * ch] = jnp.where(x_at == width - 1, 0.0, pltpu.roll(mine, width - 1, 0)).astype(
                jnp.bfloat16
            )

    def decode(at, many):
        source = [act_ref[(at + dy) * width : (at + dy + many) * width, :] for dy in range(3)]
        total = jnp.dot(jnp.concatenate(source, axis=1), wmid_ref[...], preferred_element_type=jnp.float32)
        total = total + bmid_ref[...][None]
        for y in range(many):
            dec_ref[at + y] = (total[y * width : (y + 1) * width] + first_ref[at + y + 1]).astype(jnp.bfloat16)
        some = pl.ds(at, many)
        store = pltpu.make_async_copy(dec_ref.at[some], dec_out.at[some], out_sem.at[at // many])
        store.start()
        stores.append(store)

    stores = []
    group = 2 if rows % 2 == 0 else 1
    for dt in range(3):
        ext_ref[dt, :, 128 : 128 + packed] = lat_ref[dt].astype(jnp.float32)
    spread(2)
    for load in loads[1:]:
        load.wait()
    win_ref[...] = jnp.zeros_like(win_ref)
    for dy in range(3):
        for dt in range(3):
            source = (dt * 3 + dy) * taps
            win_ref[dy, at_row[dt] : at_row[dt] + taps] = cin_ref[source : source + taps]
    order = list(range(2, rows, group)) + [0, rows]
    size = {i: group for i in order}
    size[0] = size[rows] = 2
    done, ready = set(), []
    spans = [(at, group) for at in range(0, rows, group)]
    middle_waited = False
    total = convolve(order[0], size[order[0]])
    for k, i in enumerate(order):
        here = total
        if k + 1 < len(order):
            if order[k + 1] == 0:
                arrive((0,))
                for dt in range(3):
                    up = pltpu.roll(above_ref[...].astype(jnp.float32), (8 - 2 * dt) % 8, 0)
                    down = pltpu.roll(below_ref[...].astype(jnp.float32), 6 - 2 * dt, 0)
                    ext_ref[dt, :, 128 : 128 + packed] = jnp.where(sub < 4, up, down)
                spread(rows + 2)
                middle.wait()
                middle_waited = True
            total = convolve(order[k + 1], size[order[k + 1]])
        if middle_waited:
            ready = [span for span in spans if set(range(span[0], span[0] + span[1] + 2)) <= done]
            for span in ready[:1]:
                spans.remove(span)
                decode(*span)
        activate(i, size[i], here)
        done |= set(range(i, i + size[i]))
    for span in spans:
        decode(*span)

    arrive((1,))
    sent((0, 1))

    @pl.when(place == 0)
    def _():
        pltpu.make_async_copy(q_ref.at[0], qp_ref, local_sem.at[0]).wait()

    @pl.when(place == count - 1)
    def _():
        pltpu.make_async_copy(q_ref.at[last], qn_ref, local_sem.at[1]).wait()

    for store in stores:
        store.wait()


def decoder(queries, latent, conv_in, bias_in, norm_gain, conv_mid, bias_mid):
    cols, wide = queries.shape[1:]
    times, rows, packed = latent.shape
    ch = conv_in.shape[1]
    width = packed // (conv_in.shape[0] // 27)
    anywhere = pl.BlockSpec(memory_space=pl.ANY)
    return pl.pallas_call(
        decoder_kernel,
        out_shape=(
            jax.ShapeDtypeStruct((cols, wide), jnp.bfloat16),
            jax.ShapeDtypeStruct((cols, wide), jnp.bfloat16),
            jax.ShapeDtypeStruct((rows, width, ch), jnp.bfloat16),
        ),
        in_specs=[anywhere] * 7,
        out_specs=(anywhere,) * 3,
        scratch_shapes=[
            *[pltpu.VMEM((8, packed), jnp.bfloat16)] * 4,
            pltpu.VMEM((times, 8, packed + 256), jnp.float32),
            pltpu.VMEM(((rows + 10) * width, 128), jnp.float32),
            pltpu.VMEM(((rows + 10) * width, 128), jnp.float32),
            pltpu.VMEM((3, 256, ch), jnp.bfloat16),
            pltpu.VMEM(conv_mid.shape, jnp.bfloat16),
            pltpu.VMEM((rows + 2, width, ch), jnp.float32),
            pltpu.VMEM(((rows + 2) * width, 3 * ch), jnp.bfloat16),
            pltpu.VMEM((rows, width, ch), jnp.bfloat16),
            pltpu.VMEM(latent.shape, jnp.bfloat16),
            pltpu.VMEM(conv_in.shape, jnp.bfloat16),
            *[pltpu.VMEM((ch,), jnp.float32)] * 3,
            pltpu.SemaphoreType.DMA((4,)),
            pltpu.SemaphoreType.DMA((4,)),
            pltpu.SemaphoreType.DMA((2,)),
            pltpu.SemaphoreType.DMA((6,)),
            pltpu.SemaphoreType.DMA((rows,)),
        ],
        compiler_params=pltpu.CompilerParams(
            collective_id=0, has_side_effects=True, vmem_limit_bytes=VMEM_BYTES
        ),
        name="decoder",
    )(queries, latent, conv_in, conv_mid, bias_in, norm_gain, bias_mid)


def body(
    queries, kv_frames, frame_mask, col_shift, latent, conv_in, bias_in, norm_gain, conv_mid, bias_mid
):
    q_prev, q_next, decoded = decoder(queries, latent, conv_in, bias_in, norm_gain, conv_mid, bias_mid)
    o_prev, o_next = edge_attention(kv_frames, frame_mask, col_shift, q_prev, q_next)
    back_prev = to_next(o_next, "band")
    back_next = to_previous(o_prev, "band")
    partial, level, decoded = main_attention(queries, kv_frames, frame_mask, col_shift, decoded)
    return (combine(partial, level, back_prev, back_next), decoded)


def solution(mesh):
    placed = (
        P(("groups", "band"), None, None),
        P("groups", None, "band", None, None),
        P("groups"),
        P("groups"),
        P("groups", "band", None),
        P(),
        P(),
        P(),
        P(),
        P(),
    )
    return jax.shard_map(
        body,
        mesh=mesh,
        in_specs=placed,
        out_specs=(P(("groups", "band"), None, None), P(("groups", "band"), None, None)),
        check_vma=False,
    )
```

```python
import functools
import math

import jax
import jax.numpy as jnp
from jax import lax
from jax.experimental import pallas as pl
from jax.experimental.pallas import tpu as pltpu
from jax.sharding import PartitionSpec as P

HD = 128
RC = 8
NEG = -1e30
MESH = pl.DeviceIdType.MESH
SCALE2 = math.log2(math.e) / math.sqrt(HD)
HEADS_PER_STEP = 5
EDGE_HEADS = 10
VMEM_BYTES = 56 * 2**20
COMBINE_BYTES = 48 * 2**20
LEVEL_BYTES = 24 * 2**20


def to_next(block, axis):
    count = lax.axis_size(axis)
    return lax.ppermute(block, axis, [(i, i + 1) for i in range(count - 1)])


def to_previous(block, axis):
    count = lax.axis_size(axis)
    return lax.ppermute(block, axis, [(i + 1, i) for i in range(count - 1)])


def key_bias(cols, padded, slots, shift, open_slots):
    lane = lax.broadcasted_iota(jnp.int32, (cols, padded), 1)
    query = lax.broadcasted_iota(jnp.int32, (cols, padded), 0)
    column = lane
    level = jnp.full((cols, padded), NEG, jnp.float32)
    for s in range(slots):
        inside = (lane >= s * cols) & (lane < (s + 1) * cols)
        level = jnp.where(inside, open_slots[s], level)
        column = jnp.where(lane >= s * cols, lane - s * cols, column)
    return jnp.where(jnp.abs(column - query - shift) <= RC, level, NEG)


def heads_per_step(heads, most):
    return next(size for size in range(min(most, heads), 0, -1) if heads % size == 0)


def over_frames(mask_ref, frames, run):
    open_frames = [jnp.where(mask_ref[f] == 1, 0.0, NEG) for f in range(frames - 1)] + [jnp.float32(0.0)]
    closed = jnp.int32(frames - 1)
    for f in reversed(range(frames - 1)):
        closed = jnp.where(mask_ref[f] == 1, closed, f)

    @pl.when(closed < frames - 1)
    def _():
        run(
            lambda s: jnp.where(s < closed, s, s + 1),
            [jnp.where(s < closed, open_frames[s], open_frames[s + 1]) for s in range(frames - 1)],
        )

    @pl.when(closed == frames - 1)
    def _():
        run(lambda s: s, open_frames)


def attend(total_rows, cols, shift_ref, bias_ref, plan, places, query_row, kv_row, emit, each, ahead, frame_of, open_slots):
    step = pl.program_id(0)
    slots = len(open_slots)
    span = slots * cols
    padded = -(-span // 128) * 128
    queries = sorted({r for _, seen in plan for r in seen})
    near = {r: [(k, seen.index(r)) for k, (_, seen) in enumerate(plan) if r in seen] for r in queries}

    @pl.when(step == 0)
    def _():
        for at, r in enumerate(queries):
            row = jnp.clip(places[r], 0, total_rows - 1)
            bias_ref[at, :, :padded] = key_bias(cols, padded, slots, shift_ref[row], open_slots)

    def stack(which, n, part):
        pieces = [kv_row(which, frame_of(s), n, slice(None), part) for s in range(slots)]
        if padded > span:
            pieces.append(kv_row(which, frame_of(0), n, slice(0, padded - span), part))
        return jnp.concatenate(pieces, axis=0)

    def score(j):
        part = pl.ds(j * HD, HD)
        found = []
        for n, seen in plan:
            query = jnp.concatenate([query_row(r, part) for r in seen], axis=0)
            found.append(
                lax.dot_general(query, stack(0, n, part), (((1,), (1,)), ((), ())), preferred_element_type=jnp.float32)
            )
        return found

    def soften(found):
        pieces = [[None] * len(seen) for _, seen in plan]
        totals, tops = {}, {}
        for row, r in enumerate(queries):
            bias = bias_ref[row, :, :padded]
            blocks = [found[k][d * cols : (d + 1) * cols] + bias for k, d in near[r]]
            top = jnp.max(functools.reduce(jnp.maximum, blocks), axis=-1, keepdims=True) * SCALE2
            weights = [jnp.exp2(block * SCALE2 - top) for block in blocks]
            tops[r] = top
            for (k, d), weight in zip(near[r], weights):
                pieces[k][d] = weight.astype(jnp.bfloat16)
        return [jnp.concatenate(piece, axis=0) for piece in pieces], totals, tops

    def finish(j, weights, totals, tops):
        part = pl.ds(j * HD, HD)
        ones = jnp.ones((padded, HD), jnp.bfloat16)
        sums = [
            jnp.dot(
                weights[k],
                jnp.concatenate([stack(1, n, part), ones], axis=1),
                preferred_element_type=jnp.float32,
            )
            for k, (n, _) in enumerate(plan)
        ]
        for r in queries:
            acc = functools.reduce(jnp.add, [sums[k][d * cols : (d + 1) * cols] for k, d in near[r]])
            total = acc[:, HD:]
            emit(j, step * each + j, r, (acc[:, :HD] * (1.0 / total)).astype(jnp.bfloat16), tops[r], total)

    found, soft = {}, {}
    for j in range(each + ahead[0]):
        if j < each:
            found[j] = score(j)
        at = j - ahead[1]
        if 0 <= at < each:
            soft[at] = soften(found.pop(at))
        if j >= ahead[0]:
            finish(j - ahead[0], *soft.pop(j - ahead[0]))


def edge_kernel(
    total_rows, rows, each, shift_ref, mask_ref, qp_ref, qn_ref, kvf_ref, kvl_ref, op_ref, on_ref, bias_ref, level_ref
):
    step = pl.program_id(0)
    frames, cols = kvf_ref.shape[1], kvf_ref.shape[3]
    wide = op_ref.shape[1] - 3 * 128
    first_row = lax.axis_index("band") * rows
    lane = lax.broadcasted_iota(jnp.int32, (cols, 128), 1)
    sources, keys, targets = (qp_ref, qn_ref), (kvf_ref, kvl_ref), (op_ref, on_ref)

    @pl.when(step == 0)
    def _():
        level_ref[...] = jnp.zeros_like(level_ref)

    def emit(j, head, r, out, top, total):
        targets[r][:, pl.ds(pl.multiple_of(head * HD, HD), HD)] = out
        level_ref[r] = jnp.where(lane == head, top + jnp.log2(total), level_ref[r])

    over_frames(
        mask_ref,
        frames,
        functools.partial(
            attend,
            total_rows,
            cols,
            shift_ref,
            bias_ref,
            [(0, [0]), (1, [1])],
            [first_row - 1, first_row + rows],
            lambda r, part: sources[r][:, part],
            lambda which, f, n, some, part: keys[n][which, f, 0, some, part],
            emit,
            each,
            (3, 1),
        ),
    )

    @pl.when(step == pl.num_programs(0) - 1)
    def _():
        for side, o_ref in enumerate(targets):
            rest = level_ref[side]
            for k in range(3):
                piece = rest.astype(jnp.bfloat16)
                o_ref[:, wide + k * 128 : wide + (k + 1) * 128] = piece
                rest = rest - piece.astype(jnp.float32)


def main_kernel(
    total_rows, each, shift_ref, mask_ref, q_ref, kv_ref, dec_ref, out_ref, level_ref, dec_out, bias_ref, held_ref, sems
):
    step = pl.program_id(0)
    frames, rows, cols = kv_ref.shape[1], q_ref.shape[0], q_ref.shape[1]
    first_row = lax.axis_index("band") * rows
    lane = lax.broadcasted_iota(jnp.int32, (cols, 128), 1)

    fetch = pltpu.make_async_copy(dec_ref, held_ref, sems.at[0])
    store = pltpu.make_async_copy(held_ref, dec_out, sems.at[1])
    final = pl.num_programs(0) - 1

    @pl.when(step == 0)
    def _():
        fetch.start()
        level_ref[...] = jnp.zeros_like(level_ref)

    def emit(j, head, r, out, top, total):
        out_ref[r, :, j * HD : (j + 1) * HD] = out
        for side, edge in enumerate((0, rows - 1)):
            if r == edge:
                level_ref[side] = jnp.where(lane == head, top + jnp.log2(total), level_ref[side])

    over_frames(
        mask_ref,
        frames,
        functools.partial(
            attend,
            total_rows,
            cols,
            shift_ref,
            bias_ref,
            [(n, list(range(max(n - 1, 0), min(n + 2, rows)))) for n in range(rows)],
            [first_row + r for r in range(rows)],
            lambda r, part: q_ref[r, :, part],
            lambda which, f, n, some, part: kv_ref[which, f, n, some, part],
            emit,
            each,
            (1, 1),
        ),
    )

    @pl.when(step == jnp.minimum(1, final))
    def _():
        fetch.wait()
        store.start()

    @pl.when(step == final)
    def _():
        store.wait()


def combine_kernel(own_in, lev_in, op_in, on_in, out_ref, own_ref, lev_ref, op_ref, on_ref, loads, stores):
    place = lax.axis_index("band")
    count = lax.axis_size("band")
    cols, wide = own_ref.shape[1:]
    last = own_in.shape[0] - 1
    heads = wide // HD
    chunks = next(size for size in (2, 1) if heads % size == 0)
    some = wide // chunks
    rows_of = ((0, 0), (1, last))
    copies = [
        pltpu.make_async_copy(source, target, loads.at[k])
        for k, (source, target) in enumerate(((lev_in.at[pl.ds(0, 2)], lev_ref), (op_in, op_ref), (on_in, on_ref)))
    ]
    owns, outs = [], []
    for side, row in rows_of:
        for c in range(chunks):
            part = pl.ds(c * some, some)
            at = side * chunks + c
            owns.append(pltpu.make_async_copy(own_in.at[row, :, part], own_ref.at[side, :, part], loads.at[3 + at]))
            outs.append(pltpu.make_async_copy(own_ref.at[side, :, part], out_ref.at[row, :, part], stores.at[at]))
    for copy in copies[:2] + owns[:chunks] + copies[2:] + owns[chunks:]:
        copy.start()
    copies[0].wait()
    for side, (o_ref, there) in enumerate(((op_ref, place > 0), (on_ref, place < count - 1))):
        copies[1 + side].wait()
        other = sum(o_ref[:, wide + k * 128 : wide + (k + 1) * 128].astype(jnp.float32) for k in range(3))
        share = jnp.where(there, 1.0 / (1.0 + jnp.exp2(lev_ref[side] - other)), 0.0)
        for c in range(chunks):
            owns[side * chunks + c].wait()
            for j in range(c * (heads // chunks), (c + 1) * (heads // chunks)):
                part = slice(j * HD, (j + 1) * HD)
                here = own_ref[side, :, part].astype(jnp.float32)
                far = o_ref[:, part].astype(jnp.float32)
                own_ref[side, :, part] = (here + (far - here) * share[:, j : j + 1]).astype(jnp.bfloat16)
            outs[side * chunks + c].start()
    for out in outs:
        out.wait()


def fixed(shape):
    return pl.BlockSpec(shape, lambda *_: (0,) * len(shape))


def lanes(shape, row=None):
    lead = (0,) * (len(shape) - 1) if row is None else (0,) * (len(shape) - 3) + (row, 0)
    return pl.BlockSpec(shape, lambda h: lead + (h,))


def edge_attention(kv_frames, frame_mask, col_shift, q_prev, q_next):
    frames, rows, cols, wide = kv_frames.shape[1:]
    heads = wide // HD
    each = heads_per_step(heads, EDGE_HEADS)
    smem = pl.BlockSpec(memory_space=pltpu.SMEM)
    packed = wide + 3 * 128
    padded = -(-frames * cols // 128) * 128
    return pl.pallas_call(
        functools.partial(edge_kernel, col_shift.shape[0], rows, each),
        grid=(heads // each,),
        out_shape=(jax.ShapeDtypeStruct((cols, packed), jnp.bfloat16),) * 2,
        in_specs=[
            smem,
            smem,
            lanes((cols, each * HD)),
            lanes((cols, each * HD)),
            lanes((2, frames, 1, cols, each * HD), 0),
            lanes((2, frames, 1, cols, each * HD), rows - 1),
        ],
        out_specs=(fixed((cols, packed)),) * 2,
        scratch_shapes=[
            pltpu.VMEM((2, cols, padded), jnp.float32),
            pltpu.VMEM((2, cols, 128), jnp.float32),
        ],
        compiler_params=pltpu.CompilerParams(vmem_limit_bytes=VMEM_BYTES),
        cost_estimate=pl.CostEstimate(
            flops=8 * cols * frames * cols * wide,
            bytes_accessed=4 * frames * cols * wide * 2,
            transcendentals=2 * heads * cols * frames * cols,
        ),
        name="edge_attention",
    )(col_shift, frame_mask, q_prev, q_next, kv_frames, kv_frames)


def main_attention(queries, kv_frames, frame_mask, col_shift, decoded):
    rows, cols, wide = queries.shape
    frames = kv_frames.shape[1]
    heads = wide // HD
    each = heads_per_step(heads, HEADS_PER_STEP)
    anywhere = pl.BlockSpec(memory_space=pl.ANY)
    smem = pl.BlockSpec(memory_space=pltpu.SMEM)
    padded = -(-frames * cols // 128) * 128
    return pl.pallas_call(
        functools.partial(main_kernel, col_shift.shape[0], each),
        grid=(heads // each,),
        out_shape=(
            jax.ShapeDtypeStruct(queries.shape, jnp.bfloat16),
            jax.ShapeDtypeStruct((LEVEL_BYTES // (cols * 512), cols, 128), jnp.float32),
            jax.ShapeDtypeStruct(decoded.shape, decoded.dtype),
        ),
        in_specs=[smem, smem, lanes((rows, cols, each * HD)), lanes((2, frames, rows, cols, each * HD)), anywhere],
        out_specs=(lanes((rows, cols, each * HD)), fixed((2, cols, 128)), anywhere),
        scratch_shapes=[
            pltpu.VMEM((rows, cols, padded), jnp.float32),
            pltpu.VMEM(decoded.shape, decoded.dtype),
            pltpu.SemaphoreType.DMA((2,)),
        ],
        compiler_params=pltpu.CompilerParams(vmem_limit_bytes=VMEM_BYTES),
        cost_estimate=pl.CostEstimate(
            flops=4 * rows * cols * 3 * frames * cols * wide,
            bytes_accessed=2 * rows * frames * cols * wide * 2,
            transcendentals=rows * heads * cols * 3 * frames * cols,
        ),
        name="main_attention",
    )(col_shift, frame_mask, queries, kv_frames, decoded)


def combine(partial, level, back_prev, back_next):
    rows, cols, wide = partial.shape
    anywhere = pl.BlockSpec(memory_space=pl.ANY)
    return pl.pallas_call(
        combine_kernel,
        out_shape=jax.ShapeDtypeStruct(partial.shape, jnp.bfloat16),
        in_specs=[anywhere] * 4,
        out_specs=anywhere,
        input_output_aliases={0: 0},
        scratch_shapes=[
            pltpu.VMEM((2, cols, wide), jnp.bfloat16),
            pltpu.VMEM((2, cols, 128), jnp.float32),
            pltpu.VMEM(back_prev.shape, jnp.bfloat16),
            pltpu.VMEM(back_next.shape, jnp.bfloat16),
            pltpu.SemaphoreType.DMA((11,)),
            pltpu.SemaphoreType.DMA((8,)),
        ],
        compiler_params=pltpu.CompilerParams(vmem_limit_bytes=COMBINE_BYTES),
        name="combine",
    )(partial, level, back_prev, back_next)


def hail(place, count):
    barrier = pltpu.get_barrier_semaphore()

    @pl.when(place > 0)
    def _():
        pl.semaphore_signal(barrier, 1, device_id={"band": place - 1}, device_id_type=MESH)

    @pl.when(place < count - 1)
    def _():
        pl.semaphore_signal(barrier, 1, device_id={"band": place + 1}, device_id_type=MESH)


def meet(place, count):
    barrier = pltpu.get_barrier_semaphore()
    pl.semaphore_wait(barrier, jnp.where(place > 0, 1, 0) + jnp.where(place < count - 1, 1, 0))


def swap(place, count, sends, arrivals, up, down):
    def make(triple, other):
        source, target, at = triple
        return pltpu.make_async_remote_copy(
            src_ref=source,
            dst_ref=target,
            send_sem=sends.at[at],
            recv_sem=arrivals.at[at],
            device_id={"band": other},
            device_id_type=MESH,
        )

    ups = [make(triple, jnp.minimum(place + 1, count - 1)) for triple in up]
    downs = [make(triple, jnp.maximum(place - 1, 0)) for triple in down]

    def start(which):
        @pl.when(place < count - 1)
        def _():
            for at in which:
                ups[at].start()

        @pl.when(place > 0)
        def _():
            for at in which:
                downs[at].start()

    def arrive(which):
        @pl.when(place > 0)
        def _():
            for at in which:
                ups[at].wait_recv()

        @pl.when(place < count - 1)
        def _():
            for at in which:
                downs[at].wait_recv()

    def sent(which):
        @pl.when(place < count - 1)
        def _():
            for at in which:
                ups[at].wait_send()

        @pl.when(place > 0)
        def _():
            for at in which:
                downs[at].wait_send()

    return start, arrive, sent


def decoder_kernel(
    q_ref, lat_in, cin_in, wmid_in, bin_in, gain_in, bmid_in, qp_ref, qn_ref, dec_out,
    high_ref, low_ref, below_ref, above_ref, ext_ref, pair_ref, rest_ref, win_ref, wmid_ref, first_ref, act_ref, dec_ref,
    lat_ref, cin_ref, bin_ref, gain_ref, bmid_ref,
    sends, arrivals, local_sem, load_sem, out_sem
):
    place = lax.axis_index("band")
    count = lax.axis_size("band")
    last = q_ref.shape[0] - 1
    hail(place, count)
    named = [
        (lat_in, lat_ref), (cin_in, cin_ref), (bin_in, bin_ref), (gain_in, gain_ref), (bmid_in, bmid_ref),
        (wmid_in, wmid_ref),
    ]
    loads = [pltpu.make_async_copy(source, target, load_sem.at[k]) for k, (source, target) in enumerate(named)]
    for load in loads:
        load.start()
    middle = loads.pop()
    times, rows, packed = lat_ref.shape
    depth = cin_ref.shape[0] // 27
    taps = 3 * depth
    width = packed // depth
    ch = cin_ref.shape[1]
    tiles = packed // 128
    per = 128 // depth
    wide = q_ref.shape[2]
    ahead = max(wide // 1024, 1) * 128
    early, later = pl.ds(0, ahead), pl.ds(ahead, wide - ahead)
    start, arrive, sent = swap(
        place,
        count,
        sends,
        arrivals,
        [
            (high_ref, below_ref, 0),
            (q_ref.at[last, :, early], qp_ref.at[:, early], 1),
            (q_ref.at[last, :, later], qp_ref.at[:, later], 2),
        ],
        [
            (low_ref, above_ref, 3),
            (q_ref.at[0, :, early], qn_ref.at[:, early], 4),
            (q_ref.at[0, :, later], qn_ref.at[:, later], 5),
        ],
    )
    meet(place, count)
    start((1,))
    sub = lax.broadcasted_iota(jnp.int32, (8, packed), 0)

    def gather(target, shifts):
        rows_of = [pltpu.roll(lat_ref[dt].astype(jnp.float32), shifts[dt], 0) for dt in range(3)]
        target[...] = jnp.where(sub < 2, rows_of[0], jnp.where(sub < 4, rows_of[1], rows_of[2])).astype(jnp.bfloat16)

    loads[0].wait()
    gather(high_ref, [2, 4, 6])
    gather(low_ref, [0, 2, 4])
    start((0, 2))

    @pl.when(place == 0)
    def _():
        below_ref[...] = jnp.zeros_like(below_ref)
        pltpu.make_async_copy(q_ref.at[0], qp_ref, local_sem.at[0]).start()

    @pl.when(place == count - 1)
    def _():
        above_ref[...] = jnp.zeros_like(above_ref)
        pltpu.make_async_copy(q_ref.at[last], qn_ref, local_sem.at[1]).start()

    at_row = (0, taps, 128)
    ext_ref[:, :, :128] = jnp.zeros((times, 8, 128), jnp.float32)
    ext_ref[:, :, 128 + packed :] = jnp.zeros((times, 8, 128), jnp.float32)
    lane = lax.broadcasted_iota(jnp.int32, (8, 128), 1)

    def spread(base):
        @pl.loop(0, tiles, unroll=tiles)
        def _(t):
            here = [ext_ref[dt, :, pl.ds(pl.multiple_of((t + 1) * 128, 128), 128)] for dt in range(3)]
            left = [ext_ref[dt, :, pl.ds(pl.multiple_of(t * 128, 128), 128)] for dt in range(3)]
            right = [ext_ref[dt, :, pl.ds(pl.multiple_of((t + 2) * 128, 128), 128)] for dt in range(3)]
            for j in range(per):
                moved = []
                for dt in range(3):
                    piece = here[dt]
                    if j == 0:
                        piece = jnp.where(lane >= 128 - depth, left[dt], piece)
                    if j == per - 1:
                        piece = jnp.where(lane < depth, right[dt], piece)
                    shift = (at_row[dt] - depth * (j - 1)) % 128
                    moved.append(pltpu.roll(piece, shift, 1) if shift else piece)
                both = jnp.where(lane < taps, moved[0], jnp.where(lane < 2 * taps, moved[1], 0.0))
                at = pl.ds(base * width + t * per + j, 8, stride=width)
                pair_ref[at, :] = both
                rest_ref[at, :] = jnp.where(lane < taps, moved[2], 0.0)

    x_at = lax.broadcasted_iota(jnp.int32, (width, ch), 0)

    def place_of(y):
        return y + rows + 8 if y < 2 else y

    def convolve(i, group):
        total = jnp.zeros((group * width, ch), jnp.float32)
        for dy in range(3):
            at = [place_of(i + g + dy) * width for g in range(group)]
            source = [jnp.concatenate([ref[here : here + width, :] for here in at], axis=0) for ref in (pair_ref, rest_ref)]
            source = jnp.concatenate(source, axis=1).astype(jnp.bfloat16)
            total += jnp.dot(source, win_ref[dy], preferred_element_type=jnp.float32)
        return total + bin_ref[...][None]

    def activate(i, group, total):
        scale = lax.rsqrt(jnp.mean(total * total, axis=-1, keepdims=True) + 1e-06)
        value = total * scale * gain_ref[...][None]
        half = 0.5 * value
        active = half + half * jnp.tanh(half)
        for g in range(group):
            row = i + g
            mine = active[g * width : (g + 1) * width]
            if row == 0:
                mine = jnp.where(place == 0, 0.0, mine)
            if row == rows + 1:
                mine = jnp.where(place == count - 1, 0.0, mine)
            first_ref[row] = total[g * width : (g + 1) * width]
            at = slice(row * width, (row + 1) * width)
            act_ref[at, 0:ch] = jnp.where(x_at == 0, 0.0, pltpu.roll(mine, 1, 0)).astype(jnp.bfloat16)
            act_ref[at, ch : 2 * ch] = mine.astype(jnp.bfloat16)
            act_ref[at, 2 * ch : 3 * ch] = jnp.where(x_at == width - 1, 0.0, pltpu.roll(mine, width - 1, 0)).astype(
                jnp.bfloat16
            )

    def decode(at, many):
        source = [act_ref[(at + dy) * width : (at + dy + many) * width, :] for dy in range(3)]
        total = jnp.dot(jnp.concatenate(source, axis=1), wmid_ref[...], preferred_element_type=jnp.float32)
        total = total + bmid_ref[...][None]
        for y in range(many):
            dec_ref[at + y] = (total[y * width : (y + 1) * width] + first_ref[at + y + 1]).astype(jnp.bfloat16)
        some = pl.ds(at, many)
        store = pltpu.make_async_copy(dec_ref.at[some], dec_out.at[some], out_sem.at[at // many])
        store.start()
        stores.append(store)

    stores = []
    group = 2 if rows % 2 == 0 else 1
    for dt in range(3):
        ext_ref[dt, :, 128 : 128 + packed] = lat_ref[dt].astype(jnp.float32)
    spread(2)
    for load in loads[1:]:
        load.wait()
    win_ref[...] = jnp.zeros_like(win_ref)
    for dy in range(3):
        for dt in range(3):
            source = (dt * 3 + dy) * taps
            win_ref[dy, at_row[dt] : at_row[dt] + taps] = cin_ref[source : source + taps]
    order = list(range(2, rows, group)) + [0, rows]
    size = {i: group for i in order}
    size[0] = size[rows] = 2
    done, ready = set(), []
    spans = [(at, group) for at in range(0, rows, group)]
    middle_waited = False
    total = convolve(order[0], size[order[0]])
    for k, i in enumerate(order):
        here = total
        if k + 1 < len(order):
            if order[k + 1] == 0:
                arrive((0,))
                for dt in range(3):
                    up = pltpu.roll(above_ref[...].astype(jnp.float32), (8 - 2 * dt) % 8, 0)
                    down = pltpu.roll(below_ref[...].astype(jnp.float32), 6 - 2 * dt, 0)
                    ext_ref[dt, :, 128 : 128 + packed] = jnp.where(sub < 4, up, down)
                spread(rows + 2)
                middle.wait()
                middle_waited = True
            total = convolve(order[k + 1], size[order[k + 1]])
        if middle_waited:
            ready = [span for span in spans if set(range(span[0], span[0] + span[1] + 2)) <= done]
            for span in ready[:1]:
                spans.remove(span)
                decode(*span)
        activate(i, size[i], here)
        done |= set(range(i, i + size[i]))
    for span in spans:
        decode(*span)

    arrive((1, 2))
    sent((0, 1, 2))

    @pl.when(place == 0)
    def _():
        pltpu.make_async_copy(q_ref.at[0], qp_ref, local_sem.at[0]).wait()

    @pl.when(place == count - 1)
    def _():
        pltpu.make_async_copy(q_ref.at[last], qn_ref, local_sem.at[1]).wait()

    for store in stores:
        store.wait()


def decoder(queries, latent, conv_in, bias_in, norm_gain, conv_mid, bias_mid):
    cols, wide = queries.shape[1:]
    times, rows, packed = latent.shape
    ch = conv_in.shape[1]
    width = packed // (conv_in.shape[0] // 27)
    anywhere = pl.BlockSpec(memory_space=pl.ANY)
    return pl.pallas_call(
        decoder_kernel,
        out_shape=(
            jax.ShapeDtypeStruct((cols, wide), jnp.bfloat16),
            jax.ShapeDtypeStruct((cols, wide), jnp.bfloat16),
            jax.ShapeDtypeStruct((rows, width, ch), jnp.bfloat16),
        ),
        in_specs=[anywhere] * 7,
        out_specs=(anywhere,) * 3,
        scratch_shapes=[
            *[pltpu.VMEM((8, packed), jnp.bfloat16)] * 4,
            pltpu.VMEM((times, 8, packed + 256), jnp.float32),
            pltpu.VMEM(((rows + 10) * width, 128), jnp.float32),
            pltpu.VMEM(((rows + 10) * width, 128), jnp.float32),
            pltpu.VMEM((3, 256, ch), jnp.bfloat16),
            pltpu.VMEM(conv_mid.shape, jnp.bfloat16),
            pltpu.VMEM((rows + 2, width, ch), jnp.float32),
            pltpu.VMEM(((rows + 2) * width, 3 * ch), jnp.bfloat16),
            pltpu.VMEM((rows, width, ch), jnp.bfloat16),
            pltpu.VMEM(latent.shape, jnp.bfloat16),
            pltpu.VMEM(conv_in.shape, jnp.bfloat16),
            *[pltpu.VMEM((ch,), jnp.float32)] * 3,
            pltpu.SemaphoreType.DMA((6,)),
            pltpu.SemaphoreType.DMA((6,)),
            pltpu.SemaphoreType.DMA((2,)),
            pltpu.SemaphoreType.DMA((6,)),
            pltpu.SemaphoreType.DMA((rows,)),
        ],
        compiler_params=pltpu.CompilerParams(
            collective_id=0, has_side_effects=True, vmem_limit_bytes=VMEM_BYTES
        ),
        name="decoder",
    )(queries, latent, conv_in, conv_mid, bias_in, norm_gain, bias_mid)


def body(
    queries, kv_frames, frame_mask, col_shift, latent, conv_in, bias_in, norm_gain, conv_mid, bias_mid
):
    q_prev, q_next, decoded = decoder(queries, latent, conv_in, bias_in, norm_gain, conv_mid, bias_mid)
    o_prev, o_next = edge_attention(kv_frames, frame_mask, col_shift, q_prev, q_next)
    back_prev = to_next(o_next, "band")
    back_next = to_previous(o_prev, "band")
    partial, level, decoded = main_attention(queries, kv_frames, frame_mask, col_shift, decoded)
    return (combine(partial, level, back_prev, back_next), decoded)


def solution(mesh):
    placed = (
        P(("groups", "band"), None, None),
        P("groups", None, "band", None, None),
        P("groups"),
        P("groups"),
        P("groups", "band", None),
        P(),
        P(),
        P(),
        P(),
        P(),
    )
    return jax.shard_map(
        body,
        mesh=mesh,
        in_specs=placed,
        out_specs=(P(("groups", "band"), None, None), P(("groups", "band"), None, None)),
        check_vma=False,
    )
```
